32 devices in a mesh: dp: 16 (over z, y, core), tensor: 2 (over x).
Axes of the slice: x: 2, y: 2, z: 4, core: 2. Of those that a mesh axis runs over, the one named last changes fastest.
Arguments:
- hidden_in: bfloat16 [4096, 1024], P(('dp', 'tensor')), may hold values from -6 to 6
- out_grad: bfloat16 [4096, 1024], P(('dp', 'tensor')), may hold values from -6 to 6
- span_start: int32 [16, 2], P('dp'), may hold values from 0 to 240, as said below
- span_length: int32 [16, 2], P('dp'), may hold values from 16 to 128
- attn_gain: bfloat16 [1024], P(('dp', 'tensor')), may hold values from 0.099609375 to 1.8984375
- attn_shift: bfloat16 [1024], P(('dp', 'tensor')), may hold values from -3 to 3
- mlp_gain: bfloat16 [1024], P(('dp', 'tensor')), may hold values from 0.099609375 to 1.8984375
- mlp_shift: bfloat16 [1024], P(('dp', 'tensor')), may hold values from -3 to 3
- qkv_weight: bfloat16 [1024, 3, 1024], P('dp', None, 'tensor'), may hold values from -0.1875 to 0.1875
- qkv_bias: bfloat16 [3, 1024], P(None, ('tensor', 'dp')), may hold values from -3 to 3
- dense_weight: bfloat16 [1024, 1024], P(('tensor', 'dp')), may hold values from -1.5 to 1.5
- dense_bias: bfloat16 [1024], P(('dp', 'tensor')), may hold values from -3 to 3
- up_weight: bfloat16 [1024, 4096], P('dp', 'tensor'), may hold values from -0.1875 to 0.1875
- up_bias: bfloat16 [4096], P(('tensor', 'dp')), may hold values from -3 to 3
- down_weight: bfloat16 [4096, 1024], P(('tensor', 'dp')), may hold values from -0.09375 to 0.09375
- down_bias: bfloat16 [1024], P(('dp', 'tensor')), may hold values from -3 to 3
Outputs:
- layer_out: bfloat16 [4096, 1024], P(('dp', 'tensor'))
- input_grad: bfloat16 [4096, 1024], P(('dp', 'tensor'))
- attn_gain_grad: float32 [1024], P(('dp', 'tensor'))
- attn_shift_grad: float32 [1024], P(('dp', 'tensor'))
- mlp_gain_grad: float32 [1024], P(('dp', 'tensor'))
- mlp_shift_grad: float32 [1024], P(('dp', 'tensor'))
- qkv_weight_grad: float32 [1024, 3, 1024], P('dp', None, 'tensor')
- qkv_bias_grad: float32 [3, 1024], P(None, ('tensor', 'dp'))
- dense_weight_grad: float32 [1024, 1024], P(('tensor', 'dp'))
- dense_bias_grad: float32 [1024], P(('dp', 'tensor'))
- up_weight_grad: float32 [1024, 4096], P('dp', 'tensor')
- up_bias_grad: float32 [4096], P(('tensor', 'dp'))
- down_weight_grad: float32 [4096, 1024], P(('tensor', 'dp'))
- down_bias_grad: float32 [1024], P(('dp', 'tensor'))
The draws below stay inside these ranges and needn't reach their ends.
Inputs may be any that keep to these rules, and one draw needn't show every extreme that they name: `span_start`: span slot k of a sequence lies inside its positions k * 128 to (k + 1) * 128 - 1.
All inputs are finite; a program needn't handle non-finite values.
Results may differ from the reference program's by a relative error of at most 0.011.
Values may be sent and summed in bfloat16 or wider, within the bound.
A program may use at most 128 MiB of HBM per device.

```python
import math
import jax
import jax.numpy as jnp
from jax import lax

D = 1024
H = 16
HD = 64
ROT = 16
FF = 4096
SPANS = 2
SEQ_LEN = 256
SEQS = 16
TOKENS = 4096
HALF = 128
MAXLEN = 128
MINLEN = 16


def span_table(key):
    folded = jax.random.fold_in(key, 11)
    len_key, off_key = jax.random.split(folded)
    lengths = jax.random.randint(len_key, (SEQS, SPANS), MINLEN, MAXLEN + 1, dtype=jnp.int32)
    lengths = lengths.at[0, 0].set(MAXLEN).at[0, SPANS - 1].set(MINLEN)
    offsets = jax.random.randint(off_key, (SEQS, SPANS), 0, HALF - lengths + 1, dtype=jnp.int32)
    offsets = offsets.at[0, 0].set(0).at[0, SPANS - 1].set(HALF - MINLEN)
    starts = offsets + HALF * jnp.arange(SPANS, dtype=jnp.int32)[None, :]
    return (starts, lengths)


def draw_span_start(key, part):
    return span_table(key)[0]


def draw_span_length(key, part):
    return span_table(key)[1]


def raised(array, rng, source, target, parts, factor):
    def block_of(axis_at):
        return (jnp.arange(array.shape[axis_at]) // (array.shape[axis_at] // parts)).reshape((-1,) + (1,) * (array.ndim - 1 - axis_at))

    one_side = jax.random.permutation(rng, parts)[block_of(target)]
    second = (block_of(target) + parts // 2) % parts
    return jnp.where((block_of(source) == one_side) | (block_of(source) == second), factor * array, array)


def shard_levels(rng, dims, shards, smallest, high):
    factor_of, own = 1.0, jax.random.fold_in(rng, 6)
    for dim, shards_of in shards:
        draws = jnp.exp(jax.random.uniform(jax.random.fold_in(own, dim), (shards_of,), jnp.float32, smallest / len(shards), high / len(shards)))
        factor_of = factor_of * jnp.repeat(draws, dims[dim] // shards_of).reshape([-1 if axis == dim else 1 for axis in range(len(dims))])
    return factor_of


def normal_values(stream_key, shape, scale, most, pieces=(), kind=jnp.bfloat16):
    entries = jax.random.normal(stream_key, shape, jnp.float32) * scale
    if len(pieces) > 0:
        entries = shard_levels(stream_key, shape, pieces, -0.22, 0.18) * entries
    return jnp.clip(entries, min=-most, max=most).astype(kind)


def gaussian_with(rng, dims, scale, bound, cuts, heavy, held_as=jnp.bfloat16):
    entries = scale * jax.random.normal(rng, dims, jnp.float32)
    if cuts:
        entries = entries * shard_levels(rng, dims, cuts, -0.22, 0.18)
    return jnp.clip(raised(entries, jax.random.fold_in(rng, 3), *heavy), -bound, bound).astype(held_as)


def setup_inputs(seed: int = 0) -> dict:
    key_list = jax.random.split(jax.random.key(seed), 17)
    hidden_in = gaussian_with(key_list[0], (TOKENS, D), 1.0, 6.0, ((0, 32),), (0, 1, 32, 2.75))
    out_grad = gaussian_with(key_list[1], (TOKENS, D), 1.0, 6.0, ((0, 32),), (0, 1, 32, 2.75))
    span_start = draw_span_start(jax.random.fold_in(key_list[16], 71), 0)
    span_length = draw_span_length(jax.random.fold_in(key_list[16], 71), 0)
    attn_gain = jnp.clip(1.0 + 0.18 * jax.random.normal(key_list[4], (D,), jnp.float32), 0.099609375, 1.8984375).astype(jnp.bfloat16)
    attn_shift = normal_values(key_list[5], (D,), 0.5, 3.0, ((0, 32),))
    mlp_gain = jnp.clip(1.0 + 0.18 * jax.random.normal(key_list[6], (D,), jnp.float32), 0.099609375, 1.8984375).astype(jnp.bfloat16)
    mlp_shift = normal_values(key_list[7], (D,), 0.5, 3.0, ((0, 32),))
    qkv_weight = normal_values(key_list[8], (D, 3, D), D ** -0.5, 0.1875, ((0, 16), (2, 2)))
    qkv_bias = normal_values(key_list[9], (3, D), 0.5, 3.0, ((1, 32),))
    dense_weight = normal_values(key_list[10], (D, D), (max(1, 4 * D // SEQ_LEN)) ** -0.5, 1.5, ((0, 32),))
    dense_bias = normal_values(key_list[11], (D,), 0.5, 3.0, ((0, 32),))
    up_weight = normal_values(key_list[12], (D, FF), D ** -0.5, 0.1875, ((0, 16), (1, 2)))
    up_bias = normal_values(key_list[13], (FF,), 0.5, 3.0, ((0, 32),))
    down_weight = normal_values(key_list[14], (FF, D), FF ** -0.5, 0.09375, ((0, 32),))
    down_bias = normal_values(key_list[15], (D,), 0.5, 3.0, ((0, 32),))
    return dict(hidden_in=hidden_in, out_grad=out_grad, span_start=span_start, span_length=span_length, attn_gain=attn_gain, attn_shift=attn_shift, mlp_gain=mlp_gain, mlp_shift=mlp_shift, qkv_weight=qkv_weight, qkv_bias=qkv_bias, dense_weight=dense_weight, dense_bias=dense_bias, up_weight=up_weight, up_bias=up_bias, down_weight=down_weight, down_bias=down_bias)


@jax.custom_vjp
def low(v):
    return lax.optimization_barrier(v.astype(jnp.bfloat16)).astype(jnp.float32)

@jax.custom_vjp
def low_back(v):
    return v

def low_keep(v):
    return (low(v), None)

def low_pass(kept, grad):
    return (grad,)

def back_keep(v):
    return (v, None)

def back_low(kept, grad):
    return (low(grad),)
low.defvjp(low_keep, low_pass)
low_back.defvjp(back_keep, back_low)
PRECISE = lax.Precision.HIGHEST
NORM_EPS = 1e-05
NEG_FILL = -1000000000.0

def layer_norm(rows_in, gain_vec, shift_vec):
    mean_row = lax.optimization_barrier(jnp.mean(rows_in, axis=-1, keepdims=True))
    centred = rows_in - mean_row
    spread = lax.optimization_barrier(jnp.mean(centred * centred, axis=-1, keepdims=True))
    return centred * lax.rsqrt(spread + NORM_EPS) * gain_vec + shift_vec

def rotary_tables(length):
    position = jnp.arange(length, dtype=jnp.float32)
    rates = 10000.0 ** (-jnp.arange(ROT // 2, dtype=jnp.float32) * (2.0 / ROT))
    angles = position[:, None] * rates[None, :]
    angles = jnp.concatenate([angles, angles], axis=-1)[:, None, :]
    return (jnp.cos(angles), jnp.sin(angles))

def rotate(field_in, cosine, sines):
    turned = field_in[..., :ROT]
    first_half = turned[..., :ROT // 2]
    second_half = turned[..., ROT // 2:]
    swapped = jnp.concatenate([-second_half, first_half], axis=-1)
    return jnp.concatenate([turned * cosine + swapped * sines, field_in[..., ROT:]], axis=-1)

def allowed_pairs(starts, lengths):
    position = jnp.arange(SEQ_LEN, dtype=jnp.int32)
    inside = (position[None, None, :] >= starts[:, :, None]) & (position[None, None, :] < (starts + lengths)[:, :, None])
    marks = (jnp.arange(SPANS, dtype=jnp.int32) + 1)[None, :, None]
    labels = lax.optimization_barrier(jnp.sum(jnp.where(inside, marks, 0), axis=1)).astype(jnp.int32)
    causal = position[None, :] <= position[:, None]
    same_span = (labels[:, :, None] == labels[:, None, :]) & (labels[:, :, None] > 0)
    return causal[None] | same_span

def forward(token_rows, allowed, cosine, sines, params):
    attn_gain, attn_shift, mlp_gain, mlp_shift, qkv_weight, qkv_bias, dense_weight, dense_bias, up_weight, up_bias, down_weight, down_bias = params
    group_size, length = (token_rows.shape[0], token_rows.shape[1])
    normed_attn = low(layer_norm(token_rows, attn_gain, attn_shift))
    normed_mlp = low(layer_norm(token_rows, mlp_gain, mlp_shift))
    projected = jnp.einsum('gld,dtc->gltc', normed_attn, qkv_weight, precision=PRECISE) + qkv_bias
    projected = low_back(projected)
    heads_view = projected.reshape(group_size, length, 3, H, HD)
    query_rows = low(rotate(heads_view[:, :, 0], cosine, sines))
    key_rows = low(rotate(heads_view[:, :, 1], cosine, sines))
    value_rows = low(heads_view[:, :, 2])
    scores = jnp.einsum('gqhe,gkhe->ghqk', query_rows, key_rows, precision=PRECISE) * HD ** (-0.5)
    scores = jnp.where(allowed[:, None], scores, NEG_FILL)
    scores = low_back(scores)
    prob_rows = low(jax.nn.softmax(scores, axis=-1))
    context = jnp.einsum('ghqk,gkhe->gqhe', prob_rows, value_rows, precision=PRECISE)
    context = low(low_back(context.reshape(group_size, length, D)))
    attn_part = jnp.einsum('gle,ed->gld', context, dense_weight, precision=PRECISE)
    hidden = jnp.einsum('gld,df->glf', normed_mlp, up_weight, precision=PRECISE) + up_bias
    hidden = low_back(hidden)
    active = low(jax.nn.gelu(hidden, approximate=False))
    mlp_part = jnp.einsum('glf,fd->gld', active, down_weight, precision=PRECISE)
    return token_rows + attn_part + mlp_part + dense_bias + down_bias

def reference(hidden_in, out_grad, span_start, span_length, attn_gain, attn_shift, mlp_gain, mlp_shift, qkv_weight, qkv_bias, dense_weight, dense_bias, up_weight, up_bias, down_weight, down_bias):
    params = tuple((item.astype(jnp.float32) for item in (attn_gain, attn_shift, mlp_gain, mlp_shift, qkv_weight, qkv_bias, dense_weight, dense_bias, up_weight, up_bias, down_weight, down_bias)))
    group_size = math.gcd(SEQS, max(1, 4096 // SEQ_LEN))
    steps_count = SEQS // group_size
    rows_all = hidden_in.astype(jnp.float32).reshape(steps_count, group_size, SEQ_LEN, D)
    cot_all = out_grad.astype(jnp.float32).reshape(steps_count, group_size, SEQ_LEN, D)
    starts_all = span_start.reshape(steps_count, group_size, SPANS)
    lengths_all = span_length.reshape(steps_count, group_size, SPANS)
    cosine, sines = rotary_tables(SEQ_LEN)

    def one_step(totals, inputs):
        token_rows, cotangent, starts, lengths = inputs
        allowed = allowed_pairs(starts, lengths)

        def layer_at(rows_in, *weights):
            return forward(rows_in, allowed, cosine, sines, weights)
        outcome, pullback = jax.vjp(layer_at, token_rows, *params)
        gradients = pullback(cotangent)
        totals = tuple((acc + grad_part for acc, grad_part in zip(totals, gradients[1:])))
        return (totals, (outcome.astype(jnp.bfloat16), gradients[0].astype(jnp.bfloat16)))
    initial = tuple((jnp.zeros(item.shape, jnp.float32) for item in params))
    totals, (outcomes, input_grads) = lax.scan(one_step, initial, (rows_all, cot_all, starts_all, lengths_all))
    layer_out = outcomes.reshape(TOKENS, D)
    input_grad = input_grads.reshape(TOKENS, D)
    return (layer_out, input_grad, totals[0], totals[1], totals[2], totals[3], totals[4], totals[5], totals[6], totals[7], totals[8], totals[9], totals[10], totals[11])
```

```python
import jax
import jax.numpy as jnp
import numpy as np
from jax import lax
from jax.experimental import pallas as pl
from jax.experimental.pallas import tpu as pltpu
from jax.sharding import PartitionSpec as P

HD = 64
ROT = 16


NORM_EPS = 1e-05
NEG_FILL = -1000000000.0


def layer_norm(rows_in, gain_vec, shift_vec):
    mean_row = jnp.mean(rows_in, axis=-1, keepdims=True)
    centred = rows_in - mean_row
    spread = jnp.mean(centred * centred, axis=-1, keepdims=True)
    return centred * lax.rsqrt(spread + NORM_EPS) * gain_vec + shift_vec


def rotary_tables(length):
    position = jnp.arange(length, dtype=jnp.float32)
    rates = 10000.0 ** (-jnp.arange(ROT // 2, dtype=jnp.float32) * (2.0 / ROT))
    angles = position[:, None] * rates[None, :]
    angles = jnp.concatenate([angles, angles], axis=-1)[:, None, :]
    return (jnp.cos(angles), jnp.sin(angles))


def rotate(field_in, cosine, sines):
    turned = field_in[..., :ROT]
    first_half = turned[..., : ROT // 2]
    second_half = turned[..., ROT // 2 :]
    swapped = jnp.concatenate([-second_half, first_half], axis=-1)
    return jnp.concatenate([turned * cosine + swapped * sines, field_in[..., ROT:]], axis=-1)


def gelu_exact(values_in):
    return jax.nn.gelu(values_in, approximate=False)


def shards(
    hidden_in,
    out_grad,
    span_start,
    span_length,
    attn_gain,
    attn_shift,
    mlp_gain,
    mlp_shift,
    qkv_weight,
    qkv_bias,
    dense_weight,
    dense_bias,
    up_weight,
    up_bias,
    down_weight,
    down_bias,
):
    local_rows = hidden_in.shape[0]
    length = local_rows * lax.axis_size("tensor")
    block_rows = min(512, length)
    block_count = length // block_rows
    score_scale = HD ** (-0.5)
    small_full = (
        lax.all_gather(attn_gain, ("dp", "tensor"), axis=0, tiled=True),
        lax.all_gather(attn_shift, ("dp", "tensor"), axis=0, tiled=True),
        lax.all_gather(mlp_gain, ("dp", "tensor"), axis=0, tiled=True),
        lax.all_gather(mlp_shift, ("dp", "tensor"), axis=0, tiled=True),
        lax.all_gather(dense_bias, ("dp", "tensor"), axis=0, tiled=True),
        lax.all_gather(down_bias, ("dp", "tensor"), axis=0, tiled=True),
    )
    small_vecs = [item.astype(jnp.float32) for item in small_full]
    own_rows = hidden_in.astype(jnp.float32)
    normed_attn = layer_norm(own_rows, small_vecs[0], small_vecs[1]).astype(jnp.bfloat16)
    normed_mlp = layer_norm(own_rows, small_vecs[2], small_vecs[3]).astype(jnp.bfloat16)
    attn_full, mlp_full = (
        lax.all_gather(normed_attn, "tensor", axis=0, tiled=True),
        lax.all_gather(normed_mlp, "tensor", axis=0, tiled=True),
    )
    full_qkv, full_qkv_bias, full_dense, full_up, full_up_bias, full_down = (
        lax.all_gather(qkv_weight, "dp", axis=0, tiled=True),
        lax.all_gather(qkv_bias, "dp", axis=1, tiled=True),
        lax.all_gather(dense_weight, "dp", axis=0, tiled=True),
        lax.all_gather(up_weight, "dp", axis=0, tiled=True),
        lax.all_gather(up_bias, "dp", axis=0, tiled=True),
        lax.all_gather(down_weight, "dp", axis=0, tiled=True),
    )
    model_width = full_qkv.shape[0]
    head_cols = full_qkv.shape[2]
    local_heads = head_cols // HD
    projected = jnp.dot(
        attn_full, full_qkv.reshape(model_width, 3 * head_cols), preferred_element_type=jnp.float32
    )
    projected = projected + full_qkv_bias.reshape(3 * head_cols).astype(jnp.float32)
    projected = projected.reshape(length, 3, local_heads, HD)
    cosine, sines = rotary_tables(length)
    query_rows = rotate(projected[:, 0], cosine, sines).astype(jnp.bfloat16)
    key_rows = rotate(projected[:, 1], cosine, sines).astype(jnp.bfloat16)
    value_rows = projected[:, 2].astype(jnp.bfloat16)
    position = jnp.arange(length, dtype=jnp.int32)
    starts_here = span_start[0]
    lengths_here = span_length[0]
    inside = (position[None, :] >= starts_here[:, None]) & (
        position[None, :] < (starts_here + lengths_here)[:, None]
    )
    marks = (jnp.arange(starts_here.shape[0], dtype=jnp.int32) + 1)[:, None]
    labels = jnp.sum(jnp.where(inside, marks, 0), axis=0)

    def block_scores(first_row, query_block):
        raw_scores = (
            jnp.einsum("qhe,khe->hqk", query_block, key_rows, preferred_element_type=jnp.float32)
            * score_scale
        )
        row_pos = first_row + jnp.arange(block_rows, dtype=jnp.int32)
        allowed = (position[None, :] <= row_pos[:, None]) | (labels[:, None] == labels[None, :]) & (
            labels[:, None] > 0
        )
        return jnp.where(allowed[None], raw_scores, NEG_FILL)

    def attend(first_row):
        scores = block_scores(first_row, query_rows)
        row_top = jnp.max(scores, axis=-1, keepdims=True)
        exponent = jnp.exp(scores - row_top)
        summed = jnp.sum(exponent, axis=-1, keepdims=True)
        prob_low = (exponent / summed).astype(jnp.bfloat16)
        context_block = jnp.einsum(
            "hqk,khe->qhe", prob_low, value_rows, preferred_element_type=jnp.float32
        )
        return (context_block.astype(jnp.bfloat16), (row_top + jnp.log(summed))[..., 0])

    block_starts = jnp.arange(block_count, dtype=jnp.int32) * block_rows
    context_blocks, lse_blocks = lax.map(attend, block_starts)
    context = context_blocks.reshape(length, head_cols)
    attn_part = jnp.dot(context, full_dense, preferred_element_type=jnp.float32)
    attn_mixed = lax.psum_scatter(
        attn_part.astype(jnp.bfloat16), "tensor", scatter_dimension=0, tiled=True
    ).astype(jnp.float32)
    hidden = jnp.dot(mlp_full, full_up, preferred_element_type=jnp.float32) + full_up_bias.astype(
        jnp.float32
    )
    active = gelu_exact(hidden).astype(jnp.bfloat16)
    mlp_part = jnp.dot(active, full_down, preferred_element_type=jnp.float32)
    mixed_rows = attn_mixed + lax.psum_scatter(
        mlp_part.astype(jnp.bfloat16), "tensor", scatter_dimension=0, tiled=True
    ).astype(jnp.float32)
    layer_out = (own_rows + mixed_rows + small_vecs[4] + small_vecs[5]).astype(jnp.bfloat16)
    cot_full = lax.all_gather(out_grad, "tensor", axis=0, tiled=True)
    full_qkv, full_dense, full_up, full_down = (
        lax.all_gather(qkv_weight, "dp", axis=0, tiled=True),
        lax.all_gather(dense_weight, "dp", axis=0, tiled=True),
        lax.all_gather(up_weight, "dp", axis=0, tiled=True),
        lax.all_gather(down_weight, "dp", axis=0, tiled=True),
    )
    down_grad = jnp.einsum("lf,ld->fd", active, cot_full, preferred_element_type=jnp.float32)
    dense_grad = jnp.einsum("le,ld->ed", context, cot_full, preferred_element_type=jnp.float32)
    active_grad = jnp.einsum("ld,fd->lf", cot_full, full_down, preferred_element_type=jnp.float32)
    hidden_grad = jax.vjp(gelu_exact, hidden)[1](active_grad)[0].astype(jnp.bfloat16)
    up_grad = jnp.einsum("ld,lf->df", mlp_full, hidden_grad, preferred_element_type=jnp.float32)
    up_bias_grad = jnp.sum(hidden_grad, axis=0, dtype=jnp.float32)
    mlp_in_grad = jnp.einsum("lf,df->ld", hidden_grad, full_up, preferred_element_type=jnp.float32)
    context_grad = jnp.einsum("ld,ed->le", cot_full, full_dense, preferred_element_type=jnp.float32)
    context_grad = context_grad.astype(jnp.bfloat16).reshape(length, local_heads, HD)

    def attend_back(carried, inputs):
        key_acc, value_acc = carried
        first_row, lse_block = inputs
        scores = block_scores(first_row, query_rows)
        prob_rows = jnp.exp(scores - lse_block[..., None])
        prob_low = prob_rows.astype(jnp.bfloat16)
        value_acc = value_acc + jnp.einsum(
            "hqk,qhe->khe", prob_low, context_grad, preferred_element_type=jnp.float32
        )
        prob_grad = jnp.einsum(
            "qhe,khe->hqk", context_grad, value_rows, preferred_element_type=jnp.float32
        )
        score_grad = prob_rows * (
            prob_grad - jnp.sum(prob_grad * prob_rows, axis=-1, keepdims=True)
        )
        score_grad = score_grad.astype(jnp.bfloat16)
        query_grad = (
            jnp.einsum("hqk,khe->qhe", score_grad, key_rows, preferred_element_type=jnp.float32)
            * score_scale
        )
        key_acc = (
            key_acc
            + jnp.einsum("hqk,qhe->khe", score_grad, query_rows, preferred_element_type=jnp.float32)
            * score_scale
        )
        return ((key_acc, value_acc), query_grad)

    zero_rows = jnp.zeros((length, local_heads, HD), jnp.float32)
    (key_grad, value_grad), query_blocks = lax.scan(
        attend_back, (zero_rows, zero_rows), (block_starts, lse_blocks)
    )
    query_grad = query_blocks.reshape(length, local_heads, HD)

    def turn(field_in):
        return rotate(field_in, cosine, sines)

    turn_back = jax.vjp(turn, zero_rows)[1]
    projected_grad = jnp.stack(
        [turn_back(query_grad)[0], turn_back(key_grad)[0], value_grad], axis=1
    )
    projected_grad = projected_grad.astype(jnp.bfloat16).reshape(length, 3 * head_cols)
    qkv_weight_grad = jnp.einsum(
        "ld,lc->dc", attn_full, projected_grad, preferred_element_type=jnp.float32
    )
    qkv_weight_grad = qkv_weight_grad.reshape(model_width, 3, head_cols)
    qkv_bias_grad = jnp.sum(projected_grad, axis=0, dtype=jnp.float32).reshape(3, head_cols)
    attn_in_grad = jnp.einsum(
        "lc,dc->ld",
        projected_grad,
        full_qkv.reshape(model_width, 3 * head_cols),
        preferred_element_type=jnp.float32,
    )
    reduced = (
        lax.psum_scatter(qkv_weight_grad, "dp", scatter_dimension=0, tiled=True),
        lax.psum_scatter(qkv_bias_grad, "dp", scatter_dimension=1, tiled=True),
        lax.psum_scatter(dense_grad, "dp", scatter_dimension=0, tiled=True),
        lax.psum_scatter(up_grad, "dp", scatter_dimension=0, tiled=True),
        lax.psum_scatter(up_bias_grad, "dp", scatter_dimension=0, tiled=True),
        lax.psum_scatter(down_grad, "dp", scatter_dimension=0, tiled=True),
    )
    attn_local, mlp_local = (
        lax.psum_scatter(
            attn_in_grad.astype(jnp.bfloat16), "tensor", scatter_dimension=0, tiled=True
        ).astype(jnp.float32),
        lax.psum_scatter(
            mlp_in_grad.astype(jnp.bfloat16), "tensor", scatter_dimension=0, tiled=True
        ).astype(jnp.float32),
    )
    pull_attn = jax.vjp(layer_norm, own_rows, small_vecs[0], small_vecs[1])[1]
    pull_mlp = jax.vjp(layer_norm, own_rows, small_vecs[2], small_vecs[3])[1]
    rows_grad_attn, gain_grad_attn, shift_grad_attn = pull_attn(attn_local)
    rows_grad_mlp, gain_grad_mlp, shift_grad_mlp = pull_mlp(mlp_local)
    cot_rows = out_grad.astype(jnp.float32)
    input_grad = (cot_rows + rows_grad_attn + rows_grad_mlp).astype(jnp.bfloat16)
    bias_total = jnp.sum(cot_rows, axis=0)
    small_sums = (
        lax.psum_scatter(gain_grad_attn, ("dp", "tensor"), scatter_dimension=0, tiled=True),
        lax.psum_scatter(shift_grad_attn, ("dp", "tensor"), scatter_dimension=0, tiled=True),
        lax.psum_scatter(gain_grad_mlp, ("dp", "tensor"), scatter_dimension=0, tiled=True),
        lax.psum_scatter(shift_grad_mlp, ("dp", "tensor"), scatter_dimension=0, tiled=True),
        lax.psum_scatter(bias_total, ("dp", "tensor"), scatter_dimension=0, tiled=True),
    )
    return (
        layer_out,
        input_grad,
        small_sums[0],
        small_sums[1],
        small_sums[2],
        small_sums[3],
        reduced[0],
        reduced[1],
        reduced[2],
        small_sums[4],
        reduced[3],
        reduced[4],
        reduced[5],
        small_sums[4],
    )


F32 = jnp.float32
BF16 = jnp.bfloat16
MESH_ID = pl.DeviceIdType.MESH
LINE = 4
SEQ = 256
WIDTH = 1024
HID = 512
PAIR = 128


def nn(a, b):
    return jnp.dot(a, b, preferred_element_type=F32)


def nt(a, b):
    return lax.dot_general(a, b, (((1,), (1,)), ((), ())), preferred_element_type=F32)


def tn(a, b):
    return lax.dot_general(a, b, (((0,), (0,)), ((), ())), preferred_element_type=F32)


def turn_tables():
    position = np.arange(SEQ, dtype=np.float64)[:, None]
    lane = np.arange(PAIR) % HD
    rates = 10000.0 ** (-(lane % (ROT // 2)) * (2.0 / ROT))
    angles = position * rates[None, :]
    cosine = np.where(lane < ROT, np.cos(angles), 1.0)
    toward = np.where(lane < ROT // 2, -np.sin(angles), 0.0)
    away = np.where((lane >= ROT // 2) & (lane < ROT), np.sin(angles), 0.0)
    return np.stack([cosine, toward, away]).astype(np.float32)


def rows_of(index, count):
    return pl.ds(pl.multiple_of(index * count, count), count)


class Place:
    def __init__(self):
        index = lax.axis_index("dp")
        self.t = lax.axis_index("tensor")
        self.z = index // 4
        self.k = index % 4
        self.y = self.k // 2
        self.c = self.k % 2
        self.kc = self.y * 2 + 1 - self.c
        self.ky = (1 - self.y) * 2 + self.c
        self.kyc = (1 - self.y) * 2 + 1 - self.c
        self.q = self.k * 2 + self.t
        self.core = self.at(self.z, self.kc, self.t)
        self.cross = (
            self.at(self.z, self.k, 1 - self.t),
            self.at(self.z, self.ky, self.t),
            self.at(self.z, self.ky, 1 - self.t),
        )

    def at(self, z, k, t):
        return (z * 4 + k, t)

    def line(self, z):
        return self.at(z, self.k, self.t)


class Wires:
    def __init__(self, sends, arrivals):
        self.sends, self.arrivals, self.used = sends, arrivals, 0

    def take(self, count):
        first = self.used
        self.used += count
        return first

    def copy(self, slot, src, dst, device):
        return pltpu.make_async_remote_copy(
            src_ref=src,
            dst_ref=dst,
            send_sem=self.sends.at[slot],
            recv_sem=self.arrivals.at[slot],
            device_id=device,
            device_id_type=MESH_ID,
        )


class PlaneGather:
    def __init__(self, me, wires, src, slot):
        self.me, self.wires, self.src, self.slot = me, wires, src, slot
        self.first = wires.take(7)
        self.from_cross = (me.k * 2 + 1 - me.t, me.ky * 2 + me.t, me.ky * 2 + 1 - me.t)
        self.from_core = (
            me.kc * 2 + me.t,
            me.kc * 2 + 1 - me.t,
            me.kyc * 2 + me.t,
            me.kyc * 2 + 1 - me.t,
        )

    def near(self, which, block):
        return self.wires.copy(
            self.first + which, self.slot(block), self.slot(block), self.me.core
        )

    def far(self, which, block):
        src = self.src if block is None else self.slot(block)
        dst = self.slot(self.me.q if block is None else block)
        return self.wires.copy(self.first + 4 + which, src, dst, self.me.cross[which])

    def own(self):
        return self.wires.copy(self.first, self.src, self.slot(self.me.q), self.me.core)

    def start(self):
        for which in range(3):
            self.far(which, None).start()
        self.own().start()

    def forward(self):
        for which in range(3):
            self.far(which, self.from_cross[which]).wait_recv()
            self.near(1 + which, self.from_cross[which]).start()

    def finish(self):
        for which in range(4):
            self.near(which, self.from_core[which]).wait_recv()

    def drain(self):
        self.own().wait_send()
        for which in range(3):
            self.far(which, None).wait_send()
            self.near(1 + which, self.from_cross[which]).wait_send()


class LineGather:
    def __init__(self, me, wires, views):
        self.me, self.wires, self.views = me, wires, views
        self.first = wires.take(6 * len(views))

    def part(self, way, hop, which, block):
        z = self.me.z
        view = self.views[which](block)
        slot = self.first + (way * 3 + hop) * len(self.views) + which
        return self.wires.copy(slot, view, view, self.me.line(z + 1 if way == 0 else z - 1))

    def each(self, way, hop, block, act):
        for which in range(len(self.views)):
            act(self.part(way, hop, which, block))

    def send(self, hop, act):
        z = self.me.z

        @pl.when((z >= hop) & (z < LINE - 1))
        def _():
            self.each(0, hop, z - hop, act)

        @pl.when((z + hop < LINE) & (z > 0))
        def _():
            self.each(1, hop, z + hop, act)

    def arrive(self, hop):
        z = self.me.z

        @pl.when(z > hop)
        def _():
            self.each(0, hop, z - 1 - hop, lambda copy: copy.wait_recv())

        @pl.when(z + 1 + hop < LINE)
        def _():
            self.each(1, hop, z + 1 + hop, lambda copy: copy.wait_recv())

    def start(self):
        self.send(0, lambda copy: copy.start())

    def relay(self, hop):
        self.arrive(hop - 1)
        self.send(hop, lambda copy: copy.start())

    def finish(self):
        self.arrive(LINE - 2)

    def drain(self):
        for hop in range(LINE - 1):
            self.send(hop, lambda copy: copy.wait_send())


class LineReduce:
    def __init__(self, me, wires, held, landed):
        self.me, self.wires, self.held, self.landed = me, wires, held, landed
        self.first = wires.take(2 * LINE)

    def copy(self, way, block):
        z = self.me.z
        device = self.me.line(z - 1 if way == 0 else z + 1)
        return self.wires.copy(
            self.first + way * LINE + block, self.held(block), self.landed(way, block), device
        )

    def join(self, way, block):
        self.copy(way, block).wait_recv()
        total = self.held(block)[...].astype(F32) + self.landed(way, block)[...].astype(F32)
        self.held(block)[...] = total.astype(BF16)

    def step(self, index):
        z = self.me.z
        low, high = index, LINE - 1 - index

        @pl.when(z > low)
        def _():
            @pl.when(z < LINE - 1)
            def _():
                self.join(0, low)

            self.copy(0, low).start()

        @pl.when(z < high)
        def _():
            @pl.when(z > 0)
            def _():
                self.join(1, high)

            self.copy(1, high).start()

    def finish(self):
        z = self.me.z

        @pl.when(z < LINE - 1)
        def _():
            self.join(0, z)

        @pl.when(z > 0)
        def _():
            self.join(1, z)

    def drain(self):
        z = self.me.z
        for index in range(LINE - 1):

            @pl.when(z > index)
            def _():
                self.copy(0, index).wait_send()

            @pl.when(z < LINE - 1 - index)
            def _():
                self.copy(1, LINE - 1 - index).wait_send()


class PlaneReduce:
    def __init__(self, me, wires, part, paired, crossed):
        self.me, self.wires = me, wires
        self.part, self.paired, self.crossed = part, paired, crossed
        self.first = wires.take(5)
        self.blocks = (me.k * 2 + 1 - me.t, me.ky * 2 + me.t, me.ky * 2 + 1 - me.t)

    def pair(self, y):
        rows = rows_of(y * 2 + 1 - self.me.c, SEQ)
        return self.wires.copy(
            self.first + y, self.part.at[rows], self.paired.at[y], self.me.core
        )

    def start(self):
        for y in range(2):
            self.pair(y).start()

    def cross(self, which):
        return self.wires.copy(
            self.first + 2 + which,
            self.part.at[rows_of(self.blocks[which], 128)],
            self.crossed.at[which],
            self.me.cross[which],
        )

    def middle(self):
        for y in range(2):
            self.pair(y).wait_recv()
            rows = rows_of(y * 2 + self.me.c, SEQ)
            total = self.part[rows].astype(F32) + self.paired[y].astype(F32)
            self.part[rows] = total.astype(BF16)
        for which in range(3):
            self.cross(which).start()

    def finish(self):
        for which in range(3):
            self.cross(which).wait_recv()
        total = self.part[rows_of(self.me.q, 128)].astype(F32)
        for which in range(3):
            total = total + self.crossed[which].astype(F32)
        return total

    def drain(self):
        for y in range(2):
            self.pair(y).wait_send()
        for which in range(3):
            self.cross(which).wait_send()


def layer_kernel(
    x_hbm,
    g_hbm,
    small_hbm,
    qkv_hbm,
    dense_hbm,
    up_hbm,
    down_hbm,
    turn_ref,
    layer_out_ref,
    input_grad_ref,
    qkv_grad_ref,
    dense_grad_ref,
    up_grad_ref,
    down_grad_ref,
    small_out_ref,
    x_all,
    g_all,
    small_line,
    small_all,
    qkv_w,
    dense_w,
    up_w,
    down_w,
    vec_ref,
    bias_ref,
    normed_a,
    normed_m,
    context_ref,
    turned_grad,
    active_ref,
    hidden_grad,
    part_out,
    part_attn,
    part_mlp,
    paired_ref,
    crossed_ref,
    up_held,
    up_landed,
    down_held,
    down_landed,
    qkv_held,
    qkv_landed,
    up_final,
    qkv_final,
    dense_held,
    dense_final,
    qkv_bias_held,
    qkv_bias_final,
    up_bias_held,
    up_bias_final,
    sums_held,
    sums_core,
    sums_cross,
    sums_line,
    sends,
    arrivals,
    local_sems,
):
    me = Place()
    wires = Wires(sends, arrivals)
    z, k, t = me.z, me.k, me.t

    barrier = pltpu.get_barrier_semaphore()

    def greet(device):
        pl.semaphore_signal(barrier, inc=1, device_id=device, device_id_type=MESH_ID)

    greet(me.core)
    greet(me.at(z, me.kyc, t))
    for device in me.cross:
        greet(device)
    for step in range(1, LINE):
        greet(me.line((z + step) % LINE))
    for other in range(4):

        @pl.when((k != z) | (z != other))
        def _():
            greet(me.at(other, z, t))

        @pl.when((k != z) | (k != other))
        def _():
            greet(me.at(k, other, t))

    pl.semaphore_wait(barrier, jnp.where(k == z, 14, 16))

    local_copies = []

    def local(src, dst):
        copy = pltpu.make_async_copy(src, dst, local_sems.at[len(local_copies)])
        local_copies.append(copy)
        copy.start()

    seat = pl.ds(pl.multiple_of(z * 256 + k * 64, 64), 64)
    local(qkv_hbm.at[:, :, rows_of(k, PAIR)], qkv_w.at[:, seat, :])
    local(x_hbm, x_all.at[rows_of(me.q, 128)])
    local(g_hbm, g_all.at[rows_of(me.q, 128)])
    for other in range(LINE):
        local(
            up_hbm.at[:, rows_of(other * 4 + k, 128)],
            up_w.at[seat, pl.ds(other * 128, 128)],
        )
    local(down_hbm, down_w.at[rows_of(z, 128)])
    local(small_hbm, small_line.at[z])

    first_small = wires.take(3)

    def small_copy(step, origin):
        return wires.copy(
            first_small + step - 1,
            small_hbm,
            small_line.at[origin],
            me.line((z + step) % LINE),
        )

    for step in range(1, LINE):
        small_copy(step, z).start()

    peers = (me.kc, me.ky, me.kyc)
    first_qkv = wires.take(3)

    def qkv_copy(which, origin):
        peer = peers[which]
        place = pl.ds(pl.multiple_of(z * 256 + origin * 64, 64), 64)
        return wires.copy(
            first_qkv + which,
            qkv_hbm.at[:, :, rows_of(peer, PAIR)],
            qkv_w.at[:, place, :],
            me.at(z, peer, t),
        )

    for which in range(3):
        qkv_copy(which, k).start()

    gather_x = PlaneGather(me, wires, x_hbm, lambda block: x_all.at[rows_of(block, 128)])
    gather_x.start()

    first_dense = wires.take(4)

    def dense_copy(other):
        return wires.copy(
            first_dense + k, dense_hbm, dense_w.at[rows_of(k, 32)], me.at(other, z, t)
        )

    first_dense_send = wires.take(4)

    def dense_send(other):
        return pltpu.make_async_remote_copy(
            src_ref=dense_hbm,
            dst_ref=dense_w.at[rows_of(k, 32)],
            send_sem=sends.at[first_dense_send + other],
            recv_sem=arrivals.at[first_dense + k],
            device_id=me.at(other, z, t),
            device_id_type=MESH_ID,
        )

    def dense_arrival(other):
        return wires.copy(
            first_dense + other, dense_hbm, dense_w.at[rows_of(other, 32)], me.at(k, other, t)
        )

    own_dense = pltpu.make_async_copy(
        dense_hbm, dense_w.at[rows_of(k, 32)], local_sems.at[len(local_copies)]
    )
    for other in range(4):

        @pl.when((k != z) | (z != other))
        def _():
            dense_send(other).start()

        @pl.when((k == z) & (z == other))
        def _():
            own_dense.start()

    first_up = wires.take(12)

    def up_copy(which, other, origin):
        peer = peers[which]
        place = pl.ds(pl.multiple_of(z * 256 + origin * 64, 64), 64)
        return wires.copy(
            first_up + which * 4 + other,
            up_hbm.at[:, rows_of(other * 4 + peer, 128)],
            up_w.at[place, pl.ds(other * 128, 128)],
            me.at(z, peer, t),
        )

    for which in range(3):
        for other in range(LINE):
            up_copy(which, other, k).start()

    gather_g = PlaneGather(me, wires, g_hbm, lambda block: g_all.at[rows_of(block, 128)])
    gather_g.start()

    for copy in local_copies:
        copy.wait()

    for which in range(3):
        qkv_copy(which, peers[which]).wait_recv()
    line_qkv = LineGather(me, wires, [lambda s: qkv_w.at[:, rows_of(s, 256), :]])
    line_qkv.start()
    for which in range(3):
        for other in range(LINE):
            up_copy(which, other, peers[which]).wait_recv()
    line_mlp = LineGather(
        me,
        wires,
        [lambda s: up_w.at[rows_of(s, 256)], lambda s: down_w.at[rows_of(s, 128)]],
    )
    line_mlp.start()

    for step in range(1, LINE):
        small_copy(step, (z + LINE - step) % LINE).wait_recv()
    gather_small = PlaneGather(me, wires, small_line, lambda block: small_all.at[block])
    own_small = pltpu.make_async_copy(
        small_line, small_all.at[me.q], local_sems.at[len(local_copies) + 1]
    )
    own_small.start()
    gather_small.start()
    gather_x.forward()
    gather_small.forward()
    gather_x.finish()
    gather_small.finish()
    own_small.wait()

    table = small_all[...].reshape(256, 128).astype(BF16)
    line_id = lax.broadcasted_iota(jnp.int32, (256, WIDTH), 0)
    column = lax.broadcasted_iota(jnp.int32, (256, WIDTH), 1)
    owner = ((line_id >> 3) & 3) * 8 + (line_id >> 5)
    lane_row = lax.broadcasted_iota(jnp.int32, (128, WIDTH), 0)
    lane_col = lax.broadcasted_iota(jnp.int32, (128, WIDTH), 1) & 31
    for kind, count, base in ((0, 4, 0), (1, 2, 4)):
        chosen = (owner == (column >> 5)) & ((line_id & 7) == kind)
        spread = tn(table, jnp.where(chosen, 1.0, 0.0).astype(BF16))
        for which in range(count):
            picked = jnp.where(lane_row == lane_col + which * 32, spread, 0.0)
            vec_ref[base + which : base + which + 1, :] = jnp.sum(picked, axis=0, keepdims=True)
    line_id = line_id[:, :PAIR]
    column = column[:, :PAIR]
    chosen = (
        (((line_id >> 3) & 3) == k)
        & ((line_id >> 5) == (column >> 5) * 2 + t)
        & ((line_id & 7) == 2)
    )
    spread = tn(table, jnp.where(chosen, 1.0, 0.0).astype(BF16))
    for which in range(3):
        picked = jnp.where(lane_row[:, :PAIR] == lane_col[:, :PAIR] + which * 32, spread, 0.0)
        bias_ref[which : which + 1, :] = jnp.sum(picked, axis=0, keepdims=True)

    def norm_rows(rows):
        values = x_all[rows].astype(F32)
        centred = values - jnp.mean(values, axis=-1, keepdims=True)
        rate = lax.rsqrt(jnp.mean(centred * centred, axis=-1, keepdims=True) + NORM_EPS)
        return centred * rate, rate

    def norm_block(block, carry):
        rows = rows_of(block, 128)
        unit, _ = norm_rows(rows)
        normed_a[rows] = (unit * vec_ref[0:1, :] + vec_ref[1:2, :]).astype(BF16)
        normed_m[rows] = (unit * vec_ref[2:3, :] + vec_ref[3:4, :]).astype(BF16)
        return carry

    lax.fori_loop(0, 8, norm_block, 0)

    gather_g.forward()
    gather_g.finish()
    line_qkv.relay(1)
    line_qkv.relay(2)
    line_qkv.finish()
    for other in range(4):

        @pl.when((k != z) | (k != other))
        def _():
            dense_arrival(other).wait_recv()

        @pl.when((k == z) & (z == other))
        def _():
            own_dense.wait()

    qkv_bias_held[...] = jnp.zeros_like(qkv_bias_held)
    scale = HD**-0.5

    def attend(seq, carry):
        rows = rows_of(seq, SEQ)
        cosine, toward, away = turn_ref[0], turn_ref[1], turn_ref[2]
        normed = normed_a[rows]

        def project(which):
            return nn(normed, qkv_w[which]) + bias_ref[which : which + 1, :]

        def turned(field):
            return (
                field * cosine
                + pltpu.roll(field, ROT // 2, 1) * away
                + pltpu.roll(field, PAIR - ROT // 2, 1) * toward
            )

        def turned_back(field):
            return (
                field * cosine
                - pltpu.roll(field, ROT // 2, 1) * away
                - pltpu.roll(field, PAIR - ROT // 2, 1) * toward
            )

        query = turned(project(0)).astype(BF16)
        key = turned(project(1)).astype(BF16)
        value = project(2).astype(BF16)
        context_grad = nt(g_all[rows], dense_w[...]).astype(BF16)

        spans = small_all[seq * 2, z, 1:2, :]
        down_pos = lax.broadcasted_iota(jnp.int32, (SEQ, 1), 0).astype(F32)
        over_pos = lax.broadcasted_iota(jnp.int32, (1, SEQ), 1).astype(F32)

        def labels(place):
            total = jnp.zeros(place.shape, F32)
            for span in range(2):
                begin = spans[:, 64 + span : 65 + span]
                end = begin + spans[:, 66 + span : 67 + span]
                total = total + jnp.where((place >= begin) & (place < end), span + 1.0, 0.0)
            return total

        down_label, over_label = labels(down_pos), labels(over_pos)
        allowed = (over_pos <= down_pos) | ((down_label == over_label) & (down_label > 0.0))

        lane = lax.broadcasted_iota(jnp.int32, (SEQ, PAIR), 1)
        parts = []
        for head in range(2):
            mine = (lane >= HD) if head else (lane < HD)
            zero = jnp.zeros_like(query)
            scores = nt(jnp.where(mine, query, zero), key) * scale
            scores = jnp.where(allowed, scores, NEG_FILL)
            exponent = jnp.exp(scores - jnp.max(scores, axis=-1, keepdims=True))
            probs = exponent * (1.0 / jnp.sum(exponent, axis=-1, keepdims=True))
            low = probs.astype(BF16)
            prob_grad = nt(jnp.where(mine, context_grad, zero), value)
            inner = jnp.sum(prob_grad * probs, axis=-1, keepdims=True)
            score_grad = (probs * (prob_grad - inner)).astype(BF16)
            parts.append(
                (
                    nn(low, value),
                    tn(low, context_grad),
                    nn(score_grad, key) * scale,
                    tn(score_grad, query) * scale,
                )
            )
        context, value_grad, query_grad, key_grad = (
            jnp.where(lane < HD, first, second) for first, second in zip(*parts)
        )
        context_ref[rows] = context.astype(BF16)
        grads = (
            turned_back(query_grad).astype(BF16),
            turned_back(key_grad).astype(BF16),
            value_grad.astype(BF16),
        )
        total = jnp.zeros((SEQ, WIDTH), F32)
        for which in range(3):
            turned_grad[rows, which * PAIR : (which + 1) * PAIR] = grads[which]
            qkv_bias_held[which : which + 1, :] += jnp.sum(
                grads[which].astype(F32), axis=0, keepdims=True
            )
            total = total + nt(grads[which], qkv_w[which])
        part_attn[rows] = total.astype(BF16)
        return carry

    lax.fori_loop(0, 4, attend, 0)

    reduce_attn = PlaneReduce(me, wires, part_attn, paired_ref.at[0], crossed_ref.at[0])
    reduce_attn.start()

    dense_part = tn(context_ref[...], g_all[...])
    dense_held[...] = dense_part.astype(BF16)

    def qkv_block(block, carry):
        grad = tn(normed_a[:, rows_of(block, 256)], turned_grad[...])
        for which in range(3):
            qkv_held[block, which] = grad[:, which * PAIR : (which + 1) * PAIR].astype(BF16)
        return carry

    lax.fori_loop(0, 4, qkv_block, 0)

    first_back = wires.take(8)
    first_back_send = wires.take(8)

    def back_send(other, kind):
        src = (dense_held.at[pl.ds(other * 32, 32)], qkv_bias_held)[kind]
        dst = (dense_final, qkv_bias_final)[kind].at[z]
        return pltpu.make_async_remote_copy(
            src_ref=src,
            dst_ref=dst,
            send_sem=sends.at[first_back_send + kind * 4 + other],
            recv_sem=arrivals.at[first_back + kind * 4 + z],
            device_id=me.at(k, other, t),
            device_id_type=MESH_ID,
        )

    def back_arrival(other, kind):
        src = (dense_held.at[pl.ds(0, 32)], qkv_bias_held)[kind]
        dst = (dense_final, qkv_bias_final)[kind].at[other]
        return wires.copy(first_back + kind * 4 + other, src, dst, me.at(other, z, t))

    for other in range(4):

        @pl.when((k != z) | (k != other))
        def _():
            back_send(other, 0).start()
            back_send(other, 1).start()

        @pl.when((k == z) & (k == other))
        def _():
            dense_final[z] = dense_held[other * 32 : (other + 1) * 32]
            qkv_bias_final[z] = qkv_bias_held[...]

    reduce_qkv = LineReduce(
        me, wires, lambda s: qkv_held.at[s], lambda way, s: qkv_landed.at[way, s]
    )
    reduce_attn.middle()
    for index in range(LINE - 1):
        reduce_qkv.step(index)

    line_mlp.relay(1)
    line_mlp.relay(2)
    line_mlp.finish()

    up_bias_held[...] = jnp.zeros_like(up_bias_held)
    up_bias = jnp.concatenate([small_all[me.q, s, 3:4, :] for s in range(LINE)], axis=1)

    def feed(tile, carry):
        rows = rows_of(tile, 128)
        cotangent = g_all[rows]
        hidden = nn(normed_m[rows], up_w[...]) + up_bias
        share = (1.0 + lax.erf(hidden * 0.5**0.5)) * 0.5
        slope = share + hidden * jnp.exp(hidden * hidden * -0.5) * (2.0 * np.pi) ** -0.5
        active = (hidden * share).astype(BF16)
        grad = (nt(cotangent, down_w[...]) * slope).astype(BF16)
        active_ref[rows] = active
        hidden_grad[rows] = grad
        up_bias_held[0:1, :] += jnp.sum(grad.astype(F32), axis=0, keepdims=True)
        mixed = nn(context_ref[rows], dense_w[...]) + nn(active, down_w[...])
        part_out[rows] = mixed.astype(BF16)
        part_mlp[rows] = nt(grad, up_w[...]).astype(BF16)
        return carry

    lax.fori_loop(0, 8, feed, 0)

    reduce_out = PlaneReduce(me, wires, part_out, paired_ref.at[1], crossed_ref.at[1])
    reduce_out.start()
    reduce_mlp = PlaneReduce(me, wires, part_mlp, paired_ref.at[2], crossed_ref.at[2])
    reduce_mlp.start()

    def down_block(block, carry):
        down_held[block] = tn(active_ref[:, rows_of(block, 128)], g_all[...]).astype(BF16)
        return carry

    lax.fori_loop(0, 4, down_block, 0)
    reduce_down = LineReduce(
        me, wires, lambda s: down_held.at[s], lambda way, s: down_landed.at[way, s]
    )
    reduce_down.step(0)

    def up_block(block, carry):
        up_held[block] = tn(normed_m[:, rows_of(block, 256)], hidden_grad[...]).astype(BF16)
        return carry

    lax.fori_loop(0, 4, up_block, 0)
    reduce_up = LineReduce(
        me, wires, lambda s: up_held.at[s], lambda way, s: up_landed.at[way, s]
    )
    reduce_down.step(1)
    reduce_up.step(0)
    reduce_down.step(2)
    reduce_up.step(1)
    reduce_up.step(2)
    reduce_out.middle()
    reduce_mlp.middle()

    first_ub = wires.take(3)

    def up_bias_copy(step, block, origin):
        return wires.copy(
            first_ub + step - 1,
            up_bias_held.at[:, rows_of(block, 128)],
            up_bias_final.at[origin],
            me.line((z + step) % LINE),
        )

    for step in range(1, LINE):
        up_bias_copy(step, (z + step) % LINE, z).start()
    up_bias_final[z] = up_bias_held[:, rows_of(z, 128)]

    reduce_qkv.finish()
    first_qf = wires.take(3)

    def qkv_out_copy(which, origin):
        peer = peers[which]
        return wires.copy(
            first_qf + which,
            qkv_held.at[z, :, rows_of(peer, 64), :],
            qkv_final.at[origin],
            me.at(z, peer, t),
        )

    for which in range(3):
        qkv_out_copy(which, k).start()
    qkv_final[k] = qkv_held[z, :, rows_of(k, 64), :]

    own = rows_of(me.q, 128)
    cotangent = g_all[own].astype(F32)
    mixed = reduce_out.finish()
    layer_out_ref[...] = (
        x_all[own].astype(F32) + mixed + vec_ref[4:5, :] + vec_ref[5:6, :]
    ).astype(BF16)
    from_attn = reduce_attn.finish()
    from_mlp = reduce_mlp.finish()
    unit, rate = norm_rows(own)
    sums_held[...] = jnp.zeros_like(sums_held)
    for which, field in enumerate(
        (from_attn * unit, from_attn, from_mlp * unit, from_mlp, cotangent)
    ):
        sums_held[which : which + 1, :] = jnp.sum(field, axis=0, keepdims=True)
    first_sums = wires.take(7)

    def sums_core_copy():
        return wires.copy(first_sums, sums_held.at[...], sums_core, me.core)

    sums_core_copy().start()
    pulled = from_attn * vec_ref[0:1, :] + from_mlp * vec_ref[2:3, :]
    pulled = (
        pulled
        - jnp.mean(pulled, axis=-1, keepdims=True)
        - unit * jnp.mean(pulled * unit, axis=-1, keepdims=True)
    )
    input_grad_ref[...] = (cotangent + rate * pulled).astype(BF16)

    sums_core_copy().wait()
    sums_core[...] = sums_held[...] + sums_core[...]

    def sums_cross_copy(which):
        return wires.copy(
            first_sums + 1 + which, sums_core, sums_cross.at[which], me.cross[which]
        )

    for which in range(3):
        sums_cross_copy(which).start()
    for which in range(3):
        sums_cross_copy(which).wait()
    sums_held[...] = sums_core[...] + sums_cross[0] + sums_cross[1] + sums_cross[2]

    def sums_line_copy(step, block, origin):
        return wires.copy(
            first_sums + 4 + step - 1,
            sums_held.at[:, rows_of(block, 256)],
            sums_line.at[origin],
            me.line((z + step) % LINE),
        )

    for step in range(1, LINE):
        sums_line_copy(step, (z + step) % LINE, z).start()
    sums_line[z] = sums_held[:, rows_of(z, 256)]

    reduce_down.finish()
    down_grad_ref[...] = down_held[z].astype(F32)
    reduce_up.finish()
    first_uf = wires.take(3)

    def up_out_copy(which, origin):
        peer = peers[which]
        return wires.copy(
            first_uf + which,
            up_held.at[z, rows_of(peer, 64), :],
            up_final.at[origin],
            me.at(z, peer, t),
        )

    for which in range(3):
        up_out_copy(which, k).start()
    up_final[k] = up_held[z, rows_of(k, 64), :]

    for which in range(3):
        qkv_out_copy(which, peers[which]).wait_recv()
    for origin in range(4):
        qkv_grad_ref[:, :, origin * PAIR : (origin + 1) * PAIR] = qkv_final[origin].astype(F32)
    for other in range(4):

        @pl.when((k != z) | (z != other))
        def _():
            back_arrival(other, 0).wait_recv()
            back_arrival(other, 1).wait_recv()

    dense_grad_ref[...] = (
        dense_final[0].astype(F32)
        + dense_final[1].astype(F32)
        + dense_final[2].astype(F32)
        + dense_final[3].astype(F32)
    )
    for which in range(3):
        up_out_copy(which, peers[which]).wait_recv()
    for origin in range(4):
        for other in range(LINE):
            first = (other * 4 + origin) * 128
            up_grad_ref[:, first : first + 128] = up_final[
                origin, :, other * 128 : (other + 1) * 128
            ].astype(F32)

    for step in range(1, LINE):
        sums_line_copy(step, z, (z + LINE - step) % LINE).wait_recv()
        up_bias_copy(step, z, (z + LINE - step) % LINE).wait_recv()
    sums = sums_line[0] + sums_line[1] + sums_line[2] + sums_line[3]
    sums = jnp.where(k >= 2, sums[:, 128:], sums[:, :128])
    small_out_ref[0:8, :] = pltpu.roll(sums, (128 - (me.q % 4) * 32) % 128, 1)
    bias_sum = qkv_bias_final[0] + qkv_bias_final[1] + qkv_bias_final[2] + qkv_bias_final[3]
    small_out_ref[8:16, :] = pltpu.roll(bias_sum, (128 - k * 32) % 128, 1)
    small_out_ref[16:24, :] = (
        up_bias_final[0] + up_bias_final[1] + up_bias_final[2] + up_bias_final[3]
    )

    for step in range(1, LINE):
        small_copy(step, z).wait_send()
        up_bias_copy(step, (z + step) % LINE, z).wait_send()
        sums_line_copy(step, (z + step) % LINE, z).wait_send()
    for which in range(3):
        qkv_copy(which, k).wait_send()
        qkv_out_copy(which, k).wait_send()
        up_out_copy(which, k).wait_send()
        for other in range(LINE):
            up_copy(which, other, k).wait_send()
    for other in range(4):

        @pl.when((k != z) | (z != other))
        def _():
            dense_send(other).wait_send()

        @pl.when((k != z) | (k != other))
        def _():
            back_send(other, 0).wait_send()
            back_send(other, 1).wait_send()

    for item in (
        gather_x,
        gather_g,
        gather_small,
        line_qkv,
        line_mlp,
        reduce_attn,
        reduce_out,
        reduce_mlp,
        reduce_qkv,
        reduce_down,
        reduce_up,
    ):
        item.drain()


def plane_layer(
    hidden_in,
    out_grad,
    span_start,
    span_length,
    attn_gain,
    attn_shift,
    mlp_gain,
    mlp_shift,
    qkv_weight,
    qkv_bias,
    dense_weight,
    dense_bias,
    up_weight,
    up_bias,
    down_weight,
    down_bias,
):
    smalls = jnp.concatenate(
        [
            attn_gain.astype(F32),
            attn_shift.astype(F32),
            mlp_gain.astype(F32),
            mlp_shift.astype(F32),
            dense_bias.astype(F32),
            down_bias.astype(F32),
            span_start[0].astype(F32),
            span_length[0].astype(F32),
            jnp.zeros((60,), F32),
            qkv_bias.astype(F32).reshape(96),
            jnp.zeros((32,), F32),
            up_bias.astype(F32),
            jnp.zeros((512,), F32),
        ]
    ).reshape(8, 128)
    vmem = pl.BlockSpec(memory_space=pltpu.VMEM)
    anywhere = pl.BlockSpec(memory_space=pl.ANY)
    tokens = 4 * SEQ
    outs = pl.pallas_call(
        layer_kernel,
        out_shape=(
            jax.ShapeDtypeStruct((128, WIDTH), BF16),
            jax.ShapeDtypeStruct((128, WIDTH), BF16),
            jax.ShapeDtypeStruct((3, 64, 512), F32),
            jax.ShapeDtypeStruct((32, WIDTH), F32),
            jax.ShapeDtypeStruct((64, 2048), F32),
            jax.ShapeDtypeStruct((128, WIDTH), F32),
            jax.ShapeDtypeStruct((24, 128), F32),
        ),
        in_specs=[anywhere] * 7 + [vmem],
        out_specs=(vmem,) * 7,
        scratch_shapes=[
            pltpu.VMEM((tokens, WIDTH), BF16),
            pltpu.VMEM((tokens, WIDTH), BF16),
            pltpu.VMEM((LINE, 8, 128), F32),
            pltpu.VMEM((8, LINE, 8, 128), F32),
            pltpu.VMEM((3, WIDTH, PAIR), BF16),
            pltpu.VMEM((PAIR, WIDTH), BF16),
            pltpu.VMEM((WIDTH, HID), BF16),
            pltpu.VMEM((HID, WIDTH), BF16),
            pltpu.VMEM((8, WIDTH), F32),
            pltpu.VMEM((8, PAIR), F32),
            pltpu.VMEM((tokens, WIDTH), BF16),
            pltpu.VMEM((tokens, WIDTH), BF16),
            pltpu.VMEM((tokens, PAIR), BF16),
            pltpu.VMEM((tokens, 3 * PAIR), BF16),
            pltpu.VMEM((tokens, HID), BF16),
            pltpu.VMEM((tokens, HID), BF16),
            pltpu.VMEM((tokens, WIDTH), BF16),
            pltpu.VMEM((tokens, WIDTH), BF16),
            pltpu.VMEM((tokens, WIDTH), BF16),
            pltpu.VMEM((3, 2, SEQ, WIDTH), BF16),
            pltpu.VMEM((3, 3, 128, WIDTH), BF16),
            pltpu.VMEM((LINE, 256, HID), BF16),
            pltpu.VMEM((2, LINE, 256, HID), BF16),
            pltpu.VMEM((LINE, 128, WIDTH), BF16),
            pltpu.VMEM((2, LINE, 128, WIDTH), BF16),
            pltpu.VMEM((LINE, 3, 256, PAIR), BF16),
            pltpu.VMEM((2, LINE, 3, 256, PAIR), BF16),
            pltpu.VMEM((4, 64, HID), BF16),
            pltpu.VMEM((4, 3, 64, PAIR), BF16),
            pltpu.VMEM((PAIR, WIDTH), BF16),
            pltpu.VMEM((LINE, 32, WIDTH), BF16),
            pltpu.VMEM((8, PAIR), F32),
            pltpu.VMEM((LINE, 8, PAIR), F32),
            pltpu.VMEM((8, HID), F32),
            pltpu.VMEM((LINE, 8, 128), F32),
            pltpu.VMEM((8, WIDTH), F32),
            pltpu.VMEM((8, WIDTH), F32),
            pltpu.VMEM((3, 8, WIDTH), F32),
            pltpu.VMEM((LINE, 8, 256), F32),
            pltpu.SemaphoreType.DMA((160,)),
            pltpu.SemaphoreType.DMA((160,)),
            pltpu.SemaphoreType.DMA((16,)),
        ],
        compiler_params=pltpu.CompilerParams(
            collective_id=0, has_side_effects=True, vmem_limit_bytes=60 * 2**20
        ),
    )(
        hidden_in,
        out_grad,
        smalls,
        jnp.transpose(qkv_weight, (1, 0, 2)),
        dense_weight,
        up_weight,
        down_weight,
        jnp.asarray(turn_tables()),
    )
    layer_out, input_grad, qkv_grad, dense_grad, up_grad, down_grad, small_out = outs
    bias_total = small_out[4, :32]
    return (
        layer_out,
        input_grad,
        small_out[0, :32],
        small_out[1, :32],
        small_out[2, :32],
        small_out[3, :32],
        jnp.transpose(qkv_grad, (1, 0, 2)),
        small_out[8:11, :32],
        dense_grad,
        bias_total,
        up_grad,
        small_out[16],
        down_grad,
        bias_total,
    )


def solution(mesh):
    in_specs = (
        P(("dp", "tensor"), None),
        P(("dp", "tensor"), None),
        P("dp", None),
        P("dp", None),
        P(("dp", "tensor")),
        P(("dp", "tensor")),
        P(("dp", "tensor")),
        P(("dp", "tensor")),
        P("dp", None, "tensor"),
        P(None, ("tensor", "dp")),
        P(("tensor", "dp"), None),
        P(("dp", "tensor")),
        P("dp", "tensor"),
        P(("tensor", "dp")),
        P(("tensor", "dp"), None),
        P(("dp", "tensor")),
    )
    out_specs = (
        P(("dp", "tensor"), None),
        P(("dp", "tensor"), None),
        P(("dp", "tensor")),
        P(("dp", "tensor")),
        P(("dp", "tensor")),
        P(("dp", "tensor")),
        P("dp", None, "tensor"),
        P(None, ("tensor", "dp")),
        P(("tensor", "dp"), None),
        P(("dp", "tensor")),
        P("dp", "tensor"),
        P(("tensor", "dp")),
        P(("tensor", "dp"), None),
        P(("dp", "tensor")),
    )
    fast = mesh.shape["dp"] == 16 and mesh.shape["tensor"] == 2
    return jax.shard_map(plane_layer if fast else shards, mesh=mesh, in_specs=in_specs, out_specs=out_specs, check_vma=False)
```

```python
import jax
import jax.numpy as jnp
import numpy as np
from jax import lax
from jax.experimental import pallas as pl
from jax.experimental.pallas import tpu as pltpu
from jax.sharding import PartitionSpec as P

HD = 64
ROT = 16


NORM_EPS = 1e-05
NEG_FILL = -1000000000.0


def layer_norm(rows_in, gain_vec, shift_vec):
    mean_row = jnp.mean(rows_in, axis=-1, keepdims=True)
    centred = rows_in - mean_row
    spread = jnp.mean(centred * centred, axis=-1, keepdims=True)
    return centred * lax.rsqrt(spread + NORM_EPS) * gain_vec + shift_vec


def rotary_tables(length):
    position = jnp.arange(length, dtype=jnp.float32)
    rates = 10000.0 ** (-jnp.arange(ROT // 2, dtype=jnp.float32) * (2.0 / ROT))
    angles = position[:, None] * rates[None, :]
    angles = jnp.concatenate([angles, angles], axis=-1)[:, None, :]
    return (jnp.cos(angles), jnp.sin(angles))


def rotate(field_in, cosine, sines):
    turned = field_in[..., :ROT]
    first_half = turned[..., : ROT // 2]
    second_half = turned[..., ROT // 2 :]
    swapped = jnp.concatenate([-second_half, first_half], axis=-1)
    return jnp.concatenate([turned * cosine + swapped * sines, field_in[..., ROT:]], axis=-1)


def gelu_exact(values_in):
    return jax.nn.gelu(values_in, approximate=False)


def shards(
    hidden_in,
    out_grad,
    span_start,
    span_length,
    attn_gain,
    attn_shift,
    mlp_gain,
    mlp_shift,
    qkv_weight,
    qkv_bias,
    dense_weight,
    dense_bias,
    up_weight,
    up_bias,
    down_weight,
    down_bias,
):
    local_rows = hidden_in.shape[0]
    length = local_rows * lax.axis_size("tensor")
    block_rows = min(512, length)
    block_count = length // block_rows
    score_scale = HD ** (-0.5)
    small_full = (
        lax.all_gather(attn_gain, ("dp", "tensor"), axis=0, tiled=True),
        lax.all_gather(attn_shift, ("dp", "tensor"), axis=0, tiled=True),
        lax.all_gather(mlp_gain, ("dp", "tensor"), axis=0, tiled=True),
        lax.all_gather(mlp_shift, ("dp", "tensor"), axis=0, tiled=True),
        lax.all_gather(dense_bias, ("dp", "tensor"), axis=0, tiled=True),
        lax.all_gather(down_bias, ("dp", "tensor"), axis=0, tiled=True),
    )
    small_vecs = [item.astype(jnp.float32) for item in small_full]
    own_rows = hidden_in.astype(jnp.float32)
    normed_attn = layer_norm(own_rows, small_vecs[0], small_vecs[1]).astype(jnp.bfloat16)
    normed_mlp = layer_norm(own_rows, small_vecs[2], small_vecs[3]).astype(jnp.bfloat16)
    attn_full, mlp_full = (
        lax.all_gather(normed_attn, "tensor", axis=0, tiled=True),
        lax.all_gather(normed_mlp, "tensor", axis=0, tiled=True),
    )
    full_qkv, full_qkv_bias, full_dense, full_up, full_up_bias, full_down = (
        lax.all_gather(qkv_weight, "dp", axis=0, tiled=True),
        lax.all_gather(qkv_bias, "dp", axis=1, tiled=True),
        lax.all_gather(dense_weight, "dp", axis=0, tiled=True),
        lax.all_gather(up_weight, "dp", axis=0, tiled=True),
        lax.all_gather(up_bias, "dp", axis=0, tiled=True),
        lax.all_gather(down_weight, "dp", axis=0, tiled=True),
    )
    model_width = full_qkv.shape[0]
    head_cols = full_qkv.shape[2]
    local_heads = head_cols // HD
    projected = jnp.dot(
        attn_full, full_qkv.reshape(model_width, 3 * head_cols), preferred_element_type=jnp.float32
    )
    projected = projected + full_qkv_bias.reshape(3 * head_cols).astype(jnp.float32)
    projected = projected.reshape(length, 3, local_heads, HD)
    cosine, sines = rotary_tables(length)
    query_rows = rotate(projected[:, 0], cosine, sines).astype(jnp.bfloat16)
    key_rows = rotate(projected[:, 1], cosine, sines).astype(jnp.bfloat16)
    value_rows = projected[:, 2].astype(jnp.bfloat16)
    position = jnp.arange(length, dtype=jnp.int32)
    starts_here = span_start[0]
    lengths_here = span_length[0]
    inside = (position[None, :] >= starts_here[:, None]) & (
        position[None, :] < (starts_here + lengths_here)[:, None]
    )
    marks = (jnp.arange(starts_here.shape[0], dtype=jnp.int32) + 1)[:, None]
    labels = jnp.sum(jnp.where(inside, marks, 0), axis=0)

    def block_scores(first_row, query_block):
        raw_scores = (
            jnp.einsum("qhe,khe->hqk", query_block, key_rows, preferred_element_type=jnp.float32)
            * score_scale
        )
        row_pos = first_row + jnp.arange(block_rows, dtype=jnp.int32)
        allowed = (position[None, :] <= row_pos[:, None]) | (labels[:, None] == labels[None, :]) & (
            labels[:, None] > 0
        )
        return jnp.where(allowed[None], raw_scores, NEG_FILL)

    def attend(first_row):
        scores = block_scores(first_row, query_rows)
        row_top = jnp.max(scores, axis=-1, keepdims=True)
        exponent = jnp.exp(scores - row_top)
        summed = jnp.sum(exponent, axis=-1, keepdims=True)
        prob_low = (exponent / summed).astype(jnp.bfloat16)
        context_block = jnp.einsum(
            "hqk,khe->qhe", prob_low, value_rows, preferred_element_type=jnp.float32
        )
        return (context_block.astype(jnp.bfloat16), (row_top + jnp.log(summed))[..., 0])

    block_starts = jnp.arange(block_count, dtype=jnp.int32) * block_rows
    context_blocks, lse_blocks = lax.map(attend, block_starts)
    context = context_blocks.reshape(length, head_cols)
    attn_part = jnp.dot(context, full_dense, preferred_element_type=jnp.float32)
    attn_mixed = lax.psum_scatter(
        attn_part.astype(jnp.bfloat16), "tensor", scatter_dimension=0, tiled=True
    ).astype(jnp.float32)
    hidden = jnp.dot(mlp_full, full_up, preferred_element_type=jnp.float32) + full_up_bias.astype(
        jnp.float32
    )
    active = gelu_exact(hidden).astype(jnp.bfloat16)
    mlp_part = jnp.dot(active, full_down, preferred_element_type=jnp.float32)
    mixed_rows = attn_mixed + lax.psum_scatter(
        mlp_part.astype(jnp.bfloat16), "tensor", scatter_dimension=0, tiled=True
    ).astype(jnp.float32)
    layer_out = (own_rows + mixed_rows + small_vecs[4] + small_vecs[5]).astype(jnp.bfloat16)
    cot_full = lax.all_gather(out_grad, "tensor", axis=0, tiled=True)
    full_qkv, full_dense, full_up, full_down = (
        lax.all_gather(qkv_weight, "dp", axis=0, tiled=True),
        lax.all_gather(dense_weight, "dp", axis=0, tiled=True),
        lax.all_gather(up_weight, "dp", axis=0, tiled=True),
        lax.all_gather(down_weight, "dp", axis=0, tiled=True),
    )
    down_grad = jnp.einsum("lf,ld->fd", active, cot_full, preferred_element_type=jnp.float32)
    dense_grad = jnp.einsum("le,ld->ed", context, cot_full, preferred_element_type=jnp.float32)
    active_grad = jnp.einsum("ld,fd->lf", cot_full, full_down, preferred_element_type=jnp.float32)
    hidden_grad = jax.vjp(gelu_exact, hidden)[1](active_grad)[0].astype(jnp.bfloat16)
    up_grad = jnp.einsum("ld,lf->df", mlp_full, hidden_grad, preferred_element_type=jnp.float32)
    up_bias_grad = jnp.sum(hidden_grad, axis=0, dtype=jnp.float32)
    mlp_in_grad = jnp.einsum("lf,df->ld", hidden_grad, full_up, preferred_element_type=jnp.float32)
    context_grad = jnp.einsum("ld,ed->le", cot_full, full_dense, preferred_element_type=jnp.float32)
    context_grad = context_grad.astype(jnp.bfloat16).reshape(length, local_heads, HD)

    def attend_back(carried, inputs):
        key_acc, value_acc = carried
        first_row, lse_block = inputs
        scores = block_scores(first_row, query_rows)
        prob_rows = jnp.exp(scores - lse_block[..., None])
        prob_low = prob_rows.astype(jnp.bfloat16)
        value_acc = value_acc + jnp.einsum(
            "hqk,qhe->khe", prob_low, context_grad, preferred_element_type=jnp.float32
        )
        prob_grad = jnp.einsum(
            "qhe,khe->hqk", context_grad, value_rows, preferred_element_type=jnp.float32
        )
        score_grad = prob_rows * (
            prob_grad - jnp.sum(prob_grad * prob_rows, axis=-1, keepdims=True)
        )
        score_grad = score_grad.astype(jnp.bfloat16)
        query_grad = (
            jnp.einsum("hqk,khe->qhe", score_grad, key_rows, preferred_element_type=jnp.float32)
            * score_scale
        )
        key_acc = (
            key_acc
            + jnp.einsum("hqk,qhe->khe", score_grad, query_rows, preferred_element_type=jnp.float32)
            * score_scale
        )
        return ((key_acc, value_acc), query_grad)

    zero_rows = jnp.zeros((length, local_heads, HD), jnp.float32)
    (key_grad, value_grad), query_blocks = lax.scan(
        attend_back, (zero_rows, zero_rows), (block_starts, lse_blocks)
    )
    query_grad = query_blocks.reshape(length, local_heads, HD)

    def turn(field_in):
        return rotate(field_in, cosine, sines)

    turn_back = jax.vjp(turn, zero_rows)[1]
    projected_grad = jnp.stack(
        [turn_back(query_grad)[0], turn_back(key_grad)[0], value_grad], axis=1
    )
    projected_grad = projected_grad.astype(jnp.bfloat16).reshape(length, 3 * head_cols)
    qkv_weight_grad = jnp.einsum(
        "ld,lc->dc", attn_full, projected_grad, preferred_element_type=jnp.float32
    )
    qkv_weight_grad = qkv_weight_grad.reshape(model_width, 3, head_cols)
    qkv_bias_grad = jnp.sum(projected_grad, axis=0, dtype=jnp.float32).reshape(3, head_cols)
    attn_in_grad = jnp.einsum(
        "lc,dc->ld",
        projected_grad,
        full_qkv.reshape(model_width, 3 * head_cols),
        preferred_element_type=jnp.float32,
    )
    reduced = (
        lax.psum_scatter(qkv_weight_grad, "dp", scatter_dimension=0, tiled=True),
        lax.psum_scatter(qkv_bias_grad, "dp", scatter_dimension=1, tiled=True),
        lax.psum_scatter(dense_grad, "dp", scatter_dimension=0, tiled=True),
        lax.psum_scatter(up_grad, "dp", scatter_dimension=0, tiled=True),
        lax.psum_scatter(up_bias_grad, "dp", scatter_dimension=0, tiled=True),
        lax.psum_scatter(down_grad, "dp", scatter_dimension=0, tiled=True),
    )
    attn_local, mlp_local = (
        lax.psum_scatter(
            attn_in_grad.astype(jnp.bfloat16), "tensor", scatter_dimension=0, tiled=True
        ).astype(jnp.float32),
        lax.psum_scatter(
            mlp_in_grad.astype(jnp.bfloat16), "tensor", scatter_dimension=0, tiled=True
        ).astype(jnp.float32),
    )
    pull_attn = jax.vjp(layer_norm, own_rows, small_vecs[0], small_vecs[1])[1]
    pull_mlp = jax.vjp(layer_norm, own_rows, small_vecs[2], small_vecs[3])[1]
    rows_grad_attn, gain_grad_attn, shift_grad_attn = pull_attn(attn_local)
    rows_grad_mlp, gain_grad_mlp, shift_grad_mlp = pull_mlp(mlp_local)
    cot_rows = out_grad.astype(jnp.float32)
    input_grad = (cot_rows + rows_grad_attn + rows_grad_mlp).astype(jnp.bfloat16)
    bias_total = jnp.sum(cot_rows, axis=0)
    small_sums = (
        lax.psum_scatter(gain_grad_attn, ("dp", "tensor"), scatter_dimension=0, tiled=True),
        lax.psum_scatter(shift_grad_attn, ("dp", "tensor"), scatter_dimension=0, tiled=True),
        lax.psum_scatter(gain_grad_mlp, ("dp", "tensor"), scatter_dimension=0, tiled=True),
        lax.psum_scatter(shift_grad_mlp, ("dp", "tensor"), scatter_dimension=0, tiled=True),
        lax.psum_scatter(bias_total, ("dp", "tensor"), scatter_dimension=0, tiled=True),
    )
    return (
        layer_out,
        input_grad,
        small_sums[0],
        small_sums[1],
        small_sums[2],
        small_sums[3],
        reduced[0],
        reduced[1],
        reduced[2],
        small_sums[4],
        reduced[3],
        reduced[4],
        reduced[5],
        small_sums[4],
    )


F32 = jnp.float32
BF16 = jnp.bfloat16
MESH_ID = pl.DeviceIdType.MESH
LINE = 4
SEQ = 256
WIDTH = 1024
HID = 512
PAIR = 128


def nn(a, b):
    return jnp.dot(a, b, preferred_element_type=F32)


def nt(a, b):
    return lax.dot_general(a, b, (((1,), (1,)), ((), ())), preferred_element_type=F32)


def tn(a, b):
    return lax.dot_general(a, b, (((0,), (0,)), ((), ())), preferred_element_type=F32)


def turn_tables():
    position = np.arange(SEQ, dtype=np.float64)[:, None]
    lane = np.arange(PAIR) % HD
    rates = 10000.0 ** (-(lane % (ROT // 2)) * (2.0 / ROT))
    angles = position * rates[None, :]
    cosine = np.where(lane < ROT, np.cos(angles), 1.0)
    toward = np.where(lane < ROT // 2, -np.sin(angles), 0.0)
    away = np.where((lane >= ROT // 2) & (lane < ROT), np.sin(angles), 0.0)
    return np.stack([cosine, toward, away]).astype(np.float32)


SEATS = (0, 3, 1, 2)


def seat_of(z):
    return (2 * z - z // 2) % LINE


def rows_of(index, count):
    return pl.ds(pl.multiple_of(index * count, count), count)


class Place:
    def __init__(self):
        index = lax.axis_index("dp")
        self.t = lax.axis_index("tensor")
        self.z = index // 4
        self.k = index % 4
        self.y = self.k // 2
        self.c = self.k % 2
        self.kc = self.y * 2 + 1 - self.c
        self.ky = (1 - self.y) * 2 + self.c
        self.kyc = (1 - self.y) * 2 + 1 - self.c
        self.q = self.k * 2 + self.t
        self.core = self.at(self.z, self.kc, self.t)
        self.cross = (
            self.at(self.z, self.k, 1 - self.t),
            self.at(self.z, self.ky, self.t),
            self.at(self.z, self.ky, 1 - self.t),
        )

    def at(self, z, k, t):
        return (z * 4 + k, t)

    def line(self, z):
        return self.at(z, self.k, self.t)


class Wires:
    def __init__(self, sends, arrivals):
        self.sends, self.arrivals = sends, arrivals
        self.sent, self.landed = 0, 0

    def take(self, sends, arrivals):
        first = (self.sent, self.landed)
        self.sent += sends
        self.landed += arrivals
        return first

    def copy(self, send, arrival, src, dst, device):
        return pltpu.make_async_remote_copy(
            src_ref=src,
            dst_ref=dst,
            send_sem=self.sends.at[send],
            recv_sem=self.arrivals.at[arrival],
            device_id=device,
            device_id_type=MESH_ID,
        )

    def all_sent(self, send, view, device):
        self.copy(send, 0, view, view, device).wait_send()

    def all_landed(self, arrival, view, device):
        self.copy(0, arrival, view, view, device).wait_recv()


class PlaneGather:
    def __init__(self, me, wires, src, slot, split, blocks):
        self.me, self.wires, self.src, self.slot = me, wires, src, slot
        self.blocks = blocks
        self.pieces = (pl.ds(0, split), pl.ds(split, src.shape[0] - split))
        self.send, self.arrivals = wires.take(1, 4)
        self.near_blocks = (
            me.k * 2 + 1 - me.t,
            me.ky * 2 + me.t,
            me.ky * 2 + 1 - me.t,
        )

    def start(self, which):
        device = (self.me.cross[0], self.me.cross[1], self.me.core)[which]
        arrival = self.arrivals + (0, 1, 3)[which]
        self.wires.copy(self.send, arrival, self.src, self.slot(self.me.q), device).start()

    def pass_on(self, which):
        part = self.slot(self.near_blocks[which])
        self.wires.copy(self.send, self.arrivals + 3, part, part, self.me.core).start()

    def forward(self, which):
        block = self.slot(self.near_blocks[which])
        self.wires.all_landed(self.arrivals + which, block, self.me.core)
        part = block.at[self.pieces[which]]
        device = self.me.cross[1 - which]
        self.wires.copy(self.send, self.arrivals + 2, part, part, device).start()
        self.pass_on(which)

    def corner(self):
        block = self.slot(self.near_blocks[2])
        self.wires.all_landed(self.arrivals + 2, block, self.me.core)
        self.pass_on(2)

    def finish(self):
        self.wires.all_landed(self.arrivals + 3, self.blocks(4), self.me.core)

    def drain(self):
        self.wires.all_sent(self.send, self.blocks(7), self.me.core)


class LineGather:
    def __init__(self, me, wires, view):
        self.me, self.wires, self.view = me, wires, view
        self.sends, self.arrivals = wires.take(2, 6)

    def copy(self, way, hop, block):
        z = self.me.z
        view = self.view(block, 1)
        device = self.me.line(z + 1 if way == 0 else z - 1)
        return self.wires.copy(self.sends + way, self.arrivals + way * 3 + hop, view, view, device)

    def send(self, way, hop):
        z = self.me.z
        has = (z >= hop) & (z < LINE - 1) if way == 0 else (z + hop < LINE) & (z > 0)

        @pl.when(has)
        def _():
            self.copy(way, hop, z - hop if way == 0 else z + hop).start()

    def arrive(self, way, hop):
        z = self.me.z

        @pl.when(z > hop if way == 0 else z + 1 + hop < LINE)
        def _():
            self.copy(way, hop, z - 1 - hop if way == 0 else z + 1 + hop).wait_recv()

    def start(self, way):
        @pl.when(self.me.z != (0 if way == 0 else LINE - 1))
        def _():
            self.send(way, 0)

    def outer(self):
        for way in range(2):

            @pl.when(self.me.z == (0 if way == 0 else LINE - 1))
            def _(way=way):
                self.send(way, 0)

    def relay(self, way, hop):
        self.arrive(way, hop - 1)
        self.send(way, hop)

    def finish(self, way):
        self.arrive(way, LINE - 2)

    def drain(self):
        z = self.me.z
        for way in range(2):
            for count in range(1, LINE):

                @pl.when(z == (count - 1 if way == 0 else LINE - count))
                def _():
                    self.wires.all_sent(self.sends + way, self.view(0, count), self.me.core)


class LineReduce:
    def __init__(self, me, wires, held, landed):
        self.me, self.wires, self.held, self.landed = me, wires, held, landed
        self.sends, self.arrivals = wires.take(2, 6)

    def copy(self, way, block):
        z = self.me.z
        device = self.me.line(z - 1 if way == 0 else z + 1)
        return self.wires.copy(
            self.sends + way,
            self.arrivals + way * (LINE - 2) + block,
            self.held.at[block],
            self.landed.at[way, block],
            device,
        )

    def join(self, way, block):
        self.copy(way, block).wait_recv()
        total = self.held[block].astype(F32) + self.landed[way, block].astype(F32)
        self.held[block] = total.astype(BF16)

    def each(self, way, slot, act):
        z = self.me.z
        steps = slot - (LINE - 1 - z if way == 0 else z)
        left = z if way == 0 else LINE - 1 - z
        block = steps if way == 0 else LINE - 1 - steps

        @pl.when((steps >= 0) & (steps < left))
        def _():
            act(block)

    def slot(self, way, slot):
        def act(block):
            if slot > 0:
                started = self.me.z < LINE - 1 if way == 0 else self.me.z > 0

                @pl.when(started)
                def _():
                    self.join(way, block)

            self.copy(way, block).start()

        self.each(way, slot, act)

    def finish(self, way):
        z = self.me.z

        @pl.when(z < LINE - 1 if way == 0 else z > 0)
        def _():
            self.join(way, z)

    def drain(self):
        z = self.me.z
        for way in range(2):
            for count in range(1, LINE):

                @pl.when(z == (count if way == 0 else LINE - 1 - count))
                def _():
                    view = self.held.at[pl.ds(0, count)]
                    self.wires.all_sent(self.sends + way, view, self.me.core)


class PlaneReduce:
    def __init__(self, me, wires, part, paired, crossed):
        self.me, self.wires = me, wires
        self.part, self.paired, self.crossed = part, paired, crossed
        self.send, self.arrivals = wires.take(1, 4)
        self.blocks = (me.ky * 2 + 1 - me.t, me.k * 2 + 1 - me.t, me.ky * 2 + me.t)

    def pair(self, y):
        rows = rows_of(y * 2 + 1 - self.me.c, SEQ)
        return self.wires.copy(
            self.send, self.arrivals, self.part.at[rows], self.paired.at[y], self.me.core
        )

    def rows(self, which, half):
        first = pl.multiple_of(self.blocks[which] * 128 + half * 64, 64)
        return pl.ds(first, 64)

    def cross(self, which, half):
        way = (half, 0, 1)[which]
        return self.wires.copy(
            self.send,
            self.arrivals + (1 + half if which == 0 else 3),
            self.part.at[self.rows(which, half)],
            self.crossed.at[which, pl.ds(half * 64, 64)],
            self.me.cross[way],
        )

    def middle(self):
        self.wires.all_landed(self.arrivals, self.part.at[pl.ds(0, 2 * SEQ)], self.me.core)
        for y in range(2):
            rows = rows_of(y * 2 + self.me.c, SEQ)
            total = self.part[rows].astype(F32) + self.paired[y].astype(F32)
            self.part[rows] = total.astype(BF16)
        for which, half in ((0, 0), (0, 1), (1, 0), (2, 1)):
            self.cross(which, half).start()

    def turn(self, half):
        self.cross(0, half).wait_recv()
        rows = self.rows(2 - half, half)
        total = self.part[rows].astype(F32) + self.crossed[0, pl.ds(half * 64, 64)].astype(F32)
        self.part[rows] = total.astype(BF16)
        self.cross(2 - half, half).start()

    def finish(self):
        self.wires.all_landed(self.arrivals + 3, self.part.at[pl.ds(0, SEQ)], self.me.core)
        total = self.part[rows_of(self.me.q, 128)].astype(F32)
        return total + self.crossed[1].astype(F32) + self.crossed[2].astype(F32)

    def drain(self):
        self.wires.all_sent(self.send, self.part.at[pl.ds(0, 896)], self.me.core)


def layer_kernel(
    x_hbm,
    g_hbm,
    qkv_hbm,
    dense_hbm,
    up_hbm,
    down_hbm,
    turn_hbm,
    attn_gain_ref,
    attn_shift_ref,
    mlp_gain_ref,
    mlp_shift_ref,
    dense_bias_ref,
    down_bias_ref,
    starts_ref,
    lengths_ref,
    qkv_bias_ref,
    up_bias_ref,
    layer_out_ref,
    input_grad_ref,
    qkv_grad_ref,
    dense_grad_ref,
    up_grad_ref,
    down_grad_ref,
    small_out_ref,
    turn_ref,
    x_all,
    g_all,
    small_line,
    small_all,
    qkv_w,
    dense_w,
    up_w,
    down_w,
    vec_ref,
    bias_ref,
    normed_a,
    normed_m,
    context_ref,
    turned_grad,
    active_ref,
    hidden_grad,
    slope_ref,
    part_out,
    part_attn,
    part_mlp,
    paired_ref,
    crossed_ref,
    up_held,
    up_landed,
    down_held,
    down_landed,
    qkv_held,
    qkv_landed,
    up_final,
    qkv_final,
    dense_line,
    dense_held,
    dense_mine,
    dense_landed,
    qkv_bias_held,
    qkv_bias_line,
    qkv_bias_final,
    up_bias_held,
    up_bias_final,
    sums_held,
    sums_chip,
    sums_total,
    sums_core,
    sums_cross,
    sums_line,
    sends,
    arrivals,
    local_sems,
):
    me = Place()
    wires = Wires(sends, arrivals)
    z, k, t = me.z, me.k, me.t

    barrier = pltpu.get_barrier_semaphore()

    def greet(device):
        pl.semaphore_signal(barrier, inc=1, device_id=device, device_id_type=MESH_ID)

    greet(me.core)
    greet(me.at(z, me.kyc, t))
    for device in me.cross:
        greet(device)
    for step in range(1, LINE):
        greet(me.line((z + step) % LINE))
    local_copies = []

    def local(src, dst):
        copy = pltpu.make_async_copy(src, dst, local_sems.at[len(local_copies)])
        local_copies.append(copy)
        copy.start()

    seat = pl.ds(pl.multiple_of(z * 256 + k * 64, 64), 64)
    peers = (me.kc, me.ky, me.kyc)
    devices = tuple(me.at(z, peer, t) for peer in peers)

    def three(arrival, view):
        wires.all_landed(arrival, view, me.core)

    local(dense_hbm, dense_line.at[z])
    for place, other in enumerate(SEATS):
        local(
            up_hbm.at[:, rows_of(other * 4 + k, 128)],
            up_w.at[seat, pl.ds(place * 128, 128)],
        )
    local(down_hbm, down_w.at[rows_of(seat_of(z), 128)])
    for which in range(3):
        local(
            qkv_hbm.at[which, :, rows_of(k, PAIR)],
            qkv_w.at[seat, pl.ds(which * PAIR, PAIR)],
        )
    local(x_hbm, x_all.at[rows_of(me.q, 128)])
    local(g_hbm, g_all.at[rows_of(me.q, 128)])
    local(turn_hbm, turn_ref)
    qkv_bias_held[...] = jnp.zeros_like(qkv_bias_held)
    up_bias_held[...] = jnp.zeros_like(up_bias_held)

    def side_by_side(*fields):
        return jnp.concatenate(
            [field.astype(F32).reshape(1, field.shape[-1]) for field in fields], axis=1
        )

    triple = qkv_bias_ref[...]
    blank = jnp.zeros((1, 60), F32)
    small_line[z] = jnp.concatenate(
        [
            side_by_side(
                attn_gain_ref[...], attn_shift_ref[...], mlp_gain_ref[...], mlp_shift_ref[...]
            ),
            side_by_side(
                dense_bias_ref[...], down_bias_ref[...], starts_ref[...], lengths_ref[...], blank
            ),
            side_by_side(triple[0:1], triple[1:2], triple[2:3], blank[:, :32]),
            side_by_side(up_bias_ref[...]),
            jnp.zeros((4, 128), F32),
        ],
        axis=0,
    )
    pl.semaphore_wait(barrier, 8)

    up_send, up_arrival = wires.take(1, 2)
    for place, other in enumerate(SEATS):
        for which in range(3):
            wires.copy(
                up_send,
                up_arrival + place // 2,
                up_hbm.at[:, rows_of(other * 4 + peers[which], 128)],
                up_w.at[seat, pl.ds(place * 128, 128)],
                devices[which],
            ).start()

    qkv_sends, qkv_arrival = wires.take(1, 1)

    def rows_slot(ref):
        return (lambda block: ref.at[rows_of(block, 128)]), (
            lambda count: ref.at[pl.ds(0, count * 128)]
        )

    slot, blocks = rows_slot(x_all)
    gather_x = PlaneGather(me, wires, x_hbm, slot, 48, blocks)
    for which in range(3):
        gather_x.start(which)
    slot, blocks = rows_slot(g_all)
    gather_g = PlaneGather(me, wires, g_hbm, slot, 48, blocks)
    gather_small = PlaneGather(
        me,
        wires,
        small_line,
        lambda block: small_all.at[block],
        2,
        lambda count: small_all.at[pl.ds(0, count)],
    )
    small_send, small_arrival = wires.take(1, 1)
    for step in range(1, LINE):
        wires.copy(
            small_send,
            small_arrival,
            small_line.at[z],
            small_line.at[z],
            me.line((z + step) % LINE),
        ).start()

    def line_gather(ref, count):
        return LineGather(
            me, wires, lambda s, n: ref.at[pl.ds(pl.multiple_of(s * count, count), n * count)]
        )

    line_dense = LineGather(me, wires, lambda s, n: dense_line.at[pl.ds(s, n)])
    line_qkv = line_gather(qkv_w, 256)
    line_upa, line_upb = (
        LineGather(
            me,
            wires,
            lambda s, n, first=first: up_w.at[
                pl.ds(pl.multiple_of(s * 256, 256), n * 256), pl.ds(first, 256)
            ],
        )
        for first in (0, 256)
    )
    line_down = LineGather(
        me,
        wires,
        lambda s, n: down_w.at[pl.ds(pl.multiple_of(seat_of(s) * 128, 128), n * 128)],
    )
    reduce_down = LineReduce(
        me, wires, down_held, down_landed
    )
    reduce_up = LineReduce(
        me, wires, up_held, up_landed
    )
    reduce_qkv = LineReduce(
        me, wires, qkv_held, qkv_landed
    )
    reduce_dense = LineReduce(
        me, wires, dense_mine, dense_landed
    )
    reduce_attn = PlaneReduce(me, wires, part_attn, paired_ref.at[0], crossed_ref.at[0])
    reduce_out = PlaneReduce(me, wires, part_out, paired_ref.at[1], crossed_ref.at[1])
    reduce_mlp = PlaneReduce(me, wires, part_mlp, paired_ref.at[2], crossed_ref.at[2])

    local_copies[0].wait()
    line_dense.outer()
    line_dense.start(0)
    line_dense.start(1)

    own_small = pltpu.make_async_copy(
        small_line, small_all.at[me.q], local_sems.at[len(local_copies)]
    )
    own_dense = pltpu.make_async_copy(
        dense_line.at[k], dense_w.at[rows_of(k, 32)], local_sems.at[len(local_copies) + 1]
    )
    dense_sends, dense_arrival = wires.take(1, 1)
    back_sends, back_arrival = wires.take(2, 2)
    bias_sends, bias_arrival = wires.take(2, 2)
    out_sends, out_arrival = wires.take(2, 2)
    sums_sends, sums_arrival = wires.take(3, 3)

    def along(send, arrival, source, target):
        for step in range(1, LINE):
            there = (z + step) % LINE
            wires.copy(send, arrival, source(there), target, me.line(there)).start()

    def around(send, arrival, source, target):
        for which in range(3):
            wires.copy(send, arrival, source(peers[which]), target, devices[which]).start()

    def norm_rows(rows):
        values = x_all[rows].astype(F32)
        centred = values - jnp.mean(values, axis=-1, keepdims=True)
        rate = lax.rsqrt(jnp.mean(centred * centred, axis=-1, keepdims=True) + NORM_EPS)
        return centred * rate, rate

    def norm_block(block, carry):
        rows = rows_of(block, 128)
        unit, _ = norm_rows(rows)
        normed_a[rows] = (unit * vec_ref[0:1, :] + vec_ref[1:2, :]).astype(BF16)
        normed_m[rows] = (unit * vec_ref[2:3, :] + vec_ref[3:4, :]).astype(BF16)
        return carry

    def activate(half):
        columns = slice(half * 256, (half + 1) * 256)

        def tile_of(tile, carry):
            rows = rows_of(tile, 256)
            up_bias = jnp.concatenate(
                [small_all[me.q, s, 3:4, :] for s in SEATS[half * 2 : half * 2 + 2]], axis=1
            )
            hidden = nn(normed_m[rows], up_w[:, columns]) + up_bias
            share = (1.0 + lax.erf(hidden * 0.5**0.5)) * 0.5
            bell = jnp.exp(hidden * hidden * -0.5) * (2.0 * np.pi) ** -0.5
            slope_ref[rows, columns] = share + hidden * bell
            active_ref[rows, columns] = (hidden * share).astype(BF16)
            return carry

        return tile_of

    activate_a, activate_b = activate(0), activate(1)

    def down_block(block, carry):
        units = rows_of(seat_of(block), 128)
        down_held[block] = tn(active_ref[:, units], g_all[...]).astype(BF16)
        return carry

    def feed_back(tile, carry):
        rows = rows_of(tile, 256)
        grad = (nt(g_all[rows], down_w[...]) * slope_ref[rows]).astype(BF16)
        hidden_grad[rows] = grad
        up_bias_held[0:1, :] += jnp.sum(grad.astype(F32), axis=0, keepdims=True)
        return carry

    def feed_in(tile, carry):
        rows = rows_of(tile, 256)
        part_mlp[rows] = nt(hidden_grad[rows], up_w[...]).astype(BF16)
        return carry

    def up_block(block, carry):
        up_held[block] = tn(normed_m[:, rows_of(block, 256)], hidden_grad[...]).astype(BF16)
        return carry

    scale = HD**-0.5

    def attend(seq, carry):
        rows = rows_of(seq, SEQ)
        cosine, toward, away = turn_ref[0], turn_ref[1], turn_ref[2]
        projected = nn(normed_a[rows], qkv_w[...]) + bias_ref[0:1, :]

        def project(which):
            return projected[:, which * PAIR : (which + 1) * PAIR]

        def turned(field):
            return (
                field * cosine
                + pltpu.roll(field, ROT // 2, 1) * away
                + pltpu.roll(field, PAIR - ROT // 2, 1) * toward
            )

        def turned_back(field):
            return (
                field * cosine
                - pltpu.roll(field, ROT // 2, 1) * away
                - pltpu.roll(field, PAIR - ROT // 2, 1) * toward
            )

        query = turned(project(0)).astype(BF16)
        key = turned(project(1)).astype(BF16)
        value = project(2).astype(BF16)
        context_grad = nt(g_all[rows], dense_w[...]).astype(BF16)

        spans = small_all[seq * 2, z, 1:2, :]
        down_pos = lax.broadcasted_iota(jnp.int32, (SEQ, 1), 0).astype(F32)
        over_pos = lax.broadcasted_iota(jnp.int32, (1, SEQ), 1).astype(F32)

        def labels(place):
            total = jnp.zeros(place.shape, F32)
            for span in range(2):
                begin = spans[:, 64 + span : 65 + span]
                end = begin + spans[:, 66 + span : 67 + span]
                total = total + jnp.where((place >= begin) & (place < end), span + 1.0, 0.0)
            return total

        down_label, over_label = labels(down_pos), labels(over_pos)
        allowed = (over_pos <= down_pos) | ((down_label == over_label) & (down_label > 0.0))

        lane = lax.broadcasted_iota(jnp.int32, (SEQ, PAIR), 1)
        parts = []
        for head in range(2):
            mine = (lane >= HD) if head else (lane < HD)
            zero = jnp.zeros_like(query)
            scores = nt(jnp.where(mine, query, zero), key) * scale
            scores = jnp.where(allowed, scores, NEG_FILL)
            exponent = jnp.exp(scores - jnp.max(scores, axis=-1, keepdims=True))
            probs = exponent * (1.0 / jnp.sum(exponent, axis=-1, keepdims=True))
            low = probs.astype(BF16)
            prob_grad = nt(jnp.where(mine, context_grad, zero), value)
            inner = jnp.sum(prob_grad * probs, axis=-1, keepdims=True)
            score_grad = (probs * (prob_grad - inner)).astype(BF16)
            parts.append(
                (
                    nn(low, value),
                    tn(low, context_grad),
                    nn(score_grad, key) * scale,
                    tn(score_grad, query) * scale,
                )
            )
        context, value_grad, query_grad, key_grad = (
            jnp.where(lane < HD, first, second) for first, second in zip(*parts)
        )
        context_ref[rows] = context.astype(BF16)
        grads = (
            turned_back(query_grad).astype(BF16),
            turned_back(key_grad).astype(BF16),
            value_grad.astype(BF16),
        )
        for which in range(3):
            turned_grad[rows, which * PAIR : (which + 1) * PAIR] = grads[which]
            qkv_bias_held[which : which + 1, :] += jnp.sum(
                grads[which].astype(F32), axis=0, keepdims=True
            )
        part_attn[rows] = nt(turned_grad[rows], qkv_w[...]).astype(BF16)
        return carry

    def qkv_block(block, carry):
        qkv_held[block] = tn(normed_a[:, rows_of(block, 256)], turned_grad[...]).astype(BF16)
        return carry

    def mix(tile, carry):
        rows = rows_of(tile, 256)
        mixed = nn(context_ref[rows], dense_w[...]) + nn(active_ref[rows], down_w[...])
        part_out[rows] = mixed.astype(BF16)
        return carry

    def locals_done():
        for copy in local_copies[1:]:
            copy.wait()

    def small_line_done():
        three(small_arrival, small_line.at[pl.ds(0, 3)])
        own_small.start()
        for which in range(3):
            gather_small.start(which)

    def upa_start():
        three(up_arrival, up_w.at[pl.ds(0, 96)])
        line_upa.outer()
        line_upa.start(0)
        line_upa.start(1)

    def upb_start():
        three(up_arrival + 1, up_w.at[pl.ds(0, 96)])
        line_upb.outer()
        line_upb.start(0)
        line_upb.start(1)

    def down_outer():
        line_down.outer()

    def qkv_send():
        for which in range(3):
            for part in range(3):
                wires.copy(
                    qkv_sends,
                    qkv_arrival,
                    qkv_hbm.at[part, :, rows_of(peers[which], PAIR)],
                    qkv_w.at[seat, pl.ds(part * PAIR, PAIR)],
                    devices[which],
                ).start()

    def qkv_outer():
        three(qkv_arrival, qkv_w.at[pl.ds(0, 192)])
        line_qkv.outer()

    def qkv_start():
        line_qkv.start(0)
        line_qkv.start(1)

    def down_start():
        line_down.start(0)
        line_down.start(1)

    def dense_send():
        around(
            dense_sends, dense_arrival, lambda to: dense_line.at[to], dense_w.at[rows_of(k, 32)]
        )
        own_dense.start()

    def dense_done():
        three(dense_arrival, dense_w.at[pl.ds(0, 96)])
        own_dense.wait()

    def vectors():
        own_small.wait()
        table = small_all[...].reshape(256, 128).astype(BF16)
        line_id = lax.broadcasted_iota(jnp.int32, (256, WIDTH), 0)
        column = lax.broadcasted_iota(jnp.int32, (256, WIDTH), 1)
        owner = ((line_id >> 3) & 3) * 8 + (line_id >> 5)
        lane_row = lax.broadcasted_iota(jnp.int32, (128, WIDTH), 0)
        lane_col = lax.broadcasted_iota(jnp.int32, (128, WIDTH), 1) & 31
        for kind, count, base in ((0, 4, 0), (1, 2, 4)):
            chosen = (owner == (column >> 5)) & ((line_id & 7) == kind)
            spread = tn(table, jnp.where(chosen, 1.0, 0.0).astype(BF16))
            for which in range(count):
                picked = jnp.where(lane_row == lane_col + which * 32, spread, 0.0)
                vec_ref[base + which : base + which + 1, :] = jnp.sum(picked, axis=0, keepdims=True)
        line_id = line_id[:, :PAIR]
        column = column[:, :PAIR]
        chosen = (
            (((line_id >> 3) & 3) == k)
            & ((line_id >> 5) == (column >> 5) * 2 + t)
            & ((line_id & 7) == 2)
        )
        spread = tn(table, jnp.where(chosen, 1.0, 0.0).astype(BF16))
        for which in range(3):
            picked = jnp.where(lane_row[:, :PAIR] == lane_col[:, :PAIR] + which * 32, spread, 0.0)
            total = jnp.sum(picked, axis=0, keepdims=True)
            bias_ref[0:1, which * PAIR : (which + 1) * PAIR] = total

    def up_bias_send():
        along(
            bias_sends,
            bias_arrival,
            lambda there: up_bias_held.at[:, rows_of(seat_of(there), 128)],
            up_bias_final.at[z],
        )
        up_bias_final[z] = up_bias_held[:, rows_of(seat_of(z), 128)]

    def dense_part():
        dense_held[...] = tn(context_ref[...], g_all[...]).astype(BF16)
        around(
            back_sends, back_arrival, lambda to: dense_held.at[rows_of(to, 32)], dense_mine.at[k]
        )
        around(back_sends + 1, back_arrival + 1, lambda to: qkv_bias_held, qkv_bias_line.at[k])
        dense_mine[k] = dense_held[rows_of(k, 32)]
        qkv_bias_line[k] = qkv_bias_held[...]

    def dense_back():
        three(back_arrival, dense_mine.at[pl.ds(0, 3)])
        three(back_arrival + 1, qkv_bias_line.at[pl.ds(0, 3)])
        along(
            bias_sends + 1,
            bias_arrival + 1,
            lambda there: qkv_bias_line.at[there],
            qkv_bias_final.at[z],
        )
        qkv_bias_final[z] = qkv_bias_line[z]

    def up_out():
        around(
            out_sends, out_arrival, lambda to: up_held.at[z, rows_of(to, 64)], up_final.at[k]
        )
        up_final[k] = up_held[z, rows_of(k, 64)]

    def qkv_out():
        around(
            out_sends + 1,
            out_arrival + 1,
            lambda to: qkv_held.at[z, rows_of(to, 64)],
            qkv_final.at[k],
        )
        qkv_final[k] = qkv_held[z, rows_of(k, 64)]

    def down_out():
        down_grad_ref[...] = down_held[z]

    def dense_out():
        dense_grad_ref[...] = dense_mine[z]

    def up_result():
        three(out_arrival, up_final.at[pl.ds(0, 3)])
        up_grad_ref[...] = up_final[...]

    def qkv_result():
        three(out_arrival + 1, qkv_final.at[pl.ds(0, 3)])
        qkv_grad_ref[...] = qkv_final[...]

    own = rows_of(me.q, 128)
    def layer_out():
        mixed = reduce_out.finish()
        layer_out_ref[...] = (
            x_all[own].astype(F32) + mixed + vec_ref[4:5, :] + vec_ref[5:6, :]
        ).astype(BF16)

    def norm_grads():
        from_attn = reduce_attn.finish()
        from_mlp = reduce_mlp.finish()
        cotangent = g_all[own].astype(F32)
        unit, rate = norm_rows(own)
        sums_held[...] = jnp.zeros_like(sums_held)
        for which, field in enumerate(
            (from_attn * unit, from_attn, from_mlp * unit, from_mlp, cotangent)
        ):
            sums_held[which : which + 1, :] = jnp.sum(field, axis=0, keepdims=True)
        wires.copy(sums_sends, sums_arrival, sums_held, sums_core, me.core).start()
        pulled = from_attn * vec_ref[0:1, :] + from_mlp * vec_ref[2:3, :]
        pulled = (
            pulled
            - jnp.mean(pulled, axis=-1, keepdims=True)
            - unit * jnp.mean(pulled * unit, axis=-1, keepdims=True)
        )
        input_grad_ref[...] = (cotangent + rate * pulled).astype(BF16)

    def sums_plane():
        three(sums_arrival, sums_core)
        sums_chip[...] = sums_held[...] + sums_core[...]
        for which in range(3):
            wires.copy(
                sums_sends + 1,
                sums_arrival + 1,
                sums_chip,
                sums_cross.at[which],
                me.cross[which],
            ).start()

    def sums_send():
        three(sums_arrival + 1, sums_cross)
        sums_total[...] = sums_chip[...] + sums_cross[0] + sums_cross[1] + sums_cross[2]
        along(
            sums_sends + 2,
            sums_arrival + 2,
            lambda there: sums_total.at[:, rows_of(there, 256)],
            sums_line.at[z],
        )
        sums_line[z] = sums_total[:, rows_of(z, 256)]

    def small_result():
        three(sums_arrival + 2, sums_line.at[pl.ds(0, 3)])
        three(bias_arrival, up_bias_final.at[pl.ds(0, 3)])
        three(bias_arrival + 1, qkv_bias_final.at[pl.ds(0, 3)])
        sums = sums_line[0] + sums_line[1] + sums_line[2] + sums_line[3]
        sums = jnp.where(k >= 2, sums[:, 128:], sums[:, :128])
        small_out_ref[0:8, :] = pltpu.roll(sums, (128 - (me.q % 4) * 32) % 128, 1)
        bias_sum = qkv_bias_final[0] + qkv_bias_final[1] + qkv_bias_final[2] + qkv_bias_final[3]
        small_out_ref[8:16, :] = pltpu.roll(bias_sum, (128 - k * 32) % 128, 1)
        small_out_ref[16:24, :] = (
            up_bias_final[0] + up_bias_final[1] + up_bias_final[2] + up_bias_final[3]
        )

    def ends_of(body):
        def outer(index, carry):
            return body(index * (LINE - 1), carry)

        return outer

    small_line_done()
    locals_done()
    gather_g.start(0)
    upa_start()
    gather_g.start(1)
    line_dense.relay(1, 1)
    line_upa.relay(1, 1)
    gather_small.forward(0)
    gather_g.start(2)
    gather_x.forward(0)
    upb_start()
    line_dense.relay(1, 2)
    line_dense.relay(0, 1)
    line_dense.finish(1)
    down_outer()
    line_upb.relay(1, 1)
    line_upa.relay(0, 1)
    qkv_send()
    gather_small.forward(1)
    line_upb.relay(0, 1)
    line_dense.relay(0, 2)
    gather_x.forward(1)
    line_upa.relay(1, 2)
    gather_g.forward(0)
    gather_small.corner()
    line_dense.finish(0)
    gather_x.corner()
    gather_small.finish()
    line_upa.relay(0, 2)
    dense_send()
    line_upb.relay(1, 2)
    gather_g.forward(1)
    vectors()
    gather_x.finish()
    qkv_outer()
    lax.fori_loop(0, 4, norm_block, 0)
    lax.fori_loop(4, 8, norm_block, 0)
    gather_g.corner()
    line_upb.relay(0, 2)
    line_upa.finish(0)
    line_upb.finish(1)
    qkv_start()
    gather_g.finish()
    dense_done()
    line_upa.finish(1)
    lax.fori_loop(0, 4, activate_a, 0)
    lax.fori_loop(0, 2, ends_of(down_block), 0)
    line_upb.finish(0)
    reduce_down.slot(0, 0)
    reduce_down.slot(1, 0)
    lax.fori_loop(0, 4, activate_b, 0)
    line_qkv.relay(1, 1)
    lax.fori_loop(1, 3, down_block, 0)
    line_qkv.relay(0, 1)
    reduce_down.slot(0, 1)
    reduce_down.slot(1, 1)
    line_qkv.relay(1, 2)
    line_qkv.relay(0, 2)
    line_qkv.finish(1)
    down_start()
    line_qkv.finish(0)
    reduce_down.slot(1, 2)
    reduce_down.slot(0, 2)
    lax.fori_loop(3, 4, attend, 0)
    lax.fori_loop(0, 1, attend, 0)
    lax.fori_loop(1, 2, attend, 0)
    line_down.relay(0, 1)
    lax.fori_loop(2, 3, attend, 0)
    line_down.relay(1, 1)
    reduce_attn.pair(0).start()
    reduce_attn.pair(1).start()
    dense_part()
    lax.fori_loop(0, 2, ends_of(qkv_block), 0)
    lax.fori_loop(1, 3, qkv_block, 0)
    reduce_down.finish(0)
    reduce_qkv.slot(0, 0)
    reduce_qkv.slot(1, 0)
    reduce_attn.middle()
    reduce_qkv.slot(1, 1)
    reduce_down.finish(1)
    line_down.relay(1, 2)
    reduce_qkv.slot(0, 1)
    line_down.relay(0, 2)
    reduce_attn.turn(0)
    reduce_attn.turn(1)
    reduce_qkv.slot(0, 2)
    reduce_qkv.slot(1, 2)
    line_down.finish(0)
    dense_back()
    reduce_dense.slot(0, 0)
    reduce_dense.slot(1, 0)
    line_down.finish(1)
    lax.fori_loop(2, 4, feed_back, 0)
    lax.fori_loop(0, 2, feed_back, 0)
    lax.fori_loop(0, 2, ends_of(up_block), 0)
    reduce_dense.slot(1, 1)
    lax.fori_loop(0, 2, feed_in, 0)
    reduce_dense.slot(0, 1)
    reduce_mlp.pair(0).start()
    lax.fori_loop(2, 4, feed_in, 0)
    reduce_up.slot(0, 0)
    reduce_up.slot(1, 0)
    lax.fori_loop(0, 2, mix, 0)
    reduce_qkv.finish(1)
    reduce_mlp.pair(1).start()
    reduce_qkv.finish(0)
    qkv_out()
    reduce_dense.slot(0, 2)
    reduce_mlp.middle()
    qkv_result()
    reduce_dense.slot(1, 2)
    lax.fori_loop(1, 3, up_block, 0)
    lax.fori_loop(2, 4, mix, 0)
    reduce_up.slot(0, 1)
    reduce_mlp.turn(1)
    reduce_up.slot(1, 1)
    reduce_dense.finish(1)
    reduce_out.pair(1).start()
    reduce_mlp.turn(0)
    reduce_dense.finish(0)
    reduce_out.pair(0).start()
    reduce_out.middle()
    reduce_up.slot(1, 2)
    up_bias_send()
    reduce_out.turn(0)
    dense_out()
    reduce_up.slot(0, 2)
    reduce_out.turn(1)
    norm_grads()
    down_out()
    sums_plane()
    reduce_up.finish(1)
    reduce_up.finish(0)
    up_out()
    layer_out()
    sums_send()
    small_result()
    up_result()

    for send, view in (
        (up_send, up_w.at[pl.ds(0, 192)]),
        (qkv_sends, qkv_w.at[pl.ds(0, 192)]),
        (small_send, small_line.at[pl.ds(0, 3)]),
        (dense_sends, dense_w.at[pl.ds(0, 96)]),
        (back_sends, dense_mine.at[pl.ds(0, 3)]),
        (back_sends + 1, qkv_bias_line.at[pl.ds(0, 3)]),
        (bias_sends, up_bias_final.at[pl.ds(0, 3)]),
        (bias_sends + 1, qkv_bias_final.at[pl.ds(0, 3)]),
        (out_sends, up_final.at[pl.ds(0, 3)]),
        (out_sends + 1, qkv_final.at[pl.ds(0, 3)]),
        (sums_sends, sums_core),
        (sums_sends + 1, sums_cross),
        (sums_sends + 2, sums_line.at[pl.ds(0, 3)]),
    ):
        wires.all_sent(send, view, me.core)
    for item in (
        gather_x,
        gather_g,
        gather_small,
        line_dense,
        line_qkv,
        line_upa,
        line_upb,
        line_down,
        reduce_attn,
        reduce_out,
        reduce_mlp,
        reduce_qkv,
        reduce_dense,
        reduce_down,
        reduce_up,
    ):
        item.drain()


def final_kernel(
    layer_out_ref,
    input_grad_ref,
    qkv_ref,
    dense_ref,
    up_ref,
    down_ref,
    small_ref,
    layer_out,
    input_grad,
    attn_gain_grad,
    attn_shift_grad,
    mlp_gain_grad,
    mlp_shift_grad,
    qkv_grad,
    qkv_bias_grad,
    dense_grad,
    dense_bias_grad,
    up_grad,
    up_bias_grad,
    down_grad,
    down_bias_grad,
):
    layer_out[...] = layer_out_ref[...]
    input_grad[...] = input_grad_ref[...]
    for row, out in enumerate((attn_gain_grad, attn_shift_grad, mlp_gain_grad, mlp_shift_grad)):
        out[...] = small_ref[row, :32]
    dense_bias_grad[...] = small_ref[4, :32]
    down_bias_grad[...] = small_ref[4, :32]
    qkv_bias_grad[...] = small_ref[8:11, :32]
    up_bias_grad[...] = small_ref[16, :]
    for origin in range(4):
        for which in range(3):
            qkv_grad[which, :, origin * PAIR : (origin + 1) * PAIR] = qkv_ref[
                origin, :, which * PAIR : (which + 1) * PAIR
            ].astype(F32)
        for place, other in enumerate(SEATS):
            first = (other * 4 + origin) * 128
            up_grad[:, first : first + 128] = up_ref[
                origin, :, place * 128 : (place + 1) * 128
            ].astype(F32)
    dense_grad[...] = dense_ref[...].astype(F32)
    down_grad[...] = down_ref[...].astype(F32)


def plane_layer(
    hidden_in,
    out_grad,
    span_start,
    span_length,
    attn_gain,
    attn_shift,
    mlp_gain,
    mlp_shift,
    qkv_weight,
    qkv_bias,
    dense_weight,
    dense_bias,
    up_weight,
    up_bias,
    down_weight,
    down_bias,
):
    vmem = pl.BlockSpec(memory_space=pltpu.VMEM)
    anywhere = pl.BlockSpec(memory_space=pl.ANY)
    tokens = 4 * SEQ
    outs = pl.pallas_call(
        layer_kernel,
        out_shape=(
            jax.ShapeDtypeStruct((128, WIDTH), BF16),
            jax.ShapeDtypeStruct((128, WIDTH), BF16),
            jax.ShapeDtypeStruct((4, 64, 3 * PAIR), BF16),
            jax.ShapeDtypeStruct((32, WIDTH), BF16),
            jax.ShapeDtypeStruct((4, 64, HID), BF16),
            jax.ShapeDtypeStruct((128, WIDTH), BF16),
            jax.ShapeDtypeStruct((24, 128), F32),
        ),
        in_specs=[anywhere] * 7 + [vmem] * 10,
        out_specs=(vmem,) * 7,
        scratch_shapes=[
            pltpu.VMEM((3, SEQ, PAIR), F32),
            pltpu.VMEM((tokens, WIDTH), BF16),
            pltpu.VMEM((tokens, WIDTH), BF16),
            pltpu.VMEM((LINE, 8, 128), F32),
            pltpu.VMEM((8, LINE, 8, 128), F32),
            pltpu.VMEM((WIDTH, 3 * PAIR), BF16),
            pltpu.VMEM((PAIR, WIDTH), BF16),
            pltpu.VMEM((WIDTH, HID), BF16),
            pltpu.VMEM((HID, WIDTH), BF16),
            pltpu.VMEM((8, WIDTH), F32),
            pltpu.VMEM((8, 3 * PAIR), F32),
            pltpu.VMEM((tokens, WIDTH), BF16),
            pltpu.VMEM((tokens, WIDTH), BF16),
            pltpu.VMEM((tokens, PAIR), BF16),
            pltpu.VMEM((tokens, 3 * PAIR), BF16),
            pltpu.VMEM((tokens, HID), BF16),
            pltpu.VMEM((tokens, HID), BF16),
            pltpu.VMEM((tokens, HID), F32),
            pltpu.VMEM((tokens, WIDTH), BF16),
            pltpu.VMEM((tokens, WIDTH), BF16),
            pltpu.VMEM((tokens, WIDTH), BF16),
            pltpu.VMEM((3, 2, SEQ, WIDTH), BF16),
            pltpu.VMEM((3, 3, 128, WIDTH), BF16),
            pltpu.VMEM((LINE, 256, HID), BF16),
            pltpu.VMEM((2, LINE, 256, HID), BF16),
            pltpu.VMEM((LINE, 128, WIDTH), BF16),
            pltpu.VMEM((2, LINE, 128, WIDTH), BF16),
            pltpu.VMEM((LINE, 256, 3 * PAIR), BF16),
            pltpu.VMEM((2, LINE, 256, 3 * PAIR), BF16),
            pltpu.VMEM((4, 64, HID), BF16),
            pltpu.VMEM((4, 64, 3 * PAIR), BF16),
            pltpu.VMEM((LINE, 32, WIDTH), BF16),
            pltpu.VMEM((PAIR, WIDTH), BF16),
            pltpu.VMEM((LINE, 32, WIDTH), BF16),
            pltpu.VMEM((2, LINE, 32, WIDTH), BF16),
            pltpu.VMEM((8, PAIR), F32),
            pltpu.VMEM((4, 8, PAIR), F32),
            pltpu.VMEM((LINE, 8, PAIR), F32),
            pltpu.VMEM((8, HID), F32),
            pltpu.VMEM((LINE, 8, 128), F32),
            pltpu.VMEM((8, WIDTH), F32),
            pltpu.VMEM((8, WIDTH), F32),
            pltpu.VMEM((8, WIDTH), F32),
            pltpu.VMEM((8, WIDTH), F32),
            pltpu.VMEM((3, 8, WIDTH), F32),
            pltpu.VMEM((LINE, 8, 256), F32),
            pltpu.SemaphoreType.DMA((37,)),
            pltpu.SemaphoreType.DMA((92,)),
            pltpu.SemaphoreType.DMA((14,)),
        ],
        compiler_params=pltpu.CompilerParams(
            collective_id=0, has_side_effects=True, vmem_limit_bytes=60 * 2**20
        ),
    )(
        hidden_in,
        out_grad,
        jnp.transpose(qkv_weight, (1, 0, 2)),
        dense_weight,
        up_weight,
        down_weight,
        jnp.asarray(turn_tables()),
        attn_gain,
        attn_shift,
        mlp_gain,
        mlp_shift,
        dense_bias,
        down_bias,
        span_start,
        span_length,
        qkv_bias,
        up_bias,
    )
    wide = jax.ShapeDtypeStruct((32,), F32)
    finals = pl.pallas_call(
        final_kernel,
        out_shape=(
            jax.ShapeDtypeStruct((128, WIDTH), BF16),
            jax.ShapeDtypeStruct((128, WIDTH), BF16),
            wide,
            wide,
            wide,
            wide,
            jax.ShapeDtypeStruct((3, 64, 512), F32),
            jax.ShapeDtypeStruct((3, 32), F32),
            jax.ShapeDtypeStruct((32, WIDTH), F32),
            wide,
            jax.ShapeDtypeStruct((64, 2048), F32),
            jax.ShapeDtypeStruct((128,), F32),
            jax.ShapeDtypeStruct((128, WIDTH), F32),
            wide,
        ),
        in_specs=[vmem] * 7,
        out_specs=(vmem,) * 14,
    )(*outs)
    return (*finals[:6], jnp.transpose(finals[6], (1, 0, 2)), *finals[7:])


def solution(mesh):
    in_specs = (
        P(("dp", "tensor"), None),
        P(("dp", "tensor"), None),
        P("dp", None),
        P("dp", None),
        P(("dp", "tensor")),
        P(("dp", "tensor")),
        P(("dp", "tensor")),
        P(("dp", "tensor")),
        P("dp", None, "tensor"),
        P(None, ("tensor", "dp")),
        P(("tensor", "dp"), None),
        P(("dp", "tensor")),
        P("dp", "tensor"),
        P(("tensor", "dp")),
        P(("tensor", "dp"), None),
        P(("dp", "tensor")),
    )
    out_specs = (
        P(("dp", "tensor"), None),
        P(("dp", "tensor"), None),
        P(("dp", "tensor")),
        P(("dp", "tensor")),
        P(("dp", "tensor")),
        P(("dp", "tensor")),
        P("dp", None, "tensor"),
        P(None, ("tensor", "dp")),
        P(("tensor", "dp"), None),
        P(("dp", "tensor")),
        P("dp", "tensor"),
        P(("tensor", "dp")),
        P(("tensor", "dp"), None),
        P(("dp", "tensor")),
    )
    fast = mesh.shape["dp"] == 16 and mesh.shape["tensor"] == 2
    return jax.shard_map(plane_layer if fast else shards, mesh=mesh, in_specs=in_specs, out_specs=out_specs, check_vma=False)
```

```python
import jax
import jax.numpy as jnp
import numpy as np
from jax import lax
from jax.experimental import pallas as pl
from jax.experimental.pallas import tpu as pltpu
from jax.sharding import PartitionSpec as P

HD = 64
ROT = 16


NORM_EPS = 1e-05
NEG_FILL = -1000000000.0


def layer_norm(rows_in, gain_vec, shift_vec):
    mean_row = jnp.mean(rows_in, axis=-1, keepdims=True)
    centred = rows_in - mean_row
    spread = jnp.mean(centred * centred, axis=-1, keepdims=True)
    return centred * lax.rsqrt(spread + NORM_EPS) * gain_vec + shift_vec


def rotary_tables(length):
    position = jnp.arange(length, dtype=jnp.float32)
    rates = 10000.0 ** (-jnp.arange(ROT // 2, dtype=jnp.float32) * (2.0 / ROT))
    angles = position[:, None] * rates[None, :]
    angles = jnp.concatenate([angles, angles], axis=-1)[:, None, :]
    return (jnp.cos(angles), jnp.sin(angles))


def rotate(field_in, cosine, sines):
    turned = field_in[..., :ROT]
    first_half = turned[..., : ROT // 2]
    second_half = turned[..., ROT // 2 :]
    swapped = jnp.concatenate([-second_half, first_half], axis=-1)
    return jnp.concatenate([turned * cosine + swapped * sines, field_in[..., ROT:]], axis=-1)


def gelu_exact(values_in):
    return jax.nn.gelu(values_in, approximate=False)


def shards(
    hidden_in,
    out_grad,
    span_start,
    span_length,
    attn_gain,
    attn_shift,
    mlp_gain,
    mlp_shift,
    qkv_weight,
    qkv_bias,
    dense_weight,
    dense_bias,
    up_weight,
    up_bias,
    down_weight,
    down_bias,
):
    local_rows = hidden_in.shape[0]
    length = local_rows * lax.axis_size("tensor")
    block_rows = min(512, length)
    block_count = length // block_rows
    score_scale = HD ** (-0.5)
    small_full = (
        lax.all_gather(attn_gain, ("dp", "tensor"), axis=0, tiled=True),
        lax.all_gather(attn_shift, ("dp", "tensor"), axis=0, tiled=True),
        lax.all_gather(mlp_gain, ("dp", "tensor"), axis=0, tiled=True),
        lax.all_gather(mlp_shift, ("dp", "tensor"), axis=0, tiled=True),
        lax.all_gather(dense_bias, ("dp", "tensor"), axis=0, tiled=True),
        lax.all_gather(down_bias, ("dp", "tensor"), axis=0, tiled=True),
    )
    small_vecs = [item.astype(jnp.float32) for item in small_full]
    own_rows = hidden_in.astype(jnp.float32)
    normed_attn = layer_norm(own_rows, small_vecs[0], small_vecs[1]).astype(jnp.bfloat16)
    normed_mlp = layer_norm(own_rows, small_vecs[2], small_vecs[3]).astype(jnp.bfloat16)
    attn_full, mlp_full = (
        lax.all_gather(normed_attn, "tensor", axis=0, tiled=True),
        lax.all_gather(normed_mlp, "tensor", axis=0, tiled=True),
    )
    full_qkv, full_qkv_bias, full_dense, full_up, full_up_bias, full_down = (
        lax.all_gather(qkv_weight, "dp", axis=0, tiled=True),
        lax.all_gather(qkv_bias, "dp", axis=1, tiled=True),
        lax.all_gather(dense_weight, "dp", axis=0, tiled=True),
        lax.all_gather(up_weight, "dp", axis=0, tiled=True),
        lax.all_gather(up_bias, "dp", axis=0, tiled=True),
        lax.all_gather(down_weight, "dp", axis=0, tiled=True),
    )
    model_width = full_qkv.shape[0]
    head_cols = full_qkv.shape[2]
    local_heads = head_cols // HD
    projected = jnp.dot(
        attn_full, full_qkv.reshape(model_width, 3 * head_cols), preferred_element_type=jnp.float32
    )
    projected = projected + full_qkv_bias.reshape(3 * head_cols).astype(jnp.float32)
    projected = projected.reshape(length, 3, local_heads, HD)
    cosine, sines = rotary_tables(length)
    query_rows = rotate(projected[:, 0], cosine, sines).astype(jnp.bfloat16)
    key_rows = rotate(projected[:, 1], cosine, sines).astype(jnp.bfloat16)
    value_rows = projected[:, 2].astype(jnp.bfloat16)
    position = jnp.arange(length, dtype=jnp.int32)
    starts_here = span_start[0]
    lengths_here = span_length[0]
    inside = (position[None, :] >= starts_here[:, None]) & (
        position[None, :] < (starts_here + lengths_here)[:, None]
    )
    marks = (jnp.arange(starts_here.shape[0], dtype=jnp.int32) + 1)[:, None]
    labels = jnp.sum(jnp.where(inside, marks, 0), axis=0)

    def block_scores(first_row, query_block):
        raw_scores = (
            jnp.einsum("qhe,khe->hqk", query_block, key_rows, preferred_element_type=jnp.float32)
            * score_scale
        )
        row_pos = first_row + jnp.arange(block_rows, dtype=jnp.int32)
        allowed = (position[None, :] <= row_pos[:, None]) | (labels[:, None] == labels[None, :]) & (
            labels[:, None] > 0
        )
        return jnp.where(allowed[None], raw_scores, NEG_FILL)

    def attend(first_row):
        scores = block_scores(first_row, query_rows)
        row_top = jnp.max(scores, axis=-1, keepdims=True)
        exponent = jnp.exp(scores - row_top)
        summed = jnp.sum(exponent, axis=-1, keepdims=True)
        prob_low = (exponent / summed).astype(jnp.bfloat16)
        context_block = jnp.einsum(
            "hqk,khe->qhe", prob_low, value_rows, preferred_element_type=jnp.float32
        )
        return (context_block.astype(jnp.bfloat16), (row_top + jnp.log(summed))[..., 0])

    block_starts = jnp.arange(block_count, dtype=jnp.int32) * block_rows
    context_blocks, lse_blocks = lax.map(attend, block_starts)
    context = context_blocks.reshape(length, head_cols)
    attn_part = jnp.dot(context, full_dense, preferred_element_type=jnp.float32)
    attn_mixed = lax.psum_scatter(
        attn_part.astype(jnp.bfloat16), "tensor", scatter_dimension=0, tiled=True
    ).astype(jnp.float32)
    hidden = jnp.dot(mlp_full, full_up, preferred_element_type=jnp.float32) + full_up_bias.astype(
        jnp.float32
    )
    active = gelu_exact(hidden).astype(jnp.bfloat16)
    mlp_part = jnp.dot(active, full_down, preferred_element_type=jnp.float32)
    mixed_rows = attn_mixed + lax.psum_scatter(
        mlp_part.astype(jnp.bfloat16), "tensor", scatter_dimension=0, tiled=True
    ).astype(jnp.float32)
    layer_out = (own_rows + mixed_rows + small_vecs[4] + small_vecs[5]).astype(jnp.bfloat16)
    cot_full = lax.all_gather(out_grad, "tensor", axis=0, tiled=True)
    full_qkv, full_dense, full_up, full_down = (
        lax.all_gather(qkv_weight, "dp", axis=0, tiled=True),
        lax.all_gather(dense_weight, "dp", axis=0, tiled=True),
        lax.all_gather(up_weight, "dp", axis=0, tiled=True),
        lax.all_gather(down_weight, "dp", axis=0, tiled=True),
    )
    down_grad = jnp.einsum("lf,ld->fd", active, cot_full, preferred_element_type=jnp.float32)
    dense_grad = jnp.einsum("le,ld->ed", context, cot_full, preferred_element_type=jnp.float32)
    active_grad = jnp.einsum("ld,fd->lf", cot_full, full_down, preferred_element_type=jnp.float32)
    hidden_grad = jax.vjp(gelu_exact, hidden)[1](active_grad)[0].astype(jnp.bfloat16)
    up_grad = jnp.einsum("ld,lf->df", mlp_full, hidden_grad, preferred_element_type=jnp.float32)
    up_bias_grad = jnp.sum(hidden_grad, axis=0, dtype=jnp.float32)
    mlp_in_grad = jnp.einsum("lf,df->ld", hidden_grad, full_up, preferred_element_type=jnp.float32)
    context_grad = jnp.einsum("ld,ed->le", cot_full, full_dense, preferred_element_type=jnp.float32)
    context_grad = context_grad.astype(jnp.bfloat16).reshape(length, local_heads, HD)

    def attend_back(carried, inputs):
        key_acc, value_acc = carried
        first_row, lse_block = inputs
        scores = block_scores(first_row, query_rows)
        prob_rows = jnp.exp(scores - lse_block[..., None])
        prob_low = prob_rows.astype(jnp.bfloat16)
        value_acc = value_acc + jnp.einsum(
            "hqk,qhe->khe", prob_low, context_grad, preferred_element_type=jnp.float32
        )
        prob_grad = jnp.einsum(
            "qhe,khe->hqk", context_grad, value_rows, preferred_element_type=jnp.float32
        )
        score_grad = prob_rows * (
            prob_grad - jnp.sum(prob_grad * prob_rows, axis=-1, keepdims=True)
        )
        score_grad = score_grad.astype(jnp.bfloat16)
        query_grad = (
            jnp.einsum("hqk,khe->qhe", score_grad, key_rows, preferred_element_type=jnp.float32)
            * score_scale
        )
        key_acc = (
            key_acc
            + jnp.einsum("hqk,qhe->khe", score_grad, query_rows, preferred_element_type=jnp.float32)
            * score_scale
        )
        return ((key_acc, value_acc), query_grad)

    zero_rows = jnp.zeros((length, local_heads, HD), jnp.float32)
    (key_grad, value_grad), query_blocks = lax.scan(
        attend_back, (zero_rows, zero_rows), (block_starts, lse_blocks)
    )
    query_grad = query_blocks.reshape(length, local_heads, HD)

    def turn(field_in):
        return rotate(field_in, cosine, sines)

    turn_back = jax.vjp(turn, zero_rows)[1]
    projected_grad = jnp.stack(
        [turn_back(query_grad)[0], turn_back(key_grad)[0], value_grad], axis=1
    )
    projected_grad = projected_grad.astype(jnp.bfloat16).reshape(length, 3 * head_cols)
    qkv_weight_grad = jnp.einsum(
        "ld,lc->dc", attn_full, projected_grad, preferred_element_type=jnp.float32
    )
    qkv_weight_grad = qkv_weight_grad.reshape(model_width, 3, head_cols)
    qkv_bias_grad = jnp.sum(projected_grad, axis=0, dtype=jnp.float32).reshape(3, head_cols)
    attn_in_grad = jnp.einsum(
        "lc,dc->ld",
        projected_grad,
        full_qkv.reshape(model_width, 3 * head_cols),
        preferred_element_type=jnp.float32,
    )
    reduced = (
        lax.psum_scatter(qkv_weight_grad, "dp", scatter_dimension=0, tiled=True),
        lax.psum_scatter(qkv_bias_grad, "dp", scatter_dimension=1, tiled=True),
        lax.psum_scatter(dense_grad, "dp", scatter_dimension=0, tiled=True),
        lax.psum_scatter(up_grad, "dp", scatter_dimension=0, tiled=True),
        lax.psum_scatter(up_bias_grad, "dp", scatter_dimension=0, tiled=True),
        lax.psum_scatter(down_grad, "dp", scatter_dimension=0, tiled=True),
    )
    attn_local, mlp_local = (
        lax.psum_scatter(
            attn_in_grad.astype(jnp.bfloat16), "tensor", scatter_dimension=0, tiled=True
        ).astype(jnp.float32),
        lax.psum_scatter(
            mlp_in_grad.astype(jnp.bfloat16), "tensor", scatter_dimension=0, tiled=True
        ).astype(jnp.float32),
    )
    pull_attn = jax.vjp(layer_norm, own_rows, small_vecs[0], small_vecs[1])[1]
    pull_mlp = jax.vjp(layer_norm, own_rows, small_vecs[2], small_vecs[3])[1]
    rows_grad_attn, gain_grad_attn, shift_grad_attn = pull_attn(attn_local)
    rows_grad_mlp, gain_grad_mlp, shift_grad_mlp = pull_mlp(mlp_local)
    cot_rows = out_grad.astype(jnp.float32)
    input_grad = (cot_rows + rows_grad_attn + rows_grad_mlp).astype(jnp.bfloat16)
    bias_total = jnp.sum(cot_rows, axis=0)
    small_sums = (
        lax.psum_scatter(gain_grad_attn, ("dp", "tensor"), scatter_dimension=0, tiled=True),
        lax.psum_scatter(shift_grad_attn, ("dp", "tensor"), scatter_dimension=0, tiled=True),
        lax.psum_scatter(gain_grad_mlp, ("dp", "tensor"), scatter_dimension=0, tiled=True),
        lax.psum_scatter(shift_grad_mlp, ("dp", "tensor"), scatter_dimension=0, tiled=True),
        lax.psum_scatter(bias_total, ("dp", "tensor"), scatter_dimension=0, tiled=True),
    )
    return (
        layer_out,
        input_grad,
        small_sums[0],
        small_sums[1],
        small_sums[2],
        small_sums[3],
        reduced[0],
        reduced[1],
        reduced[2],
        small_sums[4],
        reduced[3],
        reduced[4],
        reduced[5],
        small_sums[4],
    )


F32 = jnp.float32
BF16 = jnp.bfloat16
MESH_ID = pl.DeviceIdType.MESH
LINE = 4
SEQ = 256
WIDTH = 1024
HID = 512
PAIR = 128


def nn(a, b):
    return jnp.dot(a, b, preferred_element_type=F32)


def nt(a, b):
    return lax.dot_general(a, b, (((1,), (1,)), ((), ())), preferred_element_type=F32)


def tn(a, b):
    return lax.dot_general(a, b, (((0,), (0,)), ((), ())), preferred_element_type=F32)


def turn_tables():
    position = np.arange(SEQ, dtype=np.float64)[:, None]
    lane = np.arange(PAIR) % HD
    rates = 10000.0 ** (-(lane % (ROT // 2)) * (2.0 / ROT))
    angles = position * rates[None, :]
    cosine = np.where(lane < ROT, np.cos(angles), 1.0)
    toward = np.where(lane < ROT // 2, -np.sin(angles), 0.0)
    away = np.where((lane >= ROT // 2) & (lane < ROT), np.sin(angles), 0.0)
    return np.stack([cosine, toward, away]).astype(np.float32)


SEATS = (0, 3, 1, 2)


def seat_of(z):
    return (2 * z - z // 2) % LINE


def rows_of(index, count):
    return pl.ds(pl.multiple_of(index * count, count), count)


class Place:
    def __init__(self):
        index = lax.axis_index("dp")
        self.t = lax.axis_index("tensor")
        self.z = index // 4
        self.k = index % 4
        self.y = self.k // 2
        self.c = self.k % 2
        self.kc = self.y * 2 + 1 - self.c
        self.ky = (1 - self.y) * 2 + self.c
        self.kyc = (1 - self.y) * 2 + 1 - self.c
        self.q = self.k * 2 + self.t
        self.core = self.at(self.z, self.kc, self.t)
        self.cross = (
            self.at(self.z, self.k, 1 - self.t),
            self.at(self.z, self.ky, self.t),
            self.at(self.z, self.ky, 1 - self.t),
        )

    def at(self, z, k, t):
        return (z * 4 + k, t)

    def line(self, z):
        return self.at(z, self.k, self.t)


class Wires:
    def __init__(self, sends, arrivals):
        self.sends, self.arrivals = sends, arrivals
        self.sent, self.landed = 0, 0

    def take(self, sends, arrivals):
        first = (self.sent, self.landed)
        self.sent += sends
        self.landed += arrivals
        return first

    def copy(self, send, arrival, src, dst, device):
        return pltpu.make_async_remote_copy(
            src_ref=src,
            dst_ref=dst,
            send_sem=self.sends.at[send],
            recv_sem=self.arrivals.at[arrival],
            device_id=device,
            device_id_type=MESH_ID,
        )

    def all_sent(self, send, view, device):
        self.copy(send, 0, view, view, device).wait_send()

    def all_landed(self, arrival, view, device):
        self.copy(0, arrival, view, view, device).wait_recv()


class PlaneGather:
    def __init__(self, me, wires, src, slot, split, blocks):
        self.me, self.wires, self.src, self.slot = me, wires, src, slot
        self.blocks = blocks
        self.pieces = (pl.ds(0, split), pl.ds(split, src.shape[0] - split))
        self.send, self.arrivals = wires.take(1, 4)
        self.near_blocks = (
            me.k * 2 + 1 - me.t,
            me.ky * 2 + me.t,
            me.ky * 2 + 1 - me.t,
        )

    def start(self, which):
        device = (self.me.cross[0], self.me.cross[1], self.me.core)[which]
        arrival = self.arrivals + (0, 1, 3)[which]
        self.wires.copy(self.send, arrival, self.src, self.slot(self.me.q), device).start()

    def pass_on(self, which):
        part = self.slot(self.near_blocks[which])
        self.wires.copy(self.send, self.arrivals + 3, part, part, self.me.core).start()

    def forward(self, which):
        block = self.slot(self.near_blocks[which])
        self.wires.all_landed(self.arrivals + which, block, self.me.core)
        part = block.at[self.pieces[which]]
        device = self.me.cross[1 - which]
        self.wires.copy(self.send, self.arrivals + 2, part, part, device).start()
        self.pass_on(which)

    def corner(self):
        block = self.slot(self.near_blocks[2])
        self.wires.all_landed(self.arrivals + 2, block, self.me.core)
        self.pass_on(2)

    def finish(self):
        self.wires.all_landed(self.arrivals + 3, self.blocks(4), self.me.core)

    def drain(self):
        self.wires.all_sent(self.send, self.blocks(7), self.me.core)


class LineGather:
    def __init__(self, me, wires, view):
        self.me, self.wires, self.view = me, wires, view
        self.sends, self.arrivals = wires.take(2, 6)

    def copy(self, way, hop, block):
        z = self.me.z
        view = self.view(block, 1)
        device = self.me.line(z + 1 if way == 0 else z - 1)
        return self.wires.copy(self.sends + way, self.arrivals + way * 3 + hop, view, view, device)

    def send(self, way, hop):
        z = self.me.z
        has = (z >= hop) & (z < LINE - 1) if way == 0 else (z + hop < LINE) & (z > 0)

        @pl.when(has)
        def _():
            self.copy(way, hop, z - hop if way == 0 else z + hop).start()

    def arrive(self, way, hop):
        z = self.me.z

        @pl.when(z > hop if way == 0 else z + 1 + hop < LINE)
        def _():
            self.copy(way, hop, z - 1 - hop if way == 0 else z + 1 + hop).wait_recv()

    def start(self, way):
        @pl.when(self.me.z != (0 if way == 0 else LINE - 1))
        def _():
            self.send(way, 0)

    def outer(self):
        for way in range(2):

            @pl.when(self.me.z == (0 if way == 0 else LINE - 1))
            def _(way=way):
                self.send(way, 0)

    def relay(self, way, hop):
        self.arrive(way, hop - 1)
        self.send(way, hop)

    def finish(self, way):
        self.arrive(way, LINE - 2)

    def drain(self):
        z = self.me.z
        for way in range(2):
            for count in range(1, LINE):

                @pl.when(z == (count - 1 if way == 0 else LINE - count))
                def _():
                    self.wires.all_sent(self.sends + way, self.view(0, count), self.me.core)


class LineReduce:
    def __init__(self, me, wires, held, landed):
        self.me, self.wires, self.held, self.landed = me, wires, held, landed
        self.sends, self.arrivals = wires.take(2, 6)

    def copy(self, way, block):
        z = self.me.z
        device = self.me.line(z - 1 if way == 0 else z + 1)
        return self.wires.copy(
            self.sends + way,
            self.arrivals + way * (LINE - 2) + block,
            self.held.at[block],
            self.landed.at[way, block],
            device,
        )

    def join(self, way, block):
        self.copy(way, block).wait_recv()
        total = self.held[block].astype(F32) + self.landed[way, block].astype(F32)
        self.held[block] = total.astype(BF16)

    def each(self, way, slot, act):
        z = self.me.z
        steps = slot - (LINE - 1 - z if way == 0 else z)
        left = z if way == 0 else LINE - 1 - z
        block = steps if way == 0 else LINE - 1 - steps

        @pl.when((steps >= 0) & (steps < left))
        def _():
            act(block)

    def slot(self, way, slot):
        def act(block):
            if slot > 0:
                started = self.me.z < LINE - 1 if way == 0 else self.me.z > 0

                @pl.when(started)
                def _():
                    self.join(way, block)

            self.copy(way, block).start()

        self.each(way, slot, act)

    def finish(self, way):
        z = self.me.z

        @pl.when(z < LINE - 1 if way == 0 else z > 0)
        def _():
            self.join(way, z)

    def drain(self):
        z = self.me.z
        for way in range(2):
            for count in range(1, LINE):

                @pl.when(z == (count if way == 0 else LINE - 1 - count))
                def _():
                    view = self.held.at[pl.ds(0, count)]
                    self.wires.all_sent(self.sends + way, view, self.me.core)


class PlaneReduce:
    def __init__(self, me, wires, part, paired, crossed):
        self.me, self.wires = me, wires
        self.part, self.paired, self.crossed = part, paired, crossed
        self.send, self.arrivals = wires.take(1, 4)
        self.blocks = (me.ky * 2 + 1 - me.t, me.k * 2 + 1 - me.t, me.ky * 2 + me.t)

    def pair(self, y):
        rows = rows_of(y * 2 + 1 - self.me.c, SEQ)
        return self.wires.copy(
            self.send, self.arrivals, self.part.at[rows], self.paired.at[y], self.me.core
        )

    def rows(self, which, half):
        first = pl.multiple_of(self.blocks[which] * 128 + half * 64, 64)
        return pl.ds(first, 64)

    def cross(self, which, half):
        way = (half, 0, 1)[which]
        return self.wires.copy(
            self.send,
            self.arrivals + (1 + half if which == 0 else 3),
            self.part.at[self.rows(which, half)],
            self.crossed.at[which, pl.ds(half * 64, 64)],
            self.me.cross[way],
        )

    def middle(self):
        self.wires.all_landed(self.arrivals, self.part.at[pl.ds(0, 2 * SEQ)], self.me.core)
        for y in range(2):
            rows = rows_of(y * 2 + self.me.c, SEQ)
            total = self.part[rows].astype(F32) + self.paired[y].astype(F32)
            self.part[rows] = total.astype(BF16)
        for which, half in ((0, 0), (0, 1), (1, 0), (2, 1)):
            self.cross(which, half).start()

    def turn(self, half):
        self.cross(0, half).wait_recv()
        rows = self.rows(2 - half, half)
        total = self.part[rows].astype(F32) + self.crossed[0, pl.ds(half * 64, 64)].astype(F32)
        self.part[rows] = total.astype(BF16)
        self.cross(2 - half, half).start()

    def finish(self):
        self.wires.all_landed(self.arrivals + 3, self.part.at[pl.ds(0, SEQ)], self.me.core)
        total = self.part[rows_of(self.me.q, 128)].astype(F32)
        return total + self.crossed[1].astype(F32) + self.crossed[2].astype(F32)

    def drain(self):
        self.wires.all_sent(self.send, self.part.at[pl.ds(0, 896)], self.me.core)


def layer_kernel(
    x_hbm,
    g_hbm,
    qkv_hbm,
    dense_hbm,
    up_hbm,
    down_hbm,
    turn_hbm,
    attn_gain_ref,
    attn_shift_ref,
    mlp_gain_ref,
    mlp_shift_ref,
    dense_bias_ref,
    down_bias_ref,
    starts_ref,
    lengths_ref,
    qkv_bias_ref,
    up_bias_ref,
    layer_out_ref,
    input_grad_ref,
    qkv_grad_ref,
    dense_grad_ref,
    up_grad_ref,
    down_grad_ref,
    small_out_ref,
    turn_ref,
    x_all,
    g_all,
    small_line,
    small_all,
    qkv_w,
    dense_w,
    up_w,
    down_w,
    vec_ref,
    bias_ref,
    normed_a,
    normed_m,
    context_ref,
    turned_grad,
    active_ref,
    hidden_grad,
    slope_ref,
    part_out,
    part_attn,
    part_mlp,
    paired_ref,
    crossed_ref,
    up_held,
    up_landed,
    down_held,
    down_landed,
    qkv_held,
    qkv_landed,
    up_final,
    qkv_final,
    dense_line,
    dense_held,
    dense_mine,
    dense_landed,
    qkv_bias_held,
    qkv_bias_line,
    qkv_bias_final,
    up_bias_held,
    up_bias_final,
    sums_held,
    sums_chip,
    sums_total,
    sums_core,
    sums_cross,
    sums_line,
    sends,
    arrivals,
    local_sems,
):
    me = Place()
    wires = Wires(sends, arrivals)
    z, k, t = me.z, me.k, me.t

    barrier = pltpu.get_barrier_semaphore()

    def greet(device):
        pl.semaphore_signal(barrier, inc=1, device_id=device, device_id_type=MESH_ID)

    greet(me.core)
    greet(me.at(z, me.kyc, t))
    for device in me.cross:
        greet(device)
    for step in range(1, LINE):
        greet(me.line((z + step) % LINE))
    local_copies = []

    def local(src, dst):
        copy = pltpu.make_async_copy(src, dst, local_sems.at[len(local_copies)])
        local_copies.append(copy)
        copy.start()

    seat = pl.ds(pl.multiple_of(z * 256 + k * 64, 64), 64)
    peers = (me.kc, me.ky, me.kyc)
    devices = tuple(me.at(z, peer, t) for peer in peers)

    def three(arrival, view):
        wires.all_landed(arrival, view, me.core)

    local(dense_hbm, dense_line.at[z])
    for place, other in enumerate(SEATS):
        local(
            up_hbm.at[:, rows_of(other * 4 + k, 128)],
            up_w.at[seat, pl.ds(place * 128, 128)],
        )
    local(down_hbm, down_w.at[rows_of(seat_of(z), 128)])
    for which in range(3):
        local(
            qkv_hbm.at[which, :, rows_of(k, PAIR)],
            qkv_w.at[seat, pl.ds(which * PAIR, PAIR)],
        )
    local(x_hbm, x_all.at[rows_of(me.q, 128)])
    local(g_hbm, g_all.at[rows_of(me.q, 128)])
    local(turn_hbm, turn_ref)
    qkv_bias_held[...] = jnp.zeros_like(qkv_bias_held)
    up_bias_held[...] = jnp.zeros_like(up_bias_held)

    def side_by_side(*fields):
        return jnp.concatenate(
            [field.astype(F32).reshape(1, field.shape[-1]) for field in fields], axis=1
        )

    triple = qkv_bias_ref[...]
    blank = jnp.zeros((1, 60), F32)
    small_line[z] = jnp.concatenate(
        [
            side_by_side(
                attn_gain_ref[...], attn_shift_ref[...], mlp_gain_ref[...], mlp_shift_ref[...]
            ),
            side_by_side(
                dense_bias_ref[...], down_bias_ref[...], starts_ref[...], lengths_ref[...], blank
            ),
            side_by_side(triple[0:1], triple[1:2], triple[2:3], blank[:, :32]),
            side_by_side(up_bias_ref[...]),
            jnp.zeros((4, 128), F32),
        ],
        axis=0,
    )
    pl.semaphore_wait(barrier, 8)

    up_send, up_arrival = wires.take(1, 2)
    for place, other in enumerate(SEATS):
        for which in range(3):
            wires.copy(
                up_send,
                up_arrival + place // 2,
                up_hbm.at[:, rows_of(other * 4 + peers[which], 128)],
                up_w.at[seat, pl.ds(place * 128, 128)],
                devices[which],
            ).start()

    qkv_sends, qkv_arrival = wires.take(1, 1)

    def rows_slot(ref):
        return (lambda block: ref.at[rows_of(block, 128)]), (
            lambda count: ref.at[pl.ds(0, count * 128)]
        )

    slot, blocks = rows_slot(x_all)
    gather_x = PlaneGather(me, wires, x_hbm, slot, 48, blocks)
    for which in range(3):
        gather_x.start(which)
    slot, blocks = rows_slot(g_all)
    gather_g = PlaneGather(me, wires, g_hbm, slot, 48, blocks)
    gather_small = PlaneGather(
        me,
        wires,
        small_line,
        lambda block: small_all.at[block],
        2,
        lambda count: small_all.at[pl.ds(0, count)],
    )
    small_send, small_arrival = wires.take(1, 1)
    for step in range(1, LINE):
        wires.copy(
            small_send,
            small_arrival,
            small_line.at[z],
            small_line.at[z],
            me.line((z + step) % LINE),
        ).start()

    def line_gather(ref, count):
        return LineGather(
            me, wires, lambda s, n: ref.at[pl.ds(pl.multiple_of(s * count, count), n * count)]
        )

    line_dense = LineGather(me, wires, lambda s, n: dense_line.at[pl.ds(s, n)])
    line_qkv = line_gather(qkv_w, 256)
    line_upa, line_upb = (
        LineGather(
            me,
            wires,
            lambda s, n, first=first: up_w.at[
                pl.ds(pl.multiple_of(s * 256, 256), n * 256), pl.ds(first, 256)
            ],
        )
        for first in (0, 256)
    )
    line_down = LineGather(
        me,
        wires,
        lambda s, n: down_w.at[pl.ds(pl.multiple_of(seat_of(s) * 128, 128), n * 128)],
    )
    reduce_down = LineReduce(
        me, wires, down_held, down_landed
    )
    reduce_up = LineReduce(
        me, wires, up_held, up_landed
    )
    reduce_qkv = LineReduce(
        me, wires, qkv_held, qkv_landed
    )
    reduce_dense = LineReduce(
        me, wires, dense_mine, dense_landed
    )
    reduce_attn = PlaneReduce(me, wires, part_attn, paired_ref.at[0], crossed_ref.at[0])
    reduce_out = PlaneReduce(me, wires, part_out, paired_ref.at[1], crossed_ref.at[1])
    reduce_mlp = PlaneReduce(me, wires, part_mlp, paired_ref.at[2], crossed_ref.at[2])

    local_copies[0].wait()
    line_dense.outer()
    line_dense.start(0)
    line_dense.start(1)

    own_small = pltpu.make_async_copy(
        small_line, small_all.at[me.q], local_sems.at[len(local_copies)]
    )
    own_dense = pltpu.make_async_copy(
        dense_line.at[k], dense_w.at[rows_of(k, 32)], local_sems.at[len(local_copies) + 1]
    )
    dense_sends, dense_arrival = wires.take(1, 1)
    back_sends, back_arrival = wires.take(2, 2)
    bias_sends, bias_arrival = wires.take(2, 2)
    out_sends, out_arrival = wires.take(2, 2)
    sums_sends, sums_arrival = wires.take(3, 3)

    def along(send, arrival, source, target):
        for step in range(1, LINE):
            there = (z + step) % LINE
            wires.copy(send, arrival, source(there), target, me.line(there)).start()

    def around(send, arrival, source, target):
        for which in range(3):
            wires.copy(send, arrival, source(peers[which]), target, devices[which]).start()

    def norm_rows(rows):
        values = x_all[rows].astype(F32)
        centred = values - jnp.mean(values, axis=-1, keepdims=True)
        rate = lax.rsqrt(jnp.mean(centred * centred, axis=-1, keepdims=True) + NORM_EPS)
        return centred * rate, rate

    def norm_block(block, carry):
        rows = rows_of(block, 128)
        unit, _ = norm_rows(rows)
        normed_a[rows] = (unit * vec_ref[0:1, :] + vec_ref[1:2, :]).astype(BF16)
        normed_m[rows] = (unit * vec_ref[2:3, :] + vec_ref[3:4, :]).astype(BF16)
        return carry

    def activate(half):
        columns = slice(half * 256, (half + 1) * 256)

        def tile_of(tile, carry):
            rows = rows_of(tile, 256)
            up_bias = jnp.concatenate(
                [small_all[me.q, s, 3:4, :] for s in SEATS[half * 2 : half * 2 + 2]], axis=1
            )
            hidden = nn(normed_m[rows], up_w[:, columns]) + up_bias
            share = (1.0 + lax.erf(hidden * 0.5**0.5)) * 0.5
            bell = jnp.exp(hidden * hidden * -0.5) * (2.0 * np.pi) ** -0.5
            slope_ref[rows, columns] = share + hidden * bell
            active_ref[rows, columns] = (hidden * share).astype(BF16)
            return carry

        return tile_of

    activate_a, activate_b = activate(0), activate(1)

    def down_block(block, carry):
        units = rows_of(seat_of(block), 128)
        down_held[block] = tn(active_ref[:, units], g_all[...]).astype(BF16)
        return carry

    def feed_back(tile, carry):
        rows = rows_of(tile, 256)
        grad = (nt(g_all[rows], down_w[...]) * slope_ref[rows]).astype(BF16)
        hidden_grad[rows] = grad
        up_bias_held[0:1, :] += jnp.sum(grad.astype(F32), axis=0, keepdims=True)
        return carry

    def feed_in(tile, carry):
        rows = rows_of(tile, 256)
        part_mlp[rows] = nt(hidden_grad[rows], up_w[...]).astype(BF16)
        return carry

    def up_block(block, carry):
        up_held[block] = tn(normed_m[:, rows_of(block, 256)], hidden_grad[...]).astype(BF16)
        return carry

    scale = HD**-0.5

    def attend(seq, carry):
        rows = rows_of(seq, SEQ)
        cosine, toward, away = turn_ref[0], turn_ref[1], turn_ref[2]
        projected = nn(normed_a[rows], qkv_w[...]) + bias_ref[0:1, :]

        def project(which):
            return projected[:, which * PAIR : (which + 1) * PAIR]

        def turned(field):
            return (
                field * cosine
                + pltpu.roll(field, ROT // 2, 1) * away
                + pltpu.roll(field, PAIR - ROT // 2, 1) * toward
            )

        def turned_back(field):
            return (
                field * cosine
                - pltpu.roll(field, ROT // 2, 1) * away
                - pltpu.roll(field, PAIR - ROT // 2, 1) * toward
            )

        query = turned(project(0)).astype(BF16)
        key = turned(project(1)).astype(BF16)
        value = project(2).astype(BF16)
        context_grad = nt(g_all[rows], dense_w[...]).astype(BF16)

        spans = small_all[seq * 2, z, 1:2, :]
        down_pos = lax.broadcasted_iota(jnp.int32, (SEQ, 1), 0).astype(F32)
        over_pos = lax.broadcasted_iota(jnp.int32, (1, SEQ), 1).astype(F32)

        def labels(place):
            total = jnp.zeros(place.shape, F32)
            for span in range(2):
                begin = spans[:, 64 + span : 65 + span]
                end = begin + spans[:, 66 + span : 67 + span]
                total = total + jnp.where((place >= begin) & (place < end), span + 1.0, 0.0)
            return total

        down_label, over_label = labels(down_pos), labels(over_pos)
        allowed = (over_pos <= down_pos) | ((down_label == over_label) & (down_label > 0.0))

        lane = lax.broadcasted_iota(jnp.int32, (SEQ, PAIR), 1)
        parts = []
        for head in range(2):
            mine = (lane >= HD) if head else (lane < HD)
            zero = jnp.zeros_like(query)
            scores = nt(jnp.where(mine, query, zero), key) * scale
            scores = jnp.where(allowed, scores, NEG_FILL)
            exponent = jnp.exp(scores - jnp.max(scores, axis=-1, keepdims=True))
            probs = exponent * (1.0 / jnp.sum(exponent, axis=-1, keepdims=True))
            low = probs.astype(BF16)
            prob_grad = nt(jnp.where(mine, context_grad, zero), value)
            inner = jnp.sum(prob_grad * probs, axis=-1, keepdims=True)
            score_grad = (probs * (prob_grad - inner)).astype(BF16)
            parts.append(
                (
                    nn(low, value),
                    tn(low, context_grad),
                    nn(score_grad, key) * scale,
                    tn(score_grad, query) * scale,
                )
            )
        context, value_grad, query_grad, key_grad = (
            jnp.where(lane < HD, first, second) for first, second in zip(*parts)
        )
        context_ref[rows] = context.astype(BF16)
        grads = (
            turned_back(query_grad).astype(BF16),
            turned_back(key_grad).astype(BF16),
            value_grad.astype(BF16),
        )
        for which in range(3):
            turned_grad[rows, which * PAIR : (which + 1) * PAIR] = grads[which]
            qkv_bias_held[which : which + 1, :] += jnp.sum(
                grads[which].astype(F32), axis=0, keepdims=True
            )
        part_attn[rows] = nt(turned_grad[rows], qkv_w[...]).astype(BF16)
        return carry

    def qkv_block(block, carry):
        qkv_held[block] = tn(normed_a[:, rows_of(block, 256)], turned_grad[...]).astype(BF16)
        return carry

    def mix(tile, carry):
        rows = rows_of(tile, 256)
        mixed = nn(context_ref[rows], dense_w[...]) + nn(active_ref[rows], down_w[...])
        part_out[rows] = mixed.astype(BF16)
        return carry

    def locals_done():
        for copy in local_copies[1:]:
            copy.wait()

    def small_line_done():
        three(small_arrival, small_line.at[pl.ds(0, 3)])
        own_small.start()
        for which in range(3):
            gather_small.start(which)

    def upa_start():
        three(up_arrival, up_w.at[pl.ds(0, 96)])
        line_upa.outer()
        line_upa.start(0)
        line_upa.start(1)

    def upb_start():
        three(up_arrival + 1, up_w.at[pl.ds(0, 96)])
        line_upb.outer()
        line_upb.start(0)
        line_upb.start(1)

    def down_outer():
        line_down.outer()

    def qkv_send():
        for which in range(3):
            for part in range(3):
                wires.copy(
                    qkv_sends,
                    qkv_arrival,
                    qkv_hbm.at[part, :, rows_of(peers[which], PAIR)],
                    qkv_w.at[seat, pl.ds(part * PAIR, PAIR)],
                    devices[which],
                ).start()

    def qkv_outer():
        three(qkv_arrival, qkv_w.at[pl.ds(0, 192)])
        line_qkv.outer()

    def qkv_start():
        line_qkv.start(0)
        line_qkv.start(1)

    def down_start():
        line_down.start(0)
        line_down.start(1)

    def dense_send():
        around(
            dense_sends, dense_arrival, lambda to: dense_line.at[to], dense_w.at[rows_of(k, 32)]
        )
        own_dense.start()

    def dense_done():
        three(dense_arrival, dense_w.at[pl.ds(0, 96)])
        own_dense.wait()

    def vectors():
        own_small.wait()
        table = small_all[...].reshape(256, 128).astype(BF16)
        line_id = lax.broadcasted_iota(jnp.int32, (256, WIDTH), 0)
        column = lax.broadcasted_iota(jnp.int32, (256, WIDTH), 1)
        owner = ((line_id >> 3) & 3) * 8 + (line_id >> 5)
        lane_row = lax.broadcasted_iota(jnp.int32, (128, WIDTH), 0)
        lane_col = lax.broadcasted_iota(jnp.int32, (128, WIDTH), 1) & 31
        for kind, count, base in ((0, 4, 0), (1, 2, 4)):
            chosen = (owner == (column >> 5)) & ((line_id & 7) == kind)
            spread = tn(table, jnp.where(chosen, 1.0, 0.0).astype(BF16))
            for which in range(count):
                picked = jnp.where(lane_row == lane_col + which * 32, spread, 0.0)
                vec_ref[base + which : base + which + 1, :] = jnp.sum(picked, axis=0, keepdims=True)
        line_id = line_id[:, :PAIR]
        column = column[:, :PAIR]
        chosen = (
            (((line_id >> 3) & 3) == k)
            & ((line_id >> 5) == (column >> 5) * 2 + t)
            & ((line_id & 7) == 2)
        )
        spread = tn(table, jnp.where(chosen, 1.0, 0.0).astype(BF16))
        for which in range(3):
            picked = jnp.where(lane_row[:, :PAIR] == lane_col[:, :PAIR] + which * 32, spread, 0.0)
            total = jnp.sum(picked, axis=0, keepdims=True)
            bias_ref[0:1, which * PAIR : (which + 1) * PAIR] = total

    def up_bias_send():
        along(
            bias_sends,
            bias_arrival,
            lambda there: up_bias_held.at[:, rows_of(seat_of(there), 128)],
            up_bias_final.at[z],
        )
        up_bias_final[z] = up_bias_held[:, rows_of(seat_of(z), 128)]

    def dense_part():
        dense_held[...] = tn(context_ref[...], g_all[...]).astype(BF16)
        around(
            back_sends, back_arrival, lambda to: dense_held.at[rows_of(to, 32)], dense_mine.at[k]
        )
        around(back_sends + 1, back_arrival + 1, lambda to: qkv_bias_held, qkv_bias_line.at[k])
        dense_mine[k] = dense_held[rows_of(k, 32)]
        qkv_bias_line[k] = qkv_bias_held[...]

    def dense_back():
        three(back_arrival, dense_mine.at[pl.ds(0, 3)])
        three(back_arrival + 1, qkv_bias_line.at[pl.ds(0, 3)])
        along(
            bias_sends + 1,
            bias_arrival + 1,
            lambda there: qkv_bias_line.at[there],
            qkv_bias_final.at[z],
        )
        qkv_bias_final[z] = qkv_bias_line[z]

    def up_out():
        around(
            out_sends, out_arrival, lambda to: up_held.at[z, rows_of(to, 64)], up_final.at[k]
        )
        up_final[k] = up_held[z, rows_of(k, 64)]

    def qkv_out():
        around(
            out_sends + 1,
            out_arrival + 1,
            lambda to: qkv_held.at[z, rows_of(to, 64)],
            qkv_final.at[k],
        )
        qkv_final[k] = qkv_held[z, rows_of(k, 64)]

    def down_out():
        down_grad_ref[...] = down_held[z]

    def dense_out():
        dense_grad_ref[...] = dense_mine[z]

    def up_result():
        three(out_arrival, up_final.at[pl.ds(0, 3)])
        up_grad_ref[...] = up_final[...]

    def qkv_result():
        three(out_arrival + 1, qkv_final.at[pl.ds(0, 3)])
        qkv_grad_ref[...] = qkv_final[...]

    own = rows_of(me.q, 128)
    def layer_out():
        mixed = reduce_out.finish()
        layer_out_ref[...] = (
            x_all[own].astype(F32) + mixed + vec_ref[4:5, :] + vec_ref[5:6, :]
        ).astype(BF16)

    def norm_grads():
        from_attn = reduce_attn.finish()
        from_mlp = reduce_mlp.finish()
        cotangent = g_all[own].astype(F32)
        unit, rate = norm_rows(own)
        sums_held[...] = jnp.zeros_like(sums_held)
        for which, field in enumerate(
            (from_attn * unit, from_attn, from_mlp * unit, from_mlp, cotangent)
        ):
            sums_held[which : which + 1, :] = jnp.sum(field, axis=0, keepdims=True)
        wires.copy(sums_sends, sums_arrival, sums_held, sums_core, me.core).start()
        pulled = from_attn * vec_ref[0:1, :] + from_mlp * vec_ref[2:3, :]
        pulled = (
            pulled
            - jnp.mean(pulled, axis=-1, keepdims=True)
            - unit * jnp.mean(pulled * unit, axis=-1, keepdims=True)
        )
        input_grad_ref[...] = (cotangent + rate * pulled).astype(BF16)

    def sums_plane():
        three(sums_arrival, sums_core)
        sums_chip[...] = sums_held[...] + sums_core[...]
        for which in range(3):
            wires.copy(
                sums_sends + 1,
                sums_arrival + 1,
                sums_chip,
                sums_cross.at[which],
                me.cross[which],
            ).start()

    def sums_send():
        three(sums_arrival + 1, sums_cross)
        sums_total[...] = sums_chip[...] + sums_cross[0] + sums_cross[1] + sums_cross[2]
        along(
            sums_sends + 2,
            sums_arrival + 2,
            lambda there: sums_total.at[:, rows_of(there, 256)],
            sums_line.at[z],
        )
        sums_line[z] = sums_total[:, rows_of(z, 256)]

    def small_result():
        three(sums_arrival + 2, sums_line.at[pl.ds(0, 3)])
        three(bias_arrival, up_bias_final.at[pl.ds(0, 3)])
        three(bias_arrival + 1, qkv_bias_final.at[pl.ds(0, 3)])
        sums = sums_line[0] + sums_line[1] + sums_line[2] + sums_line[3]
        sums = jnp.where(k >= 2, sums[:, 128:], sums[:, :128])
        small_out_ref[0:8, :] = pltpu.roll(sums, (128 - (me.q % 4) * 32) % 128, 1)
        bias_sum = qkv_bias_final[0] + qkv_bias_final[1] + qkv_bias_final[2] + qkv_bias_final[3]
        small_out_ref[8:16, :] = pltpu.roll(bias_sum, (128 - k * 32) % 128, 1)
        small_out_ref[16:24, :] = (
            up_bias_final[0] + up_bias_final[1] + up_bias_final[2] + up_bias_final[3]
        )

    def ends_of(body):
        def outer(index, carry):
            return body(index * (LINE - 1), carry)

        return outer

    locals_done()
    upa_start()
    line_dense.relay(0, 1)
    upb_start()
    small_line_done()
    qkv_send()
    gather_g.start(0)
    line_dense.relay(1, 1)
    line_upa.relay(1, 1)
    line_upa.relay(0, 1)
    qkv_outer()
    qkv_start()
    gather_small.forward(0)
    line_upb.relay(0, 1)
    gather_x.forward(0)
    line_dense.relay(1, 2)
    gather_small.forward(1)
    gather_g.start(1)
    line_upb.relay(1, 1)
    gather_x.forward(1)
    gather_x.corner()
    line_upa.relay(0, 2)
    gather_small.corner()
    gather_small.finish()
    gather_g.forward(0)
    line_upa.finish(0)
    line_dense.relay(0, 2)
    line_qkv.relay(1, 1)
    line_dense.finish(1)
    gather_g.forward(1)
    line_dense.finish(0)
    line_qkv.relay(0, 1)
    vectors()
    line_upb.relay(1, 2)
    gather_x.finish()
    dense_send()
    line_upb.relay(0, 2)
    line_upa.relay(1, 2)
    gather_g.start(2)
    down_outer()
    gather_g.corner()
    line_qkv.relay(0, 2)
    lax.fori_loop(4, 8, norm_block, 0)
    lax.fori_loop(0, 4, norm_block, 0)
    line_qkv.relay(1, 2)
    line_upa.finish(1)
    line_upb.finish(0)
    line_upb.finish(1)
    lax.fori_loop(0, 4, activate_a, 0)
    dense_done()
    down_start()
    gather_g.finish()
    lax.fori_loop(0, 4, activate_b, 0)
    lax.fori_loop(0, 2, ends_of(down_block), 0)
    line_qkv.finish(1)
    line_qkv.finish(0)
    reduce_down.slot(1, 0)
    reduce_down.slot(0, 0)
    lax.fori_loop(2, 3, attend, 0)
    lax.fori_loop(1, 2, attend, 0)
    line_down.relay(1, 1)
    line_down.relay(0, 1)
    lax.fori_loop(1, 3, down_block, 0)
    reduce_down.slot(0, 1)
    lax.fori_loop(3, 4, attend, 0)
    reduce_down.slot(1, 1)
    lax.fori_loop(0, 1, attend, 0)
    line_down.relay(1, 2)
    line_down.relay(0, 2)
    lax.fori_loop(0, 2, ends_of(qkv_block), 0)
    reduce_qkv.slot(0, 0)
    reduce_qkv.slot(1, 0)
    reduce_down.slot(0, 2)
    dense_part()
    lax.fori_loop(1, 3, qkv_block, 0)
    line_down.finish(1)
    line_down.finish(0)
    lax.fori_loop(0, 2, feed_back, 0)
    reduce_qkv.slot(0, 1)
    reduce_qkv.slot(1, 1)
    lax.fori_loop(2, 4, feed_back, 0)
    reduce_attn.pair(0).start()
    lax.fori_loop(0, 2, ends_of(up_block), 0)
    reduce_up.slot(1, 0)
    reduce_attn.pair(1).start()
    lax.fori_loop(0, 2, mix, 0)
    reduce_attn.middle()
    reduce_up.slot(0, 0)
    reduce_out.pair(0).start()
    dense_back()
    lax.fori_loop(2, 4, mix, 0)
    reduce_out.pair(1).start()
    lax.fori_loop(2, 4, feed_in, 0)
    reduce_qkv.slot(1, 2)
    reduce_out.middle()
    reduce_qkv.slot(0, 2)
    reduce_attn.turn(0)
    reduce_down.finish(0)
    lax.fori_loop(0, 2, feed_in, 0)
    lax.fori_loop(1, 3, up_block, 0)
    reduce_mlp.pair(1).start()
    reduce_mlp.pair(0).start()
    reduce_dense.slot(1, 0)
    reduce_up.slot(1, 1)
    reduce_up.slot(0, 1)
    reduce_qkv.finish(1)
    reduce_dense.slot(0, 0)
    up_bias_send()
    reduce_dense.slot(1, 1)
    reduce_mlp.middle()
    reduce_attn.turn(1)
    reduce_up.slot(1, 2)
    reduce_mlp.turn(0)
    reduce_mlp.turn(1)
    reduce_out.turn(1)
    reduce_qkv.finish(0)
    reduce_down.slot(1, 2)
    reduce_dense.slot(1, 2)
    reduce_up.slot(0, 2)
    reduce_out.turn(0)
    reduce_dense.slot(0, 1)
    qkv_out()
    norm_grads()
    reduce_up.finish(1)
    sums_plane()
    reduce_up.finish(0)
    layer_out()
    up_out()
    reduce_dense.slot(0, 2)
    sums_send()
    reduce_dense.finish(0)
    qkv_result()
    reduce_down.finish(1)
    down_out()
    reduce_dense.finish(1)
    up_result()
    small_result()
    dense_out()

    for send, view in (
        (up_send, up_w.at[pl.ds(0, 192)]),
        (qkv_sends, qkv_w.at[pl.ds(0, 192)]),
        (small_send, small_line.at[pl.ds(0, 3)]),
        (dense_sends, dense_w.at[pl.ds(0, 96)]),
        (back_sends, dense_mine.at[pl.ds(0, 3)]),
        (back_sends + 1, qkv_bias_line.at[pl.ds(0, 3)]),
        (bias_sends, up_bias_final.at[pl.ds(0, 3)]),
        (bias_sends + 1, qkv_bias_final.at[pl.ds(0, 3)]),
        (out_sends, up_final.at[pl.ds(0, 3)]),
        (out_sends + 1, qkv_final.at[pl.ds(0, 3)]),
        (sums_sends, sums_core),
        (sums_sends + 1, sums_cross),
        (sums_sends + 2, sums_line.at[pl.ds(0, 3)]),
    ):
        wires.all_sent(send, view, me.core)
    for item in (
        gather_x,
        gather_g,
        gather_small,
        line_dense,
        line_qkv,
        line_upa,
        line_upb,
        line_down,
        reduce_attn,
        reduce_out,
        reduce_mlp,
        reduce_qkv,
        reduce_dense,
        reduce_down,
        reduce_up,
    ):
        item.drain()


def final_kernel(
    layer_out_ref,
    input_grad_ref,
    qkv_ref,
    dense_ref,
    up_ref,
    down_ref,
    small_ref,
    layer_out,
    input_grad,
    attn_gain_grad,
    attn_shift_grad,
    mlp_gain_grad,
    mlp_shift_grad,
    qkv_grad,
    qkv_bias_grad,
    dense_grad,
    dense_bias_grad,
    up_grad,
    up_bias_grad,
    down_grad,
    down_bias_grad,
):
    layer_out[...] = layer_out_ref[...]
    input_grad[...] = input_grad_ref[...]
    for row, out in enumerate((attn_gain_grad, attn_shift_grad, mlp_gain_grad, mlp_shift_grad)):
        out[...] = small_ref[row, :32]
    dense_bias_grad[...] = small_ref[4, :32]
    down_bias_grad[...] = small_ref[4, :32]
    qkv_bias_grad[...] = small_ref[8:11, :32]
    up_bias_grad[...] = small_ref[16, :]
    for origin in range(4):
        for which in range(3):
            qkv_grad[which, :, origin * PAIR : (origin + 1) * PAIR] = qkv_ref[
                origin, :, which * PAIR : (which + 1) * PAIR
            ].astype(F32)
        for place, other in enumerate(SEATS):
            first = (other * 4 + origin) * 128
            up_grad[:, first : first + 128] = up_ref[
                origin, :, place * 128 : (place + 1) * 128
            ].astype(F32)
    dense_grad[...] = dense_ref[...].astype(F32)
    down_grad[...] = down_ref[...].astype(F32)


def plane_layer(
    hidden_in,
    out_grad,
    span_start,
    span_length,
    attn_gain,
    attn_shift,
    mlp_gain,
    mlp_shift,
    qkv_weight,
    qkv_bias,
    dense_weight,
    dense_bias,
    up_weight,
    up_bias,
    down_weight,
    down_bias,
):
    vmem = pl.BlockSpec(memory_space=pltpu.VMEM)
    anywhere = pl.BlockSpec(memory_space=pl.ANY)
    tokens = 4 * SEQ
    outs = pl.pallas_call(
        layer_kernel,
        out_shape=(
            jax.ShapeDtypeStruct((128, WIDTH), BF16),
            jax.ShapeDtypeStruct((128, WIDTH), BF16),
            jax.ShapeDtypeStruct((4, 64, 3 * PAIR), BF16),
            jax.ShapeDtypeStruct((32, WIDTH), BF16),
            jax.ShapeDtypeStruct((4, 64, HID), BF16),
            jax.ShapeDtypeStruct((128, WIDTH), BF16),
            jax.ShapeDtypeStruct((24, 128), F32),
        ),
        in_specs=[anywhere] * 7 + [vmem] * 10,
        out_specs=(vmem,) * 7,
        scratch_shapes=[
            pltpu.VMEM((3, SEQ, PAIR), F32),
            pltpu.VMEM((tokens, WIDTH), BF16),
            pltpu.VMEM((tokens, WIDTH), BF16),
            pltpu.VMEM((LINE, 8, 128), F32),
            pltpu.VMEM((8, LINE, 8, 128), F32),
            pltpu.VMEM((WIDTH, 3 * PAIR), BF16),
            pltpu.VMEM((PAIR, WIDTH), BF16),
            pltpu.VMEM((WIDTH, HID), BF16),
            pltpu.VMEM((HID, WIDTH), BF16),
            pltpu.VMEM((8, WIDTH), F32),
            pltpu.VMEM((8, 3 * PAIR), F32),
            pltpu.VMEM((tokens, WIDTH), BF16),
            pltpu.VMEM((tokens, WIDTH), BF16),
            pltpu.VMEM((tokens, PAIR), BF16),
            pltpu.VMEM((tokens, 3 * PAIR), BF16),
            pltpu.VMEM((tokens, HID), BF16),
            pltpu.VMEM((tokens, HID), BF16),
            pltpu.VMEM((tokens, HID), F32),
            pltpu.VMEM((tokens, WIDTH), BF16),
            pltpu.VMEM((tokens, WIDTH), BF16),
            pltpu.VMEM((tokens, WIDTH), BF16),
            pltpu.VMEM((3, 2, SEQ, WIDTH), BF16),
            pltpu.VMEM((3, 3, 128, WIDTH), BF16),
            pltpu.VMEM((LINE, 256, HID), BF16),
            pltpu.VMEM((2, LINE, 256, HID), BF16),
            pltpu.VMEM((LINE, 128, WIDTH), BF16),
            pltpu.VMEM((2, LINE, 128, WIDTH), BF16),
            pltpu.VMEM((LINE, 256, 3 * PAIR), BF16),
            pltpu.VMEM((2, LINE, 256, 3 * PAIR), BF16),
            pltpu.VMEM((4, 64, HID), BF16),
            pltpu.VMEM((4, 64, 3 * PAIR), BF16),
            pltpu.VMEM((LINE, 32, WIDTH), BF16),
            pltpu.VMEM((PAIR, WIDTH), BF16),
            pltpu.VMEM((LINE, 32, WIDTH), BF16),
            pltpu.VMEM((2, LINE, 32, WIDTH), BF16),
            pltpu.VMEM((8, PAIR), F32),
            pltpu.VMEM((4, 8, PAIR), F32),
            pltpu.VMEM((LINE, 8, PAIR), F32),
            pltpu.VMEM((8, HID), F32),
            pltpu.VMEM((LINE, 8, 128), F32),
            pltpu.VMEM((8, WIDTH), F32),
            pltpu.VMEM((8, WIDTH), F32),
            pltpu.VMEM((8, WIDTH), F32),
            pltpu.VMEM((8, WIDTH), F32),
            pltpu.VMEM((3, 8, WIDTH), F32),
            pltpu.VMEM((LINE, 8, 256), F32),
            pltpu.SemaphoreType.DMA((37,)),
            pltpu.SemaphoreType.DMA((92,)),
            pltpu.SemaphoreType.DMA((14,)),
        ],
        compiler_params=pltpu.CompilerParams(
            collective_id=0, has_side_effects=True, vmem_limit_bytes=60 * 2**20
        ),
    )(
        hidden_in,
        out_grad,
        jnp.transpose(qkv_weight, (1, 0, 2)),
        dense_weight,
        up_weight,
        down_weight,
        jnp.asarray(turn_tables()),
        attn_gain,
        attn_shift,
        mlp_gain,
        mlp_shift,
        dense_bias,
        down_bias,
        span_start,
        span_length,
        qkv_bias,
        up_bias,
    )
    wide = jax.ShapeDtypeStruct((32,), F32)
    finals = pl.pallas_call(
        final_kernel,
        out_shape=(
            jax.ShapeDtypeStruct((128, WIDTH), BF16),
            jax.ShapeDtypeStruct((128, WIDTH), BF16),
            wide,
            wide,
            wide,
            wide,
            jax.ShapeDtypeStruct((3, 64, 512), F32),
            jax.ShapeDtypeStruct((3, 32), F32),
            jax.ShapeDtypeStruct((32, WIDTH), F32),
            wide,
            jax.ShapeDtypeStruct((64, 2048), F32),
            jax.ShapeDtypeStruct((128,), F32),
            jax.ShapeDtypeStruct((128, WIDTH), F32),
            wide,
        ),
        in_specs=[vmem] * 7,
        out_specs=(vmem,) * 14,
    )(*outs)
    return (*finals[:6], jnp.transpose(finals[6], (1, 0, 2)), *finals[7:])


def solution(mesh):
    in_specs = (
        P(("dp", "tensor"), None),
        P(("dp", "tensor"), None),
        P("dp", None),
        P("dp", None),
        P(("dp", "tensor")),
        P(("dp", "tensor")),
        P(("dp", "tensor")),
        P(("dp", "tensor")),
        P("dp", None, "tensor"),
        P(None, ("tensor", "dp")),
        P(("tensor", "dp"), None),
        P(("dp", "tensor")),
        P("dp", "tensor"),
        P(("tensor", "dp")),
        P(("tensor", "dp"), None),
        P(("dp", "tensor")),
    )
    out_specs = (
        P(("dp", "tensor"), None),
        P(("dp", "tensor"), None),
        P(("dp", "tensor")),
        P(("dp", "tensor")),
        P(("dp", "tensor")),
        P(("dp", "tensor")),
        P("dp", None, "tensor"),
        P(None, ("tensor", "dp")),
        P(("tensor", "dp"), None),
        P(("dp", "tensor")),
        P("dp", "tensor"),
        P(("tensor", "dp")),
        P(("tensor", "dp"), None),
        P(("dp", "tensor")),
    )
    fast = mesh.shape["dp"] == 16 and mesh.shape["tensor"] == 2
    return jax.shard_map(plane_layer if fast else shards, mesh=mesh, in_specs=in_specs, out_specs=out_specs, check_vma=False)
```

```python
import jax
import jax.numpy as jnp
import numpy as np
from jax import lax
from jax.experimental import pallas as pl
from jax.experimental.pallas import tpu as pltpu
from jax.sharding import PartitionSpec as P

HD = 64
ROT = 16


NORM_EPS = 1e-05
NEG_FILL = -1000000000.0


def layer_norm(rows_in, gain_vec, shift_vec):
    mean_row = jnp.mean(rows_in, axis=-1, keepdims=True)
    centred = rows_in - mean_row
    spread = jnp.mean(centred * centred, axis=-1, keepdims=True)
    return centred * lax.rsqrt(spread + NORM_EPS) * gain_vec + shift_vec


def rotary_tables(length):
    position = jnp.arange(length, dtype=jnp.float32)
    rates = 10000.0 ** (-jnp.arange(ROT // 2, dtype=jnp.float32) * (2.0 / ROT))
    angles = position[:, None] * rates[None, :]
    angles = jnp.concatenate([angles, angles], axis=-1)[:, None, :]
    return (jnp.cos(angles), jnp.sin(angles))


def rotate(field_in, cosine, sines):
    turned = field_in[..., :ROT]
    first_half = turned[..., : ROT // 2]
    second_half = turned[..., ROT // 2 :]
    swapped = jnp.concatenate([-second_half, first_half], axis=-1)
    return jnp.concatenate([turned * cosine + swapped * sines, field_in[..., ROT:]], axis=-1)


def gelu_exact(values_in):
    return jax.nn.gelu(values_in, approximate=False)


def shards(
    hidden_in,
    out_grad,
    span_start,
    span_length,
    attn_gain,
    attn_shift,
    mlp_gain,
    mlp_shift,
    qkv_weight,
    qkv_bias,
    dense_weight,
    dense_bias,
    up_weight,
    up_bias,
    down_weight,
    down_bias,
):
    local_rows = hidden_in.shape[0]
    length = local_rows * lax.axis_size("tensor")
    block_rows = min(512, length)
    block_count = length // block_rows
    score_scale = HD ** (-0.5)
    small_full = (
        lax.all_gather(attn_gain, ("dp", "tensor"), axis=0, tiled=True),
        lax.all_gather(attn_shift, ("dp", "tensor"), axis=0, tiled=True),
        lax.all_gather(mlp_gain, ("dp", "tensor"), axis=0, tiled=True),
        lax.all_gather(mlp_shift, ("dp", "tensor"), axis=0, tiled=True),
        lax.all_gather(dense_bias, ("dp", "tensor"), axis=0, tiled=True),
        lax.all_gather(down_bias, ("dp", "tensor"), axis=0, tiled=True),
    )
    small_vecs = [item.astype(jnp.float32) for item in small_full]
    own_rows = hidden_in.astype(jnp.float32)
    normed_attn = layer_norm(own_rows, small_vecs[0], small_vecs[1]).astype(jnp.bfloat16)
    normed_mlp = layer_norm(own_rows, small_vecs[2], small_vecs[3]).astype(jnp.bfloat16)
    attn_full, mlp_full = (
        lax.all_gather(normed_attn, "tensor", axis=0, tiled=True),
        lax.all_gather(normed_mlp, "tensor", axis=0, tiled=True),
    )
    full_qkv, full_qkv_bias, full_dense, full_up, full_up_bias, full_down = (
        lax.all_gather(qkv_weight, "dp", axis=0, tiled=True),
        lax.all_gather(qkv_bias, "dp", axis=1, tiled=True),
        lax.all_gather(dense_weight, "dp", axis=0, tiled=True),
        lax.all_gather(up_weight, "dp", axis=0, tiled=True),
        lax.all_gather(up_bias, "dp", axis=0, tiled=True),
        lax.all_gather(down_weight, "dp", axis=0, tiled=True),
    )
    model_width = full_qkv.shape[0]
    head_cols = full_qkv.shape[2]
    local_heads = head_cols // HD
    projected = jnp.dot(
        attn_full, full_qkv.reshape(model_width, 3 * head_cols), preferred_element_type=jnp.float32
    )
    projected = projected + full_qkv_bias.reshape(3 * head_cols).astype(jnp.float32)
    projected = projected.reshape(length, 3, local_heads, HD)
    cosine, sines = rotary_tables(length)
    query_rows = rotate(projected[:, 0], cosine, sines).astype(jnp.bfloat16)
    key_rows = rotate(projected[:, 1], cosine, sines).astype(jnp.bfloat16)
    value_rows = projected[:, 2].astype(jnp.bfloat16)
    position = jnp.arange(length, dtype=jnp.int32)
    starts_here = span_start[0]
    lengths_here = span_length[0]
    inside = (position[None, :] >= starts_here[:, None]) & (
        position[None, :] < (starts_here + lengths_here)[:, None]
    )
    marks = (jnp.arange(starts_here.shape[0], dtype=jnp.int32) + 1)[:, None]
    labels = jnp.sum(jnp.where(inside, marks, 0), axis=0)

    def block_scores(first_row, query_block):
        raw_scores = (
            jnp.einsum("qhe,khe->hqk", query_block, key_rows, preferred_element_type=jnp.float32)
            * score_scale
        )
        row_pos = first_row + jnp.arange(block_rows, dtype=jnp.int32)
        allowed = (position[None, :] <= row_pos[:, None]) | (labels[:, None] == labels[None, :]) & (
            labels[:, None] > 0
        )
        return jnp.where(allowed[None], raw_scores, NEG_FILL)

    def attend(first_row):
        scores = block_scores(first_row, query_rows)
        row_top = jnp.max(scores, axis=-1, keepdims=True)
        exponent = jnp.exp(scores - row_top)
        summed = jnp.sum(exponent, axis=-1, keepdims=True)
        prob_low = (exponent / summed).astype(jnp.bfloat16)
        context_block = jnp.einsum(
            "hqk,khe->qhe", prob_low, value_rows, preferred_element_type=jnp.float32
        )
        return (context_block.astype(jnp.bfloat16), (row_top + jnp.log(summed))[..., 0])

    block_starts = jnp.arange(block_count, dtype=jnp.int32) * block_rows
    context_blocks, lse_blocks = lax.map(attend, block_starts)
    context = context_blocks.reshape(length, head_cols)
    attn_part = jnp.dot(context, full_dense, preferred_element_type=jnp.float32)
    attn_mixed = lax.psum_scatter(
        attn_part.astype(jnp.bfloat16), "tensor", scatter_dimension=0, tiled=True
    ).astype(jnp.float32)
    hidden = jnp.dot(mlp_full, full_up, preferred_element_type=jnp.float32) + full_up_bias.astype(
        jnp.float32
    )
    active = gelu_exact(hidden).astype(jnp.bfloat16)
    mlp_part = jnp.dot(active, full_down, preferred_element_type=jnp.float32)
    mixed_rows = attn_mixed + lax.psum_scatter(
        mlp_part.astype(jnp.bfloat16), "tensor", scatter_dimension=0, tiled=True
    ).astype(jnp.float32)
    layer_out = (own_rows + mixed_rows + small_vecs[4] + small_vecs[5]).astype(jnp.bfloat16)
    cot_full = lax.all_gather(out_grad, "tensor", axis=0, tiled=True)
    full_qkv, full_dense, full_up, full_down = (
        lax.all_gather(qkv_weight, "dp", axis=0, tiled=True),
        lax.all_gather(dense_weight, "dp", axis=0, tiled=True),
        lax.all_gather(up_weight, "dp", axis=0, tiled=True),
        lax.all_gather(down_weight, "dp", axis=0, tiled=True),
    )
    down_grad = jnp.einsum("lf,ld->fd", active, cot_full, preferred_element_type=jnp.float32)
    dense_grad = jnp.einsum("le,ld->ed", context, cot_full, preferred_element_type=jnp.float32)
    active_grad = jnp.einsum("ld,fd->lf", cot_full, full_down, preferred_element_type=jnp.float32)
    hidden_grad = jax.vjp(gelu_exact, hidden)[1](active_grad)[0].astype(jnp.bfloat16)
    up_grad = jnp.einsum("ld,lf->df", mlp_full, hidden_grad, preferred_element_type=jnp.float32)
    up_bias_grad = jnp.sum(hidden_grad, axis=0, dtype=jnp.float32)
    mlp_in_grad = jnp.einsum("lf,df->ld", hidden_grad, full_up, preferred_element_type=jnp.float32)
    context_grad = jnp.einsum("ld,ed->le", cot_full, full_dense, preferred_element_type=jnp.float32)
    context_grad = context_grad.astype(jnp.bfloat16).reshape(length, local_heads, HD)

    def attend_back(carried, inputs):
        key_acc, value_acc = carried
        first_row, lse_block = inputs
        scores = block_scores(first_row, query_rows)
        prob_rows = jnp.exp(scores - lse_block[..., None])
        prob_low = prob_rows.astype(jnp.bfloat16)
        value_acc = value_acc + jnp.einsum(
            "hqk,qhe->khe", prob_low, context_grad, preferred_element_type=jnp.float32
        )
        prob_grad = jnp.einsum(
            "qhe,khe->hqk", context_grad, value_rows, preferred_element_type=jnp.float32
        )
        score_grad = prob_rows * (
            prob_grad - jnp.sum(prob_grad * prob_rows, axis=-1, keepdims=True)
        )
        score_grad = score_grad.astype(jnp.bfloat16)
        query_grad = (
            jnp.einsum("hqk,khe->qhe", score_grad, key_rows, preferred_element_type=jnp.float32)
            * score_scale
        )
        key_acc = (
            key_acc
            + jnp.einsum("hqk,qhe->khe", score_grad, query_rows, preferred_element_type=jnp.float32)
            * score_scale
        )
        return ((key_acc, value_acc), query_grad)

    zero_rows = jnp.zeros((length, local_heads, HD), jnp.float32)
    (key_grad, value_grad), query_blocks = lax.scan(
        attend_back, (zero_rows, zero_rows), (block_starts, lse_blocks)
    )
    query_grad = query_blocks.reshape(length, local_heads, HD)

    def turn(field_in):
        return rotate(field_in, cosine, sines)

    turn_back = jax.vjp(turn, zero_rows)[1]
    projected_grad = jnp.stack(
        [turn_back(query_grad)[0], turn_back(key_grad)[0], value_grad], axis=1
    )
    projected_grad = projected_grad.astype(jnp.bfloat16).reshape(length, 3 * head_cols)
    qkv_weight_grad = jnp.einsum(
        "ld,lc->dc", attn_full, projected_grad, preferred_element_type=jnp.float32
    )
    qkv_weight_grad = qkv_weight_grad.reshape(model_width, 3, head_cols)
    qkv_bias_grad = jnp.sum(projected_grad, axis=0, dtype=jnp.float32).reshape(3, head_cols)
    attn_in_grad = jnp.einsum(
        "lc,dc->ld",
        projected_grad,
        full_qkv.reshape(model_width, 3 * head_cols),
        preferred_element_type=jnp.float32,
    )
    reduced = (
        lax.psum_scatter(qkv_weight_grad, "dp", scatter_dimension=0, tiled=True),
        lax.psum_scatter(qkv_bias_grad, "dp", scatter_dimension=1, tiled=True),
        lax.psum_scatter(dense_grad, "dp", scatter_dimension=0, tiled=True),
        lax.psum_scatter(up_grad, "dp", scatter_dimension=0, tiled=True),
        lax.psum_scatter(up_bias_grad, "dp", scatter_dimension=0, tiled=True),
        lax.psum_scatter(down_grad, "dp", scatter_dimension=0, tiled=True),
    )
    attn_local, mlp_local = (
        lax.psum_scatter(
            attn_in_grad.astype(jnp.bfloat16), "tensor", scatter_dimension=0, tiled=True
        ).astype(jnp.float32),
        lax.psum_scatter(
            mlp_in_grad.astype(jnp.bfloat16), "tensor", scatter_dimension=0, tiled=True
        ).astype(jnp.float32),
    )
    pull_attn = jax.vjp(layer_norm, own_rows, small_vecs[0], small_vecs[1])[1]
    pull_mlp = jax.vjp(layer_norm, own_rows, small_vecs[2], small_vecs[3])[1]
    rows_grad_attn, gain_grad_attn, shift_grad_attn = pull_attn(attn_local)
    rows_grad_mlp, gain_grad_mlp, shift_grad_mlp = pull_mlp(mlp_local)
    cot_rows = out_grad.astype(jnp.float32)
    input_grad = (cot_rows + rows_grad_attn + rows_grad_mlp).astype(jnp.bfloat16)
    bias_total = jnp.sum(cot_rows, axis=0)
    small_sums = (
        lax.psum_scatter(gain_grad_attn, ("dp", "tensor"), scatter_dimension=0, tiled=True),
        lax.psum_scatter(shift_grad_attn, ("dp", "tensor"), scatter_dimension=0, tiled=True),
        lax.psum_scatter(gain_grad_mlp, ("dp", "tensor"), scatter_dimension=0, tiled=True),
        lax.psum_scatter(shift_grad_mlp, ("dp", "tensor"), scatter_dimension=0, tiled=True),
        lax.psum_scatter(bias_total, ("dp", "tensor"), scatter_dimension=0, tiled=True),
    )
    return (
        layer_out,
        input_grad,
        small_sums[0],
        small_sums[1],
        small_sums[2],
        small_sums[3],
        reduced[0],
        reduced[1],
        reduced[2],
        small_sums[4],
        reduced[3],
        reduced[4],
        reduced[5],
        small_sums[4],
    )


F32 = jnp.float32
BF16 = jnp.bfloat16
MESH_ID = pl.DeviceIdType.MESH
LINE = 4
SEQ = 256
WIDTH = 1024
HID = 512
PAIR = 128


def nn(a, b):
    return jnp.dot(a, b, preferred_element_type=F32)


def nt(a, b):
    return lax.dot_general(a, b, (((1,), (1,)), ((), ())), preferred_element_type=F32)


def tn(a, b):
    return lax.dot_general(a, b, (((0,), (0,)), ((), ())), preferred_element_type=F32)


def turn_tables():
    position = np.arange(SEQ, dtype=np.float64)[:, None]
    lane = np.arange(PAIR) % HD
    rates = 10000.0 ** (-(lane % (ROT // 2)) * (2.0 / ROT))
    angles = position * rates[None, :]
    cosine = np.where(lane < ROT, np.cos(angles), 1.0)
    toward = np.where(lane < ROT // 2, -np.sin(angles), 0.0)
    away = np.where((lane >= ROT // 2) & (lane < ROT), np.sin(angles), 0.0)
    return np.stack([cosine, toward, away]).astype(np.float32)


SEATS = (0, 3, 1, 2)


def seat_of(z):
    return (2 * z - z // 2) % LINE


def rows_of(index, count):
    return pl.ds(pl.multiple_of(index * count, count), count)


class Place:
    def __init__(self):
        index = lax.axis_index("dp")
        self.t = lax.axis_index("tensor")
        self.z = index // 4
        self.k = index % 4
        self.y = self.k // 2
        self.c = self.k % 2
        self.kc = self.y * 2 + 1 - self.c
        self.ky = (1 - self.y) * 2 + self.c
        self.kyc = (1 - self.y) * 2 + 1 - self.c
        self.q = self.k * 2 + self.t
        self.core = self.at(self.z, self.kc, self.t)
        self.cross = (
            self.at(self.z, self.k, 1 - self.t),
            self.at(self.z, self.ky, self.t),
            self.at(self.z, self.ky, 1 - self.t),
        )

    def at(self, z, k, t):
        return (z * 4 + k, t)

    def line(self, z):
        return self.at(z, self.k, self.t)


class Wires:
    def __init__(self, sends, arrivals):
        self.sends, self.arrivals = sends, arrivals
        self.sent, self.landed = 0, 0

    def take(self, sends, arrivals):
        first = (self.sent, self.landed)
        self.sent += sends
        self.landed += arrivals
        return first

    def copy(self, send, arrival, src, dst, device):
        return pltpu.make_async_remote_copy(
            src_ref=src,
            dst_ref=dst,
            send_sem=self.sends.at[send],
            recv_sem=self.arrivals.at[arrival],
            device_id=device,
            device_id_type=MESH_ID,
        )

    def all_sent(self, send, view, device):
        self.copy(send, 0, view, view, device).wait_send()

    def all_landed(self, arrival, view, device):
        self.copy(0, arrival, view, view, device).wait_recv()


class PlaneGather:
    def __init__(self, me, wires, src, slot, split, blocks):
        self.me, self.wires, self.src, self.slot = me, wires, src, slot
        self.blocks = blocks
        self.pieces = (pl.ds(0, split), pl.ds(split, src.shape[0] - split))
        self.send, self.arrivals = wires.take(1, 4)
        self.near_blocks = (
            me.k * 2 + 1 - me.t,
            me.ky * 2 + me.t,
            me.ky * 2 + 1 - me.t,
        )

    def start(self, which):
        device = (self.me.cross[0], self.me.cross[1], self.me.core)[which]
        arrival = self.arrivals + (0, 1, 3)[which]
        self.wires.copy(self.send, arrival, self.src, self.slot(self.me.q), device).start()

    def pass_on(self, which):
        part = self.slot(self.near_blocks[which])
        self.wires.copy(self.send, self.arrivals + 3, part, part, self.me.core).start()

    def forward(self, which):
        block = self.slot(self.near_blocks[which])
        self.wires.all_landed(self.arrivals + which, block, self.me.core)
        part = block.at[self.pieces[which]]
        device = self.me.cross[1 - which]
        self.wires.copy(self.send, self.arrivals + 2, part, part, device).start()
        self.pass_on(which)

    def corner(self):
        block = self.slot(self.near_blocks[2])
        self.wires.all_landed(self.arrivals + 2, block, self.me.core)
        self.pass_on(2)

    def finish(self):
        self.wires.all_landed(self.arrivals + 3, self.blocks(4), self.me.core)

    def drain(self):
        self.wires.all_sent(self.send, self.blocks(7), self.me.core)


class LineGather:
    def __init__(self, me, wires, view):
        self.me, self.wires, self.view = me, wires, view
        self.sends, self.arrivals = wires.take(2, 6)

    def copy(self, way, hop, block):
        z = self.me.z
        view = self.view(block, 1)
        device = self.me.line(z + 1 if way == 0 else z - 1)
        return self.wires.copy(self.sends + way, self.arrivals + way * 3 + hop, view, view, device)

    def send(self, way, hop):
        z = self.me.z
        has = (z >= hop) & (z < LINE - 1) if way == 0 else (z + hop < LINE) & (z > 0)

        @pl.when(has)
        def _():
            self.copy(way, hop, z - hop if way == 0 else z + hop).start()

    def arrive(self, way, hop):
        z = self.me.z

        @pl.when(z > hop if way == 0 else z + 1 + hop < LINE)
        def _():
            self.copy(way, hop, z - 1 - hop if way == 0 else z + 1 + hop).wait_recv()

    def start(self, way):
        @pl.when(self.me.z != (0 if way == 0 else LINE - 1))
        def _():
            self.send(way, 0)

    def outer(self):
        for way in range(2):

            @pl.when(self.me.z == (0 if way == 0 else LINE - 1))
            def _(way=way):
                self.send(way, 0)

    def relay(self, way, hop):
        self.arrive(way, hop - 1)
        self.send(way, hop)

    def finish(self, way):
        self.arrive(way, LINE - 2)

    def drain(self):
        z = self.me.z
        for way in range(2):
            for count in range(1, LINE):

                @pl.when(z == (count - 1 if way == 0 else LINE - count))
                def _():
                    self.wires.all_sent(self.sends + way, self.view(0, count), self.me.core)


class LineReduce:
    def __init__(self, me, wires, held, landed):
        self.me, self.wires, self.held, self.landed = me, wires, held, landed
        self.sends, self.arrivals = wires.take(2, 6)

    def copy(self, way, block):
        z = self.me.z
        device = self.me.line(z - 1 if way == 0 else z + 1)
        return self.wires.copy(
            self.sends + way,
            self.arrivals + way * (LINE - 2) + block,
            self.held.at[block],
            self.landed.at[way, block],
            device,
        )

    def join(self, way, block):
        self.copy(way, block).wait_recv()
        total = self.held[block].astype(F32) + self.landed[way, block].astype(F32)
        self.held[block] = total.astype(BF16)

    def each(self, way, slot, act):
        z = self.me.z
        steps = slot - (LINE - 1 - z if way == 0 else z)
        left = z if way == 0 else LINE - 1 - z
        block = steps if way == 0 else LINE - 1 - steps

        @pl.when((steps >= 0) & (steps < left))
        def _():
            act(block)

    def slot(self, way, slot):
        def act(block):
            if slot > 0:
                started = self.me.z < LINE - 1 if way == 0 else self.me.z > 0

                @pl.when(started)
                def _():
                    self.join(way, block)

            self.copy(way, block).start()

        self.each(way, slot, act)

    def finish(self, way):
        z = self.me.z

        @pl.when(z < LINE - 1 if way == 0 else z > 0)
        def _():
            self.join(way, z)

    def drain(self):
        z = self.me.z
        for way in range(2):
            for count in range(1, LINE):

                @pl.when(z == (count if way == 0 else LINE - 1 - count))
                def _():
                    view = self.held.at[pl.ds(0, count)]
                    self.wires.all_sent(self.sends + way, view, self.me.core)


class PlaneReduce:
    def __init__(self, me, wires, part, paired, crossed):
        self.me, self.wires = me, wires
        self.part, self.paired, self.crossed = part, paired, crossed
        self.send, self.arrivals = wires.take(1, 4)
        self.blocks = (me.ky * 2 + 1 - me.t, me.k * 2 + 1 - me.t, me.ky * 2 + me.t)

    def pair(self, y):
        rows = rows_of(y * 2 + 1 - self.me.c, SEQ)
        return self.wires.copy(
            self.send, self.arrivals, self.part.at[rows], self.paired.at[y], self.me.core
        )

    def rows(self, which, half):
        first = pl.multiple_of(self.blocks[which] * 128 + half * 64, 64)
        return pl.ds(first, 64)

    def cross(self, which, half):
        way = (half, 0, 1)[which]
        return self.wires.copy(
            self.send,
            self.arrivals + (1 + half if which == 0 else 3),
            self.part.at[self.rows(which, half)],
            self.crossed.at[which, pl.ds(half * 64, 64)],
            self.me.cross[way],
        )

    def middle(self):
        self.wires.all_landed(self.arrivals, self.part.at[pl.ds(0, 2 * SEQ)], self.me.core)
        for y in range(2):
            rows = rows_of(y * 2 + self.me.c, SEQ)
            total = self.part[rows].astype(F32) + self.paired[y].astype(F32)
            self.part[rows] = total.astype(BF16)
        for which, half in ((0, 0), (0, 1), (1, 0), (2, 1)):
            self.cross(which, half).start()

    def turn(self, half):
        self.cross(0, half).wait_recv()
        rows = self.rows(2 - half, half)
        total = self.part[rows].astype(F32) + self.crossed[0, pl.ds(half * 64, 64)].astype(F32)
        self.part[rows] = total.astype(BF16)
        self.cross(2 - half, half).start()

    def finish(self):
        self.wires.all_landed(self.arrivals + 3, self.part.at[pl.ds(0, SEQ)], self.me.core)
        total = self.part[rows_of(self.me.q, 128)].astype(F32)
        return total + self.crossed[1].astype(F32) + self.crossed[2].astype(F32)

    def drain(self):
        self.wires.all_sent(self.send, self.part.at[pl.ds(0, 896)], self.me.core)


def layer_kernel(
    x_hbm,
    g_hbm,
    qkv_hbm,
    dense_hbm,
    up_hbm,
    down_hbm,
    turn_hbm,
    attn_gain_ref,
    attn_shift_ref,
    mlp_gain_ref,
    mlp_shift_ref,
    dense_bias_ref,
    down_bias_ref,
    starts_ref,
    lengths_ref,
    qkv_bias_ref,
    up_bias_ref,
    layer_out_ref,
    input_grad_ref,
    qkv_grad_ref,
    dense_grad_ref,
    up_grad_ref,
    down_grad_ref,
    small_out_ref,
    turn_ref,
    x_all,
    g_all,
    small_line,
    small_all,
    qkv_w,
    dense_w,
    up_w,
    down_w,
    vec_ref,
    bias_ref,
    normed_a,
    normed_m,
    context_ref,
    turned_grad,
    active_ref,
    hidden_grad,
    slope_ref,
    part_out,
    part_attn,
    part_mlp,
    paired_ref,
    crossed_ref,
    up_held,
    up_landed,
    down_held,
    down_landed,
    qkv_held,
    qkv_landed,
    up_final,
    qkv_final,
    dense_line,
    dense_held,
    dense_mine,
    dense_landed,
    qkv_bias_held,
    qkv_bias_line,
    qkv_bias_final,
    up_bias_held,
    up_bias_final,
    sums_held,
    sums_chip,
    sums_total,
    sums_core,
    sums_cross,
    sums_line,
    sends,
    arrivals,
    local_sems,
):
    me = Place()
    wires = Wires(sends, arrivals)
    z, k, t = me.z, me.k, me.t

    barrier = pltpu.get_barrier_semaphore()

    def greet(device):
        pl.semaphore_signal(barrier, inc=1, device_id=device, device_id_type=MESH_ID)

    greet(me.core)
    greet(me.at(z, me.kyc, t))
    for device in me.cross:
        greet(device)
    for step in range(1, LINE):
        greet(me.line((z + step) % LINE))
    local_copies = []

    def local(src, dst):
        copy = pltpu.make_async_copy(src, dst, local_sems.at[len(local_copies)])
        local_copies.append(copy)
        copy.start()

    seat = pl.ds(pl.multiple_of(z * 256 + k * 64, 64), 64)
    peers = (me.kc, me.ky, me.kyc)
    devices = tuple(me.at(z, peer, t) for peer in peers)

    def three(arrival, view):
        wires.all_landed(arrival, view, me.core)

    local(dense_hbm, dense_line.at[z])
    for place, other in enumerate(SEATS):
        local(
            up_hbm.at[:, rows_of(other * 4 + k, 128)],
            up_w.at[seat, pl.ds(place * 128, 128)],
        )
    local(down_hbm, down_w.at[rows_of(seat_of(z), 128)])
    for which in range(3):
        local(
            qkv_hbm.at[which, :, rows_of(k, PAIR)],
            qkv_w.at[seat, pl.ds(which * PAIR, PAIR)],
        )
    local(x_hbm, x_all.at[rows_of(me.q, 128)])
    local(g_hbm, g_all.at[rows_of(me.q, 128)])
    local(turn_hbm, turn_ref)
    qkv_bias_held[...] = jnp.zeros_like(qkv_bias_held)
    up_bias_held[...] = jnp.zeros_like(up_bias_held)

    def side_by_side(*fields):
        return jnp.concatenate(
            [field.astype(F32).reshape(1, field.shape[-1]) for field in fields], axis=1
        )

    triple = qkv_bias_ref[...]
    blank = jnp.zeros((1, 60), F32)
    small_line[z] = jnp.concatenate(
        [
            side_by_side(
                attn_gain_ref[...], attn_shift_ref[...], mlp_gain_ref[...], mlp_shift_ref[...]
            ),
            side_by_side(
                dense_bias_ref[...], down_bias_ref[...], starts_ref[...], lengths_ref[...], blank
            ),
            side_by_side(triple[0:1], triple[1:2], triple[2:3], blank[:, :32]),
            side_by_side(up_bias_ref[...]),
            jnp.zeros((4, 128), F32),
        ],
        axis=0,
    )
    pl.semaphore_wait(barrier, 8)

    up_send, up_arrival = wires.take(1, 2)
    for place, other in enumerate(SEATS):
        for which in range(3):
            wires.copy(
                up_send,
                up_arrival + place // 2,
                up_hbm.at[:, rows_of(other * 4 + peers[which], 128)],
                up_w.at[seat, pl.ds(place * 128, 128)],
                devices[which],
            ).start()

    qkv_sends, qkv_arrival = wires.take(1, 1)

    def rows_slot(ref):
        return (lambda block: ref.at[rows_of(block, 128)]), (
            lambda count: ref.at[pl.ds(0, count * 128)]
        )

    slot, blocks = rows_slot(x_all)
    gather_x = PlaneGather(me, wires, x_hbm, slot, 48, blocks)
    for which in range(3):
        gather_x.start(which)
    slot, blocks = rows_slot(g_all)
    gather_g = PlaneGather(me, wires, g_hbm, slot, 48, blocks)
    gather_small = PlaneGather(
        me,
        wires,
        small_line,
        lambda block: small_all.at[block],
        2,
        lambda count: small_all.at[pl.ds(0, count)],
    )
    small_send, small_arrival = wires.take(1, 1)
    for step in range(1, LINE):
        wires.copy(
            small_send,
            small_arrival,
            small_line.at[z],
            small_line.at[z],
            me.line((z + step) % LINE),
        ).start()

    def line_gather(ref, count):
        return LineGather(
            me, wires, lambda s, n: ref.at[pl.ds(pl.multiple_of(s * count, count), n * count)]
        )

    line_dense = LineGather(me, wires, lambda s, n: dense_line.at[pl.ds(s, n)])
    line_qkv = line_gather(qkv_w, 256)
    line_upa, line_upb = (
        LineGather(
            me,
            wires,
            lambda s, n, first=first: up_w.at[
                pl.ds(pl.multiple_of(s * 256, 256), n * 256), pl.ds(first, 256)
            ],
        )
        for first in (0, 256)
    )
    line_down = LineGather(
        me,
        wires,
        lambda s, n: down_w.at[pl.ds(pl.multiple_of(seat_of(s) * 128, 128), n * 128)],
    )
    reduce_down = LineReduce(
        me, wires, down_held, down_landed
    )
    reduce_up = LineReduce(
        me, wires, up_held, up_landed
    )
    reduce_qkv = LineReduce(
        me, wires, qkv_held, qkv_landed
    )
    reduce_dense = LineReduce(
        me, wires, dense_mine, dense_landed
    )
    reduce_attn = PlaneReduce(me, wires, part_attn, paired_ref.at[0], crossed_ref.at[0])
    reduce_out = PlaneReduce(me, wires, part_out, paired_ref.at[1], crossed_ref.at[1])
    reduce_mlp = PlaneReduce(me, wires, part_mlp, paired_ref.at[2], crossed_ref.at[2])

    local_copies[0].wait()
    line_dense.outer()
    line_dense.start(0)
    line_dense.start(1)

    own_small = pltpu.make_async_copy(
        small_line, small_all.at[me.q], local_sems.at[len(local_copies)]
    )
    own_dense = pltpu.make_async_copy(
        dense_line.at[k], dense_w.at[rows_of(k, 32)], local_sems.at[len(local_copies) + 1]
    )
    dense_sends, dense_arrival = wires.take(1, 1)
    back_sends, back_arrival = wires.take(2, 2)
    bias_sends, bias_arrival = wires.take(2, 2)
    out_sends, out_arrival = wires.take(2, 2)
    sums_sends, sums_arrival = wires.take(3, 3)

    def along(send, arrival, source, target):
        for step in range(1, LINE):
            there = (z + step) % LINE
            wires.copy(send, arrival, source(there), target, me.line(there)).start()

    def around(send, arrival, source, target):
        for which in range(3):
            wires.copy(send, arrival, source(peers[which]), target, devices[which]).start()

    def norm_rows(rows):
        values = x_all[rows].astype(F32)
        centred = values - jnp.mean(values, axis=-1, keepdims=True)
        rate = lax.rsqrt(jnp.mean(centred * centred, axis=-1, keepdims=True) + NORM_EPS)
        return centred * rate, rate

    def norm_block(block, carry):
        rows = rows_of(block, 128)
        unit, _ = norm_rows(rows)
        normed_m[rows] = (unit * vec_ref[2:3, :] + vec_ref[3:4, :]).astype(BF16)
        return carry

    def attn_norm(block, carry):
        rows = rows_of(block, 128)
        unit, _ = norm_rows(rows)
        normed_a[rows] = (unit * vec_ref[0:1, :] + vec_ref[1:2, :]).astype(BF16)
        return carry

    def activate(half):
        columns = slice(half * 256, (half + 1) * 256)

        def tile_of(tile, carry):
            rows = rows_of(tile, 256)
            up_bias = jnp.concatenate(
                [small_all[me.q, s, 3:4, :] for s in SEATS[half * 2 : half * 2 + 2]], axis=1
            )
            hidden = nn(normed_m[rows], up_w[:, columns]) + up_bias
            share = (1.0 + lax.erf(hidden * 0.5**0.5)) * 0.5
            bell = jnp.exp(hidden * hidden * -0.5) * (2.0 * np.pi) ** -0.5
            slope_ref[rows, columns] = share + hidden * bell
            active_ref[rows, columns] = (hidden * share).astype(BF16)
            return carry

        return tile_of

    activate_a, activate_b = activate(0), activate(1)

    def down_block(block, carry):
        units = rows_of(seat_of(block), 128)
        down_held[block] = tn(active_ref[:, units], g_all[...]).astype(BF16)
        return carry

    def feed_back(tile, carry):
        rows = rows_of(tile, 256)
        grad = (nt(g_all[rows], down_w[...]) * slope_ref[rows]).astype(BF16)
        hidden_grad[rows] = grad
        up_bias_held[0:1, :] += jnp.sum(grad.astype(F32), axis=0, keepdims=True)
        return carry

    def feed_in(tile, carry):
        rows = rows_of(tile, 256)
        part_mlp[rows] = nt(hidden_grad[rows], up_w[...]).astype(BF16)
        return carry

    def up_block(block, carry):
        up_held[block] = tn(normed_m[:, rows_of(block, 256)], hidden_grad[...]).astype(BF16)
        return carry

    scale = HD**-0.5

    def attend(seq, carry):
        rows = rows_of(seq, SEQ)
        cosine, toward, away = turn_ref[0], turn_ref[1], turn_ref[2]
        projected = nn(normed_a[rows], qkv_w[...]) + bias_ref[0:1, :]

        def project(which):
            return projected[:, which * PAIR : (which + 1) * PAIR]

        def turned(field):
            return (
                field * cosine
                + pltpu.roll(field, ROT // 2, 1) * away
                + pltpu.roll(field, PAIR - ROT // 2, 1) * toward
            )

        def turned_back(field):
            return (
                field * cosine
                - pltpu.roll(field, ROT // 2, 1) * away
                - pltpu.roll(field, PAIR - ROT // 2, 1) * toward
            )

        query = turned(project(0)).astype(BF16)
        key = turned(project(1)).astype(BF16)
        value = project(2).astype(BF16)
        context_grad = nt(g_all[rows], dense_w[...]).astype(BF16)

        spans = small_all[seq * 2, z, 1:2, :]
        down_pos = lax.broadcasted_iota(jnp.int32, (SEQ, 1), 0).astype(F32)
        over_pos = lax.broadcasted_iota(jnp.int32, (1, SEQ), 1).astype(F32)

        def labels(place):
            total = jnp.zeros(place.shape, F32)
            for span in range(2):
                begin = spans[:, 64 + span : 65 + span]
                end = begin + spans[:, 66 + span : 67 + span]
                total = total + jnp.where((place >= begin) & (place < end), span + 1.0, 0.0)
            return total

        down_label, over_label = labels(down_pos), labels(over_pos)
        allowed = (over_pos <= down_pos) | ((down_label == over_label) & (down_label > 0.0))

        lane = lax.broadcasted_iota(jnp.int32, (SEQ, PAIR), 1)
        parts = []
        for head in range(2):
            mine = (lane >= HD) if head else (lane < HD)
            zero = jnp.zeros_like(query)
            scores = nt(jnp.where(mine, query, zero), key) * scale
            scores = jnp.where(allowed, scores, NEG_FILL)
            exponent = jnp.exp(scores - jnp.max(scores, axis=-1, keepdims=True))
            probs = exponent * (1.0 / jnp.sum(exponent, axis=-1, keepdims=True))
            low = probs.astype(BF16)
            prob_grad = nt(jnp.where(mine, context_grad, zero), value)
            inner = jnp.sum(prob_grad * probs, axis=-1, keepdims=True)
            score_grad = (probs * (prob_grad - inner)).astype(BF16)
            parts.append(
                (
                    nn(low, value),
                    tn(low, context_grad),
                    nn(score_grad, key) * scale,
                    tn(score_grad, query) * scale,
                )
            )
        context, value_grad, query_grad, key_grad = (
            jnp.where(lane < HD, first, second) for first, second in zip(*parts)
        )
        context_ref[rows] = context.astype(BF16)
        grads = (
            turned_back(query_grad).astype(BF16),
            turned_back(key_grad).astype(BF16),
            value_grad.astype(BF16),
        )
        for which in range(3):
            turned_grad[rows, which * PAIR : (which + 1) * PAIR] = grads[which]
            qkv_bias_held[which : which + 1, :] += jnp.sum(
                grads[which].astype(F32), axis=0, keepdims=True
            )
        return carry

    def attend_in(tile, carry):
        rows = rows_of(tile, 256)
        part_attn[rows] = nt(turned_grad[rows], qkv_w[...]).astype(BF16)
        return carry

    def qkv_block(block, carry):
        qkv_held[block] = tn(normed_a[:, rows_of(block, 256)], turned_grad[...]).astype(BF16)
        return carry

    def mix(tile, carry):
        rows = rows_of(tile, 256)
        mixed = nn(context_ref[rows], dense_w[...]) + nn(active_ref[rows], down_w[...])
        part_out[rows] = mixed.astype(BF16)
        return carry

    def locals_done():
        for copy in local_copies[1:]:
            copy.wait()

    def small_line_done():
        three(small_arrival, small_line.at[pl.ds(0, 3)])
        own_small.start()
        for which in range(3):
            gather_small.start(which)

    def upa_start():
        three(up_arrival, up_w.at[pl.ds(0, 96)])
        line_upa.outer()
        line_upa.start(0)
        line_upa.start(1)

    def upb_start():
        three(up_arrival + 1, up_w.at[pl.ds(0, 96)])
        line_upb.outer()
        line_upb.start(0)
        line_upb.start(1)

    def down_outer():
        line_down.outer()

    def qkv_send():
        for which in range(3):
            for part in range(3):
                wires.copy(
                    qkv_sends,
                    qkv_arrival,
                    qkv_hbm.at[part, :, rows_of(peers[which], PAIR)],
                    qkv_w.at[seat, pl.ds(part * PAIR, PAIR)],
                    devices[which],
                ).start()

    def qkv_outer():
        three(qkv_arrival, qkv_w.at[pl.ds(0, 192)])
        line_qkv.outer()

    def qkv_start():
        line_qkv.start(0)
        line_qkv.start(1)

    def down_start():
        line_down.start(0)
        line_down.start(1)

    def dense_send():
        around(
            dense_sends, dense_arrival, lambda to: dense_line.at[to], dense_w.at[rows_of(k, 32)]
        )
        own_dense.start()

    def dense_done():
        three(dense_arrival, dense_w.at[pl.ds(0, 96)])
        own_dense.wait()

    def spread_table(kind, width):
        table = small_all[...].reshape(256, 128).astype(BF16)
        line_id = lax.broadcasted_iota(jnp.int32, (256, width), 0)
        column = lax.broadcasted_iota(jnp.int32, (256, width), 1)
        from_z, from_q = (line_id >> 3) & 3, line_id >> 5
        if width == WIDTH:
            chosen = from_z * 8 + from_q == column >> 5
        else:
            chosen = (from_z == k) & (from_q == (column >> 5) * 2 + t)
        chosen = chosen & ((line_id & 7) == kind)
        spread = tn(table, jnp.where(chosen, 1.0, 0.0).astype(BF16))
        lane_row = lax.broadcasted_iota(jnp.int32, (128, width), 0)
        lane_col = lax.broadcasted_iota(jnp.int32, (128, width), 1) & 31

        def vector(which):
            picked = jnp.where(lane_row == lane_col + which * 32, spread, 0.0)
            return jnp.sum(picked, axis=0, keepdims=True)

        return vector

    def vectors():
        own_small.wait()
        vector = spread_table(0, WIDTH)
        for which in range(4):
            vec_ref[which : which + 1, :] = vector(which)

    def more_vectors():
        vector = spread_table(1, WIDTH)
        for which in range(2):
            vec_ref[4 + which : 5 + which, :] = vector(which)
        vector = spread_table(2, PAIR)
        for which in range(3):
            bias_ref[0:1, which * PAIR : (which + 1) * PAIR] = vector(which)

    def up_bias_send():
        along(
            bias_sends,
            bias_arrival,
            lambda there: up_bias_held.at[:, rows_of(seat_of(there), 128)],
            up_bias_final.at[z],
        )
        up_bias_final[z] = up_bias_held[:, rows_of(seat_of(z), 128)]

    def dense_part():
        dense_held[...] = tn(context_ref[...], g_all[...]).astype(BF16)
        around(
            back_sends, back_arrival, lambda to: dense_held.at[rows_of(to, 32)], dense_mine.at[k]
        )
        around(back_sends + 1, back_arrival + 1, lambda to: qkv_bias_held, qkv_bias_line.at[k])
        dense_mine[k] = dense_held[rows_of(k, 32)]
        qkv_bias_line[k] = qkv_bias_held[...]

    def dense_back():
        three(back_arrival, dense_mine.at[pl.ds(0, 3)])
        three(back_arrival + 1, qkv_bias_line.at[pl.ds(0, 3)])
        along(
            bias_sends + 1,
            bias_arrival + 1,
            lambda there: qkv_bias_line.at[there],
            qkv_bias_final.at[z],
        )
        qkv_bias_final[z] = qkv_bias_line[z]

    def up_out():
        around(
            out_sends, out_arrival, lambda to: up_held.at[z, rows_of(to, 64)], up_final.at[k]
        )
        up_final[k] = up_held[z, rows_of(k, 64)]

    def qkv_out():
        around(
            out_sends + 1,
            out_arrival + 1,
            lambda to: qkv_held.at[z, rows_of(to, 64)],
            qkv_final.at[k],
        )
        qkv_final[k] = qkv_held[z, rows_of(k, 64)]

    def down_out():
        down_grad_ref[...] = down_held[z]

    def dense_out():
        dense_grad_ref[...] = dense_mine[z]

    def up_result():
        three(out_arrival, up_final.at[pl.ds(0, 3)])
        up_grad_ref[...] = up_final[...]

    def qkv_result():
        three(out_arrival + 1, qkv_final.at[pl.ds(0, 3)])
        qkv_grad_ref[...] = qkv_final[...]

    own = rows_of(me.q, 128)
    def layer_out():
        mixed = reduce_out.finish()
        layer_out_ref[...] = (
            x_all[own].astype(F32) + mixed + vec_ref[4:5, :] + vec_ref[5:6, :]
        ).astype(BF16)

    def norm_grads():
        from_attn = reduce_attn.finish()
        from_mlp = reduce_mlp.finish()
        cotangent = g_all[own].astype(F32)
        unit, rate = norm_rows(own)
        sums_held[...] = jnp.zeros_like(sums_held)
        for which, field in enumerate(
            (from_attn * unit, from_attn, from_mlp * unit, from_mlp, cotangent)
        ):
            sums_held[which : which + 1, :] = jnp.sum(field, axis=0, keepdims=True)
        wires.copy(sums_sends, sums_arrival, sums_held, sums_core, me.core).start()
        pulled = from_attn * vec_ref[0:1, :] + from_mlp * vec_ref[2:3, :]
        pulled = (
            pulled
            - jnp.mean(pulled, axis=-1, keepdims=True)
            - unit * jnp.mean(pulled * unit, axis=-1, keepdims=True)
        )
        input_grad_ref[...] = (cotangent + rate * pulled).astype(BF16)

    def sums_plane():
        three(sums_arrival, sums_core)
        sums_chip[...] = sums_held[...] + sums_core[...]
        for which in range(3):
            wires.copy(
                sums_sends + 1,
                sums_arrival + 1,
                sums_chip,
                sums_cross.at[which],
                me.cross[which],
            ).start()

    def sums_send():
        three(sums_arrival + 1, sums_cross)
        sums_total[...] = sums_chip[...] + sums_cross[0] + sums_cross[1] + sums_cross[2]
        along(
            sums_sends + 2,
            sums_arrival + 2,
            lambda there: sums_total.at[:, rows_of(there, 256)],
            sums_line.at[z],
        )
        sums_line[z] = sums_total[:, rows_of(z, 256)]

    def small_result():
        three(sums_arrival + 2, sums_line.at[pl.ds(0, 3)])
        three(bias_arrival, up_bias_final.at[pl.ds(0, 3)])
        three(bias_arrival + 1, qkv_bias_final.at[pl.ds(0, 3)])
        sums = sums_line[0] + sums_line[1] + sums_line[2] + sums_line[3]
        sums = jnp.where(k >= 2, sums[:, 128:], sums[:, :128])
        small_out_ref[0:8, :] = pltpu.roll(sums, (128 - (me.q % 4) * 32) % 128, 1)
        bias_sum = qkv_bias_final[0] + qkv_bias_final[1] + qkv_bias_final[2] + qkv_bias_final[3]
        small_out_ref[8:16, :] = pltpu.roll(bias_sum, (128 - k * 32) % 128, 1)
        small_out_ref[16:24, :] = (
            up_bias_final[0] + up_bias_final[1] + up_bias_final[2] + up_bias_final[3]
        )

    def ends_of(body):
        def outer(index, carry):
            return body(index * (LINE - 1), carry)

        return outer

    locals_done()
    upa_start()
    upb_start()
    small_line_done()
    qkv_send()
    line_dense.relay(0, 1)
    line_upa.relay(1, 1)
    gather_g.start(0)
    line_upa.relay(0, 1)
    gather_g.start(1)
    gather_x.forward(0)
    line_dense.relay(1, 1)
    gather_g.start(2)
    line_upb.relay(1, 1)
    gather_x.forward(1)
    qkv_outer()
    qkv_start()
    line_upb.relay(0, 1)
    line_upb.relay(1, 2)
    gather_small.forward(1)
    down_outer()
    line_dense.relay(1, 2)
    gather_small.forward(0)
    line_upa.relay(0, 2)
    line_upa.relay(1, 2)
    gather_x.corner()
    gather_g.forward(1)
    line_upb.finish(1)
    gather_g.forward(0)
    line_dense.finish(1)
    gather_small.corner()
    line_dense.relay(0, 2)
    gather_small.finish()
    gather_x.finish()
    line_qkv.relay(1, 1)
    line_qkv.relay(0, 1)
    line_upb.relay(0, 2)
    line_upa.finish(0)
    vectors()
    lax.fori_loop(4, 8, norm_block, 0)
    gather_g.corner()
    line_dense.finish(0)
    line_upa.finish(1)
    dense_send()
    gather_g.finish()
    lax.fori_loop(0, 4, norm_block, 0)
    lax.fori_loop(0, 4, attn_norm, 0)
    lax.fori_loop(4, 8, attn_norm, 0)
    more_vectors()
    lax.fori_loop(0, 4, activate_a, 0)
    line_qkv.relay(0, 2)
    lax.fori_loop(0, 2, ends_of(down_block), 0)
    line_qkv.relay(1, 2)
    reduce_down.slot(0, 0)
    line_upb.finish(0)
    down_start()
    reduce_down.slot(1, 0)
    dense_done()
    lax.fori_loop(0, 4, activate_b, 0)
    lax.fori_loop(1, 3, down_block, 0)
    line_qkv.finish(1)
    line_qkv.finish(0)
    lax.fori_loop(0, 1, attend, 0)
    lax.fori_loop(1, 2, attend, 0)
    lax.fori_loop(3, 4, attend, 0)
    line_down.relay(1, 1)
    line_down.relay(0, 1)
    reduce_down.slot(0, 1)
    reduce_down.slot(1, 1)
    lax.fori_loop(2, 3, attend, 0)
    lax.fori_loop(0, 2, attend_in, 0)
    lax.fori_loop(2, 4, attend_in, 0)
    lax.fori_loop(0, 2, ends_of(qkv_block), 0)
    reduce_attn.pair(0).start()
    reduce_attn.pair(1).start()
    reduce_qkv.slot(0, 0)
    line_down.relay(1, 2)
    reduce_qkv.slot(1, 0)
    line_down.relay(0, 2)
    reduce_attn.middle()
    reduce_down.slot(0, 2)
    reduce_down.slot(1, 2)
    dense_part()
    line_down.finish(1)
    line_down.finish(0)
    lax.fori_loop(2, 4, feed_back, 0)
    lax.fori_loop(2, 4, feed_in, 0)
    lax.fori_loop(0, 2, feed_back, 0)
    reduce_mlp.pair(1).start()
    lax.fori_loop(0, 2, ends_of(up_block), 0)
    reduce_up.slot(1, 0)
    reduce_up.slot(0, 0)
    lax.fori_loop(0, 2, feed_in, 0)
    lax.fori_loop(1, 3, qkv_block, 0)
    lax.fori_loop(2, 4, mix, 0)
    reduce_qkv.slot(1, 1)
    reduce_qkv.slot(0, 1)
    reduce_mlp.pair(0).start()
    dense_back()
    reduce_mlp.middle()
    lax.fori_loop(1, 3, up_block, 0)
    reduce_up.slot(0, 1)
    reduce_attn.turn(1)
    lax.fori_loop(0, 2, mix, 0)
    reduce_dense.slot(0, 0)
    reduce_up.slot(1, 1)
    reduce_mlp.turn(1)
    reduce_attn.turn(0)
    reduce_out.pair(1).start()
    reduce_mlp.turn(0)
    reduce_out.pair(0).start()
    reduce_qkv.slot(1, 2)
    reduce_out.middle()
    reduce_qkv.slot(0, 2)
    reduce_dense.slot(1, 0)
    reduce_up.slot(1, 2)
    reduce_up.slot(0, 2)
    reduce_dense.slot(0, 1)
    norm_grads()
    reduce_down.finish(1)
    sums_plane()
    reduce_down.finish(0)
    reduce_qkv.finish(1)
    reduce_qkv.finish(0)
    up_bias_send()
    reduce_out.turn(0)
    reduce_dense.slot(1, 1)
    reduce_out.turn(1)
    qkv_out()
    sums_send()
    reduce_up.finish(0)
    reduce_up.finish(1)
    up_out()
    reduce_dense.slot(0, 2)
    down_out()
    reduce_dense.slot(1, 2)
    small_result()
    qkv_result()
    layer_out()
    reduce_dense.finish(0)
    reduce_dense.finish(1)
    up_result()
    dense_out()

    for send, view in (
        (up_send, up_w.at[pl.ds(0, 192)]),
        (qkv_sends, qkv_w.at[pl.ds(0, 192)]),
        (small_send, small_line.at[pl.ds(0, 3)]),
        (dense_sends, dense_w.at[pl.ds(0, 96)]),
        (back_sends, dense_mine.at[pl.ds(0, 3)]),
        (back_sends + 1, qkv_bias_line.at[pl.ds(0, 3)]),
        (bias_sends, up_bias_final.at[pl.ds(0, 3)]),
        (bias_sends + 1, qkv_bias_final.at[pl.ds(0, 3)]),
        (out_sends, up_final.at[pl.ds(0, 3)]),
        (out_sends + 1, qkv_final.at[pl.ds(0, 3)]),
        (sums_sends, sums_core),
        (sums_sends + 1, sums_cross),
        (sums_sends + 2, sums_line.at[pl.ds(0, 3)]),
    ):
        wires.all_sent(send, view, me.core)
    for item in (
        gather_x,
        gather_g,
        gather_small,
        line_dense,
        line_qkv,
        line_upa,
        line_upb,
        line_down,
        reduce_attn,
        reduce_out,
        reduce_mlp,
        reduce_qkv,
        reduce_dense,
        reduce_down,
        reduce_up,
    ):
        item.drain()


def final_kernel(
    layer_out_ref,
    input_grad_ref,
    qkv_ref,
    dense_ref,
    up_ref,
    down_ref,
    small_ref,
    layer_out,
    input_grad,
    attn_gain_grad,
    attn_shift_grad,
    mlp_gain_grad,
    mlp_shift_grad,
    qkv_grad,
    qkv_bias_grad,
    dense_grad,
    dense_bias_grad,
    up_grad,
    up_bias_grad,
    down_grad,
    down_bias_grad,
):
    layer_out[...] = layer_out_ref[...]
    input_grad[...] = input_grad_ref[...]
    for row, out in enumerate((attn_gain_grad, attn_shift_grad, mlp_gain_grad, mlp_shift_grad)):
        out[...] = small_ref[row, :32]
    dense_bias_grad[...] = small_ref[4, :32]
    down_bias_grad[...] = small_ref[4, :32]
    qkv_bias_grad[...] = small_ref[8:11, :32]
    up_bias_grad[...] = small_ref[16, :]
    for origin in range(4):
        for which in range(3):
            qkv_grad[which, :, origin * PAIR : (origin + 1) * PAIR] = qkv_ref[
                origin, :, which * PAIR : (which + 1) * PAIR
            ].astype(F32)
        for place, other in enumerate(SEATS):
            first = (other * 4 + origin) * 128
            up_grad[:, first : first + 128] = up_ref[
                origin, :, place * 128 : (place + 1) * 128
            ].astype(F32)
    dense_grad[...] = dense_ref[...].astype(F32)
    down_grad[...] = down_ref[...].astype(F32)


def plane_layer(
    hidden_in,
    out_grad,
    span_start,
    span_length,
    attn_gain,
    attn_shift,
    mlp_gain,
    mlp_shift,
    qkv_weight,
    qkv_bias,
    dense_weight,
    dense_bias,
    up_weight,
    up_bias,
    down_weight,
    down_bias,
):
    vmem = pl.BlockSpec(memory_space=pltpu.VMEM)
    anywhere = pl.BlockSpec(memory_space=pl.ANY)
    tokens = 4 * SEQ
    outs = pl.pallas_call(
        layer_kernel,
        out_shape=(
            jax.ShapeDtypeStruct((128, WIDTH), BF16),
            jax.ShapeDtypeStruct((128, WIDTH), BF16),
            jax.ShapeDtypeStruct((4, 64, 3 * PAIR), BF16),
            jax.ShapeDtypeStruct((32, WIDTH), BF16),
            jax.ShapeDtypeStruct((4, 64, HID), BF16),
            jax.ShapeDtypeStruct((128, WIDTH), BF16),
            jax.ShapeDtypeStruct((24, 128), F32),
        ),
        in_specs=[anywhere] * 7 + [vmem] * 10,
        out_specs=(vmem,) * 7,
        scratch_shapes=[
            pltpu.VMEM((3, SEQ, PAIR), F32),
            pltpu.VMEM((tokens, WIDTH), BF16),
            pltpu.VMEM((tokens, WIDTH), BF16),
            pltpu.VMEM((LINE, 8, 128), F32),
            pltpu.VMEM((8, LINE, 8, 128), F32),
            pltpu.VMEM((WIDTH, 3 * PAIR), BF16),
            pltpu.VMEM((PAIR, WIDTH), BF16),
            pltpu.VMEM((WIDTH, HID), BF16),
            pltpu.VMEM((HID, WIDTH), BF16),
            pltpu.VMEM((8, WIDTH), F32),
            pltpu.VMEM((8, 3 * PAIR), F32),
            pltpu.VMEM((tokens, WIDTH), BF16),
            pltpu.VMEM((tokens, WIDTH), BF16),
            pltpu.VMEM((tokens, PAIR), BF16),
            pltpu.VMEM((tokens, 3 * PAIR), BF16),
            pltpu.VMEM((tokens, HID), BF16),
            pltpu.VMEM((tokens, HID), BF16),
            pltpu.VMEM((tokens, HID), F32),
            pltpu.VMEM((tokens, WIDTH), BF16),
            pltpu.VMEM((tokens, WIDTH), BF16),
            pltpu.VMEM((tokens, WIDTH), BF16),
            pltpu.VMEM((3, 2, SEQ, WIDTH), BF16),
            pltpu.VMEM((3, 3, 128, WIDTH), BF16),
            pltpu.VMEM((LINE, 256, HID), BF16),
            pltpu.VMEM((2, LINE, 256, HID), BF16),
            pltpu.VMEM((LINE, 128, WIDTH), BF16),
            pltpu.VMEM((2, LINE, 128, WIDTH), BF16),
            pltpu.VMEM((LINE, 256, 3 * PAIR), BF16),
            pltpu.VMEM((2, LINE, 256, 3 * PAIR), BF16),
            pltpu.VMEM((4, 64, HID), BF16),
            pltpu.VMEM((4, 64, 3 * PAIR), BF16),
            pltpu.VMEM((LINE, 32, WIDTH), BF16),
            pltpu.VMEM((PAIR, WIDTH), BF16),
            pltpu.VMEM((LINE, 32, WIDTH), BF16),
            pltpu.VMEM((2, LINE, 32, WIDTH), BF16),
            pltpu.VMEM((8, PAIR), F32),
            pltpu.VMEM((4, 8, PAIR), F32),
            pltpu.VMEM((LINE, 8, PAIR), F32),
            pltpu.VMEM((8, HID), F32),
            pltpu.VMEM((LINE, 8, 128), F32),
            pltpu.VMEM((8, WIDTH), F32),
            pltpu.VMEM((8, WIDTH), F32),
            pltpu.VMEM((8, WIDTH), F32),
            pltpu.VMEM((8, WIDTH), F32),
            pltpu.VMEM((3, 8, WIDTH), F32),
            pltpu.VMEM((LINE, 8, 256), F32),
            pltpu.SemaphoreType.DMA((37,)),
            pltpu.SemaphoreType.DMA((92,)),
            pltpu.SemaphoreType.DMA((14,)),
        ],
        compiler_params=pltpu.CompilerParams(
            collective_id=0, has_side_effects=True, vmem_limit_bytes=60 * 2**20
        ),
    )(
        hidden_in,
        out_grad,
        jnp.transpose(qkv_weight, (1, 0, 2)),
        dense_weight,
        up_weight,
        down_weight,
        jnp.asarray(turn_tables()),
        attn_gain,
        attn_shift,
        mlp_gain,
        mlp_shift,
        dense_bias,
        down_bias,
        span_start,
        span_length,
        qkv_bias,
        up_bias,
    )
    wide = jax.ShapeDtypeStruct((32,), F32)
    finals = pl.pallas_call(
        final_kernel,
        out_shape=(
            jax.ShapeDtypeStruct((128, WIDTH), BF16),
            jax.ShapeDtypeStruct((128, WIDTH), BF16),
            wide,
            wide,
            wide,
            wide,
            jax.ShapeDtypeStruct((3, 64, 512), F32),
            jax.ShapeDtypeStruct((3, 32), F32),
            jax.ShapeDtypeStruct((32, WIDTH), F32),
            wide,
            jax.ShapeDtypeStruct((64, 2048), F32),
            jax.ShapeDtypeStruct((128,), F32),
            jax.ShapeDtypeStruct((128, WIDTH), F32),
            wide,
        ),
        in_specs=[vmem] * 7,
        out_specs=(vmem,) * 14,
    )(*outs)
    return (*finals[:6], jnp.transpose(finals[6], (1, 0, 2)), *finals[7:])


def solution(mesh):
    in_specs = (
        P(("dp", "tensor"), None),
        P(("dp", "tensor"), None),
        P("dp", None),
        P("dp", None),
        P(("dp", "tensor")),
        P(("dp", "tensor")),
        P(("dp", "tensor")),
        P(("dp", "tensor")),
        P("dp", None, "tensor"),
        P(None, ("tensor", "dp")),
        P(("tensor", "dp"), None),
        P(("dp", "tensor")),
        P("dp", "tensor"),
        P(("tensor", "dp")),
        P(("tensor", "dp"), None),
        P(("dp", "tensor")),
    )
    out_specs = (
        P(("dp", "tensor"), None),
        P(("dp", "tensor"), None),
        P(("dp", "tensor")),
        P(("dp", "tensor")),
        P(("dp", "tensor")),
        P(("dp", "tensor")),
        P("dp", None, "tensor"),
        P(None, ("tensor", "dp")),
        P(("tensor", "dp"), None),
        P(("dp", "tensor")),
        P("dp", "tensor"),
        P(("tensor", "dp")),
        P(("tensor", "dp"), None),
        P(("dp", "tensor")),
    )
    fast = mesh.shape["dp"] == 16 and mesh.shape["tensor"] == 2
    return jax.shard_map(plane_layer if fast else shards, mesh=mesh, in_specs=in_specs, out_specs=out_specs, check_vma=False)
```

```python
import jax
import jax.numpy as jnp
import numpy as np
from jax import lax
from jax.experimental import pallas as pl
from jax.experimental.pallas import tpu as pltpu
from jax.sharding import PartitionSpec as P

HD = 64
ROT = 16


NORM_EPS = 1e-05
NEG_FILL = -1000000000.0


def layer_norm(rows_in, gain_vec, shift_vec):
    mean_row = jnp.mean(rows_in, axis=-1, keepdims=True)
    centred = rows_in - mean_row
    spread = jnp.mean(centred * centred, axis=-1, keepdims=True)
    return centred * lax.rsqrt(spread + NORM_EPS) * gain_vec + shift_vec


def rotary_tables(length):
    position = jnp.arange(length, dtype=jnp.float32)
    rates = 10000.0 ** (-jnp.arange(ROT // 2, dtype=jnp.float32) * (2.0 / ROT))
    angles = position[:, None] * rates[None, :]
    angles = jnp.concatenate([angles, angles], axis=-1)[:, None, :]
    return (jnp.cos(angles), jnp.sin(angles))


def rotate(field_in, cosine, sines):
    turned = field_in[..., :ROT]
    first_half = turned[..., : ROT // 2]
    second_half = turned[..., ROT // 2 :]
    swapped = jnp.concatenate([-second_half, first_half], axis=-1)
    return jnp.concatenate([turned * cosine + swapped * sines, field_in[..., ROT:]], axis=-1)


def gelu_exact(values_in):
    return jax.nn.gelu(values_in, approximate=False)


def shards(
    hidden_in,
    out_grad,
    span_start,
    span_length,
    attn_gain,
    attn_shift,
    mlp_gain,
    mlp_shift,
    qkv_weight,
    qkv_bias,
    dense_weight,
    dense_bias,
    up_weight,
    up_bias,
    down_weight,
    down_bias,
):
    local_rows = hidden_in.shape[0]
    length = local_rows * lax.axis_size("tensor")
    block_rows = min(512, length)
    block_count = length // block_rows
    score_scale = HD ** (-0.5)
    small_full = (
        lax.all_gather(attn_gain, ("dp", "tensor"), axis=0, tiled=True),
        lax.all_gather(attn_shift, ("dp", "tensor"), axis=0, tiled=True),
        lax.all_gather(mlp_gain, ("dp", "tensor"), axis=0, tiled=True),
        lax.all_gather(mlp_shift, ("dp", "tensor"), axis=0, tiled=True),
        lax.all_gather(dense_bias, ("dp", "tensor"), axis=0, tiled=True),
        lax.all_gather(down_bias, ("dp", "tensor"), axis=0, tiled=True),
    )
    small_vecs = [item.astype(jnp.float32) for item in small_full]
    own_rows = hidden_in.astype(jnp.float32)
    normed_attn = layer_norm(own_rows, small_vecs[0], small_vecs[1]).astype(jnp.bfloat16)
    normed_mlp = layer_norm(own_rows, small_vecs[2], small_vecs[3]).astype(jnp.bfloat16)
    attn_full, mlp_full = (
        lax.all_gather(normed_attn, "tensor", axis=0, tiled=True),
        lax.all_gather(normed_mlp, "tensor", axis=0, tiled=True),
    )
    full_qkv, full_qkv_bias, full_dense, full_up, full_up_bias, full_down = (
        lax.all_gather(qkv_weight, "dp", axis=0, tiled=True),
        lax.all_gather(qkv_bias, "dp", axis=1, tiled=True),
        lax.all_gather(dense_weight, "dp", axis=0, tiled=True),
        lax.all_gather(up_weight, "dp", axis=0, tiled=True),
        lax.all_gather(up_bias, "dp", axis=0, tiled=True),
        lax.all_gather(down_weight, "dp", axis=0, tiled=True),
    )
    model_width = full_qkv.shape[0]
    head_cols = full_qkv.shape[2]
    local_heads = head_cols // HD
    projected = jnp.dot(
        attn_full, full_qkv.reshape(model_width, 3 * head_cols), preferred_element_type=jnp.float32
    )
    projected = projected + full_qkv_bias.reshape(3 * head_cols).astype(jnp.float32)
    projected = projected.reshape(length, 3, local_heads, HD)
    cosine, sines = rotary_tables(length)
    query_rows = rotate(projected[:, 0], cosine, sines).astype(jnp.bfloat16)
    key_rows = rotate(projected[:, 1], cosine, sines).astype(jnp.bfloat16)
    value_rows = projected[:, 2].astype(jnp.bfloat16)
    position = jnp.arange(length, dtype=jnp.int32)
    starts_here = span_start[0]
    lengths_here = span_length[0]
    inside = (position[None, :] >= starts_here[:, None]) & (
        position[None, :] < (starts_here + lengths_here)[:, None]
    )
    marks = (jnp.arange(starts_here.shape[0], dtype=jnp.int32) + 1)[:, None]
    labels = jnp.sum(jnp.where(inside, marks, 0), axis=0)

    def block_scores(first_row, query_block):
        raw_scores = (
            jnp.einsum("qhe,khe->hqk", query_block, key_rows, preferred_element_type=jnp.float32)
            * score_scale
        )
        row_pos = first_row + jnp.arange(block_rows, dtype=jnp.int32)
        allowed = (position[None, :] <= row_pos[:, None]) | (labels[:, None] == labels[None, :]) & (
            labels[:, None] > 0
        )
        return jnp.where(allowed[None], raw_scores, NEG_FILL)

    def attend(first_row):
        scores = block_scores(first_row, query_rows)
        row_top = jnp.max(scores, axis=-1, keepdims=True)
        exponent = jnp.exp(scores - row_top)
        summed = jnp.sum(exponent, axis=-1, keepdims=True)
        prob_low = (exponent / summed).astype(jnp.bfloat16)
        context_block = jnp.einsum(
            "hqk,khe->qhe", prob_low, value_rows, preferred_element_type=jnp.float32
        )
        return (context_block.astype(jnp.bfloat16), (row_top + jnp.log(summed))[..., 0])

    block_starts = jnp.arange(block_count, dtype=jnp.int32) * block_rows
    context_blocks, lse_blocks = lax.map(attend, block_starts)
    context = context_blocks.reshape(length, head_cols)
    attn_part = jnp.dot(context, full_dense, preferred_element_type=jnp.float32)
    attn_mixed = lax.psum_scatter(
        attn_part.astype(jnp.bfloat16), "tensor", scatter_dimension=0, tiled=True
    ).astype(jnp.float32)
    hidden = jnp.dot(mlp_full, full_up, preferred_element_type=jnp.float32) + full_up_bias.astype(
        jnp.float32
    )
    active = gelu_exact(hidden).astype(jnp.bfloat16)
    mlp_part = jnp.dot(active, full_down, preferred_element_type=jnp.float32)
    mixed_rows = attn_mixed + lax.psum_scatter(
        mlp_part.astype(jnp.bfloat16), "tensor", scatter_dimension=0, tiled=True
    ).astype(jnp.float32)
    layer_out = (own_rows + mixed_rows + small_vecs[4] + small_vecs[5]).astype(jnp.bfloat16)
    cot_full = lax.all_gather(out_grad, "tensor", axis=0, tiled=True)
    full_qkv, full_dense, full_up, full_down = (
        lax.all_gather(qkv_weight, "dp", axis=0, tiled=True),
        lax.all_gather(dense_weight, "dp", axis=0, tiled=True),
        lax.all_gather(up_weight, "dp", axis=0, tiled=True),
        lax.all_gather(down_weight, "dp", axis=0, tiled=True),
    )
    down_grad = jnp.einsum("lf,ld->fd", active, cot_full, preferred_element_type=jnp.float32)
    dense_grad = jnp.einsum("le,ld->ed", context, cot_full, preferred_element_type=jnp.float32)
    active_grad = jnp.einsum("ld,fd->lf", cot_full, full_down, preferred_element_type=jnp.float32)
    hidden_grad = jax.vjp(gelu_exact, hidden)[1](active_grad)[0].astype(jnp.bfloat16)
    up_grad = jnp.einsum("ld,lf->df", mlp_full, hidden_grad, preferred_element_type=jnp.float32)
    up_bias_grad = jnp.sum(hidden_grad, axis=0, dtype=jnp.float32)
    mlp_in_grad = jnp.einsum("lf,df->ld", hidden_grad, full_up, preferred_element_type=jnp.float32)
    context_grad = jnp.einsum("ld,ed->le", cot_full, full_dense, preferred_element_type=jnp.float32)
    context_grad = context_grad.astype(jnp.bfloat16).reshape(length, local_heads, HD)

    def attend_back(carried, inputs):
        key_acc, value_acc = carried
        first_row, lse_block = inputs
        scores = block_scores(first_row, query_rows)
        prob_rows = jnp.exp(scores - lse_block[..., None])
        prob_low = prob_rows.astype(jnp.bfloat16)
        value_acc = value_acc + jnp.einsum(
            "hqk,qhe->khe", prob_low, context_grad, preferred_element_type=jnp.float32
        )
        prob_grad = jnp.einsum(
            "qhe,khe->hqk", context_grad, value_rows, preferred_element_type=jnp.float32
        )
        score_grad = prob_rows * (
            prob_grad - jnp.sum(prob_grad * prob_rows, axis=-1, keepdims=True)
        )
        score_grad = score_grad.astype(jnp.bfloat16)
        query_grad = (
            jnp.einsum("hqk,khe->qhe", score_grad, key_rows, preferred_element_type=jnp.float32)
            * score_scale
        )
        key_acc = (
            key_acc
            + jnp.einsum("hqk,qhe->khe", score_grad, query_rows, preferred_element_type=jnp.float32)
            * score_scale
        )
        return ((key_acc, value_acc), query_grad)

    zero_rows = jnp.zeros((length, local_heads, HD), jnp.float32)
    (key_grad, value_grad), query_blocks = lax.scan(
        attend_back, (zero_rows, zero_rows), (block_starts, lse_blocks)
    )
    query_grad = query_blocks.reshape(length, local_heads, HD)

    def turn(field_in):
        return rotate(field_in, cosine, sines)

    turn_back = jax.vjp(turn, zero_rows)[1]
    projected_grad = jnp.stack(
        [turn_back(query_grad)[0], turn_back(key_grad)[0], value_grad], axis=1
    )
    projected_grad = projected_grad.astype(jnp.bfloat16).reshape(length, 3 * head_cols)
    qkv_weight_grad = jnp.einsum(
        "ld,lc->dc", attn_full, projected_grad, preferred_element_type=jnp.float32
    )
    qkv_weight_grad = qkv_weight_grad.reshape(model_width, 3, head_cols)
    qkv_bias_grad = jnp.sum(projected_grad, axis=0, dtype=jnp.float32).reshape(3, head_cols)
    attn_in_grad = jnp.einsum(
        "lc,dc->ld",
        projected_grad,
        full_qkv.reshape(model_width, 3 * head_cols),
        preferred_element_type=jnp.float32,
    )
    reduced = (
        lax.psum_scatter(qkv_weight_grad, "dp", scatter_dimension=0, tiled=True),
        lax.psum_scatter(qkv_bias_grad, "dp", scatter_dimension=1, tiled=True),
        lax.psum_scatter(dense_grad, "dp", scatter_dimension=0, tiled=True),
        lax.psum_scatter(up_grad, "dp", scatter_dimension=0, tiled=True),
        lax.psum_scatter(up_bias_grad, "dp", scatter_dimension=0, tiled=True),
        lax.psum_scatter(down_grad, "dp", scatter_dimension=0, tiled=True),
    )
    attn_local, mlp_local = (
        lax.psum_scatter(
            attn_in_grad.astype(jnp.bfloat16), "tensor", scatter_dimension=0, tiled=True
        ).astype(jnp.float32),
        lax.psum_scatter(
            mlp_in_grad.astype(jnp.bfloat16), "tensor", scatter_dimension=0, tiled=True
        ).astype(jnp.float32),
    )
    pull_attn = jax.vjp(layer_norm, own_rows, small_vecs[0], small_vecs[1])[1]
    pull_mlp = jax.vjp(layer_norm, own_rows, small_vecs[2], small_vecs[3])[1]
    rows_grad_attn, gain_grad_attn, shift_grad_attn = pull_attn(attn_local)
    rows_grad_mlp, gain_grad_mlp, shift_grad_mlp = pull_mlp(mlp_local)
    cot_rows = out_grad.astype(jnp.float32)
    input_grad = (cot_rows + rows_grad_attn + rows_grad_mlp).astype(jnp.bfloat16)
    bias_total = jnp.sum(cot_rows, axis=0)
    small_sums = (
        lax.psum_scatter(gain_grad_attn, ("dp", "tensor"), scatter_dimension=0, tiled=True),
        lax.psum_scatter(shift_grad_attn, ("dp", "tensor"), scatter_dimension=0, tiled=True),
        lax.psum_scatter(gain_grad_mlp, ("dp", "tensor"), scatter_dimension=0, tiled=True),
        lax.psum_scatter(shift_grad_mlp, ("dp", "tensor"), scatter_dimension=0, tiled=True),
        lax.psum_scatter(bias_total, ("dp", "tensor"), scatter_dimension=0, tiled=True),
    )
    return (
        layer_out,
        input_grad,
        small_sums[0],
        small_sums[1],
        small_sums[2],
        small_sums[3],
        reduced[0],
        reduced[1],
        reduced[2],
        small_sums[4],
        reduced[3],
        reduced[4],
        reduced[5],
        small_sums[4],
    )


F32 = jnp.float32
BF16 = jnp.bfloat16
MESH_ID = pl.DeviceIdType.MESH
LINE = 4
SEQ = 256
WIDTH = 1024
HID = 512
PAIR = 128


def nn(a, b):
    return jnp.dot(a, b, preferred_element_type=F32)


def nt(a, b):
    return lax.dot_general(a, b, (((1,), (1,)), ((), ())), preferred_element_type=F32)


def tn(a, b):
    return lax.dot_general(a, b, (((0,), (0,)), ((), ())), preferred_element_type=F32)


def turn_tables():
    position = np.arange(SEQ, dtype=np.float64)[:, None]
    lane = np.arange(PAIR) % HD
    rates = 10000.0 ** (-(lane % (ROT // 2)) * (2.0 / ROT))
    angles = position * rates[None, :]
    cosine = np.where(lane < ROT, np.cos(angles), 1.0)
    toward = np.where(lane < ROT // 2, -np.sin(angles), 0.0)
    away = np.where((lane >= ROT // 2) & (lane < ROT), np.sin(angles), 0.0)
    return np.stack([cosine, toward, away]).astype(np.float32)


SEATS = (0, 3, 1, 2)


def seat_of(z):
    return (2 * z - z // 2) % LINE


def rows_of(index, count):
    return pl.ds(pl.multiple_of(index * count, count), count)


class Place:
    def __init__(self):
        index = lax.axis_index("dp")
        self.t = lax.axis_index("tensor")
        self.z = index // 4
        self.k = index % 4
        self.y = self.k // 2
        self.c = self.k % 2
        self.kc = self.y * 2 + 1 - self.c
        self.ky = (1 - self.y) * 2 + self.c
        self.kyc = (1 - self.y) * 2 + 1 - self.c
        self.q = self.k * 2 + self.t
        self.core = self.at(self.z, self.kc, self.t)
        self.cross = (
            self.at(self.z, self.k, 1 - self.t),
            self.at(self.z, self.ky, self.t),
            self.at(self.z, self.ky, 1 - self.t),
        )

    def at(self, z, k, t):
        return (z * 4 + k, t)

    def line(self, z):
        return self.at(z, self.k, self.t)


class Wires:
    def __init__(self, sends, arrivals):
        self.sends, self.arrivals = sends, arrivals
        self.sent, self.landed = 0, 0

    def take(self, sends, arrivals):
        first = (self.sent, self.landed)
        self.sent += sends
        self.landed += arrivals
        return first

    def copy(self, send, arrival, src, dst, device):
        return pltpu.make_async_remote_copy(
            src_ref=src,
            dst_ref=dst,
            send_sem=self.sends.at[send],
            recv_sem=self.arrivals.at[arrival],
            device_id=device,
            device_id_type=MESH_ID,
        )

    def all_sent(self, send, view, device):
        self.copy(send, 0, view, view, device).wait_send()

    def all_landed(self, arrival, view, device):
        self.copy(0, arrival, view, view, device).wait_recv()


class PlaneGather:
    def __init__(self, me, wires, src, slot, split, blocks):
        self.me, self.wires, self.src, self.slot = me, wires, src, slot
        self.blocks = blocks
        self.pieces = (pl.ds(0, split), pl.ds(split, src.shape[0] - split))
        self.send, self.arrivals = wires.take(1, 4)
        self.near_blocks = (
            me.k * 2 + 1 - me.t,
            me.ky * 2 + me.t,
            me.ky * 2 + 1 - me.t,
        )

    def start(self, which):
        device = (self.me.cross[0], self.me.cross[1], self.me.core)[which]
        arrival = self.arrivals + (0, 1, 3)[which]
        self.wires.copy(self.send, arrival, self.src, self.slot(self.me.q), device).start()

    def pass_on(self, which):
        part = self.slot(self.near_blocks[which])
        self.wires.copy(self.send, self.arrivals + 3, part, part, self.me.core).start()

    def forward(self, which):
        block = self.slot(self.near_blocks[which])
        self.wires.all_landed(self.arrivals + which, block, self.me.core)
        part = block.at[self.pieces[which]]
        device = self.me.cross[1 - which]
        self.wires.copy(self.send, self.arrivals + 2, part, part, device).start()
        self.pass_on(which)

    def corner(self):
        block = self.slot(self.near_blocks[2])
        self.wires.all_landed(self.arrivals + 2, block, self.me.core)
        self.pass_on(2)

    def finish(self):
        self.wires.all_landed(self.arrivals + 3, self.blocks(4), self.me.core)

    def drain(self):
        self.wires.all_sent(self.send, self.blocks(7), self.me.core)


class LineGather:
    def __init__(self, me, wires, view):
        self.me, self.wires, self.view = me, wires, view
        self.sends, self.arrivals = wires.take(2, 6)

    def copy(self, way, hop, block):
        z = self.me.z
        view = self.view(block, 1)
        device = self.me.line(z + 1 if way == 0 else z - 1)
        return self.wires.copy(self.sends + way, self.arrivals + way * 3 + hop, view, view, device)

    def send(self, way, hop):
        z = self.me.z
        has = (z >= hop) & (z < LINE - 1) if way == 0 else (z + hop < LINE) & (z > 0)

        @pl.when(has)
        def _():
            self.copy(way, hop, z - hop if way == 0 else z + hop).start()

    def arrive(self, way, hop):
        z = self.me.z

        @pl.when(z > hop if way == 0 else z + 1 + hop < LINE)
        def _():
            self.copy(way, hop, z - 1 - hop if way == 0 else z + 1 + hop).wait_recv()

    def start(self, way):
        @pl.when(self.me.z != (0 if way == 0 else LINE - 1))
        def _():
            self.send(way, 0)

    def outer(self):
        for way in range(2):

            @pl.when(self.me.z == (0 if way == 0 else LINE - 1))
            def _(way=way):
                self.send(way, 0)

    def relay(self, way, hop):
        self.arrive(way, hop - 1)
        self.send(way, hop)

    def finish(self, way):
        self.arrive(way, LINE - 2)

    def drain(self):
        z = self.me.z
        for way in range(2):
            for count in range(1, LINE):

                @pl.when(z == (count - 1 if way == 0 else LINE - count))
                def _():
                    self.wires.all_sent(self.sends + way, self.view(0, count), self.me.core)


class LineReduce:
    def __init__(self, me, wires, held, landed):
        self.me, self.wires, self.held, self.landed = me, wires, held, landed
        self.sends, self.arrivals = wires.take(2, 6)

    def copy(self, way, block):
        z = self.me.z
        device = self.me.line(z - 1 if way == 0 else z + 1)
        return self.wires.copy(
            self.sends + way,
            self.arrivals + way * (LINE - 2) + block,
            self.held.at[block],
            self.landed.at[way, block],
            device,
        )

    def join(self, way, block):
        self.copy(way, block).wait_recv()
        total = self.held[block].astype(F32) + self.landed[way, block].astype(F32)
        self.held[block] = total.astype(BF16)

    def each(self, way, slot, act):
        z = self.me.z
        steps = slot - (LINE - 1 - z if way == 0 else z)
        left = z if way == 0 else LINE - 1 - z
        block = steps if way == 0 else LINE - 1 - steps

        @pl.when((steps >= 0) & (steps < left))
        def _():
            act(block)

    def slot(self, way, slot):
        def act(block):
            if slot > 0:
                started = self.me.z < LINE - 1 if way == 0 else self.me.z > 0

                @pl.when(started)
                def _():
                    self.join(way, block)

            self.copy(way, block).start()

        self.each(way, slot, act)

    def finish(self, way):
        z = self.me.z

        @pl.when(z < LINE - 1 if way == 0 else z > 0)
        def _():
            self.join(way, z)

    def drain(self):
        z = self.me.z
        for way in range(2):
            for count in range(1, LINE):

                @pl.when(z == (count if way == 0 else LINE - 1 - count))
                def _():
                    view = self.held.at[pl.ds(0, count)]
                    self.wires.all_sent(self.sends + way, view, self.me.core)


class PlaneReduce:
    def __init__(self, me, wires, part, paired, crossed):
        self.me, self.wires = me, wires
        self.part, self.paired, self.crossed = part, paired, crossed
        self.send, self.arrivals = wires.take(1, 4)
        self.blocks = (me.ky * 2 + 1 - me.t, me.k * 2 + 1 - me.t, me.ky * 2 + me.t)

    def pair(self, y):
        rows = rows_of(y * 2 + 1 - self.me.c, SEQ)
        return self.wires.copy(
            self.send, self.arrivals, self.part.at[rows], self.paired.at[y], self.me.core
        )

    def rows(self, which, half):
        first = pl.multiple_of(self.blocks[which] * 128 + half * 64, 64)
        return pl.ds(first, 64)

    def cross(self, which, half):
        way = (half, 0, 1)[which]
        return self.wires.copy(
            self.send,
            self.arrivals + (1 + half if which == 0 else 3),
            self.part.at[self.rows(which, half)],
            self.crossed.at[which, pl.ds(half * 64, 64)],
            self.me.cross[way],
        )

    def middle(self):
        self.wires.all_landed(self.arrivals, self.part.at[pl.ds(0, 2 * SEQ)], self.me.core)
        for y in range(2):
            rows = rows_of(y * 2 + self.me.c, SEQ)
            total = self.part[rows].astype(F32) + self.paired[y].astype(F32)
            self.part[rows] = total.astype(BF16)
        for which, half in ((0, 0), (0, 1), (1, 0), (2, 1)):
            self.cross(which, half).start()

    def turn(self, half):
        self.cross(0, half).wait_recv()
        rows = self.rows(2 - half, half)
        total = self.part[rows].astype(F32) + self.crossed[0, pl.ds(half * 64, 64)].astype(F32)
        self.part[rows] = total.astype(BF16)
        self.cross(2 - half, half).start()

    def finish(self):
        self.wires.all_landed(self.arrivals + 3, self.part.at[pl.ds(0, SEQ)], self.me.core)
        total = self.part[rows_of(self.me.q, 128)].astype(F32)
        return total + self.crossed[1].astype(F32) + self.crossed[2].astype(F32)

    def drain(self):
        self.wires.all_sent(self.send, self.part.at[pl.ds(0, 896)], self.me.core)


def layer_kernel(
    x_hbm,
    g_hbm,
    qkv_hbm,
    dense_hbm,
    up_hbm,
    down_hbm,
    turn_hbm,
    attn_gain_ref,
    attn_shift_ref,
    mlp_gain_ref,
    mlp_shift_ref,
    dense_bias_ref,
    down_bias_ref,
    starts_ref,
    lengths_ref,
    qkv_bias_ref,
    up_bias_ref,
    layer_out_ref,
    input_grad_ref,
    qkv_grad_ref,
    dense_grad_ref,
    up_grad_ref,
    down_grad_ref,
    small_out_ref,
    turn_ref,
    x_all,
    g_all,
    small_line,
    small_all,
    qkv_w,
    dense_w,
    up_w,
    down_w,
    vec_ref,
    bias_ref,
    normed_a,
    normed_m,
    context_ref,
    turned_grad,
    active_ref,
    hidden_grad,
    slope_ref,
    part_out,
    part_attn,
    part_mlp,
    paired_ref,
    crossed_ref,
    up_held,
    up_landed,
    down_held,
    down_landed,
    late_held,
    late_landed,
    qkv_held,
    qkv_landed,
    up_final,
    qkv_final,
    dense_line,
    dense_held,
    dense_mine,
    dense_landed,
    qkv_bias_held,
    qkv_bias_line,
    qkv_bias_final,
    up_bias_held,
    up_bias_final,
    sums_held,
    sums_chip,
    sums_total,
    sums_core,
    sums_cross,
    sums_line,
    sends,
    arrivals,
    local_sems,
):
    me = Place()
    wires = Wires(sends, arrivals)
    z, k, t = me.z, me.k, me.t

    barrier = pltpu.get_barrier_semaphore()

    def greet(device):
        pl.semaphore_signal(barrier, inc=1, device_id=device, device_id_type=MESH_ID)

    greet(me.core)
    greet(me.at(z, me.kyc, t))
    for device in me.cross:
        greet(device)
    for step in range(1, LINE):
        greet(me.line((z + step) % LINE))
    local_copies = []

    def local(src, dst):
        copy = pltpu.make_async_copy(src, dst, local_sems.at[len(local_copies)])
        local_copies.append(copy)
        copy.start()

    seat = pl.ds(pl.multiple_of(z * 256 + k * 64, 64), 64)
    peers = (me.kc, me.ky, me.kyc)
    devices = tuple(me.at(z, peer, t) for peer in peers)

    def three(arrival, view):
        wires.all_landed(arrival, view, me.core)

    local(dense_hbm, dense_line.at[z])
    for place, other in enumerate(SEATS):
        local(
            up_hbm.at[:, rows_of(other * 4 + k, 128)],
            up_w.at[seat, pl.ds(place * 128, 128)],
        )
    local(down_hbm, down_w.at[rows_of(seat_of(z), 128)])
    for which in range(3):
        local(
            qkv_hbm.at[which, :, rows_of(k, PAIR)],
            qkv_w.at[seat, pl.ds(which * PAIR, PAIR)],
        )
    local(x_hbm, x_all.at[rows_of(me.q, 128)])
    local(g_hbm, g_all.at[rows_of(me.q, 128)])
    local(turn_hbm, turn_ref)
    qkv_bias_held[...] = jnp.zeros_like(qkv_bias_held)
    up_bias_held[...] = jnp.zeros_like(up_bias_held)

    def side_by_side(*fields):
        return jnp.concatenate(
            [field.astype(F32).reshape(1, field.shape[-1]) for field in fields], axis=1
        )

    triple = qkv_bias_ref[...]
    blank = jnp.zeros((1, 60), F32)
    small_line[z] = jnp.concatenate(
        [
            side_by_side(
                attn_gain_ref[...], attn_shift_ref[...], mlp_gain_ref[...], mlp_shift_ref[...]
            ),
            side_by_side(
                dense_bias_ref[...], down_bias_ref[...], starts_ref[...], lengths_ref[...], blank
            ),
            side_by_side(triple[0:1], triple[1:2], triple[2:3], blank[:, :32]),
            side_by_side(up_bias_ref[...]),
            jnp.zeros((4, 128), F32),
        ],
        axis=0,
    )
    pl.semaphore_wait(barrier, 8)

    up_send, up_arrival = wires.take(1, 2)
    for place, other in enumerate(SEATS):
        for which in range(3):
            wires.copy(
                up_send,
                up_arrival + place // 2,
                up_hbm.at[:, rows_of(other * 4 + peers[which], 128)],
                up_w.at[seat, pl.ds(place * 128, 128)],
                devices[which],
            ).start()

    qkv_sends, qkv_arrival = wires.take(1, 1)

    def rows_slot(ref):
        return (lambda block: ref.at[rows_of(block, 128)]), (
            lambda count: ref.at[pl.ds(0, count * 128)]
        )

    slot, blocks = rows_slot(x_all)
    gather_x = PlaneGather(me, wires, x_hbm, slot, 48, blocks)
    for which in range(3):
        gather_x.start(which)
    slot, blocks = rows_slot(g_all)
    gather_g = PlaneGather(me, wires, g_hbm, slot, 48, blocks)
    gather_small = PlaneGather(
        me,
        wires,
        small_line,
        lambda block: small_all.at[block],
        2,
        lambda count: small_all.at[pl.ds(0, count)],
    )
    small_send, small_arrival = wires.take(1, 1)
    for step in range(1, LINE):
        wires.copy(
            small_send,
            small_arrival,
            small_line.at[z],
            small_line.at[z],
            me.line((z + step) % LINE),
        ).start()

    def line_gather(ref, count):
        return LineGather(
            me, wires, lambda s, n: ref.at[pl.ds(pl.multiple_of(s * count, count), n * count)]
        )

    line_dense = LineGather(me, wires, lambda s, n: dense_line.at[pl.ds(s, n)])
    line_qkv = line_gather(qkv_w, 256)
    line_upa, line_upb = (
        LineGather(
            me,
            wires,
            lambda s, n, first=first: up_w.at[
                pl.ds(pl.multiple_of(s * 256, 256), n * 256), pl.ds(first, 256)
            ],
        )
        for first in (0, 256)
    )
    line_down = LineGather(
        me,
        wires,
        lambda s, n: down_w.at[pl.ds(pl.multiple_of(seat_of(s) * 128, 128), n * 128)],
    )
    reduce_down = LineReduce(
        me, wires, down_held, down_landed
    )
    reduce_late = LineReduce(
        me, wires, late_held, late_landed
    )
    reduce_up = LineReduce(
        me, wires, up_held, up_landed
    )
    reduce_qkv = LineReduce(
        me, wires, qkv_held, qkv_landed
    )
    reduce_dense = LineReduce(
        me, wires, dense_mine, dense_landed
    )
    reduce_attn = PlaneReduce(me, wires, part_attn, paired_ref.at[0], crossed_ref.at[0])
    reduce_out = PlaneReduce(me, wires, part_out, paired_ref.at[1], crossed_ref.at[1])
    reduce_mlp = PlaneReduce(me, wires, part_mlp, paired_ref.at[2], crossed_ref.at[2])

    local_copies[0].wait()
    line_dense.outer()
    line_dense.start(0)
    line_dense.start(1)

    own_small = pltpu.make_async_copy(
        small_line, small_all.at[me.q], local_sems.at[len(local_copies)]
    )
    own_dense = pltpu.make_async_copy(
        dense_line.at[k], dense_w.at[rows_of(k, 32)], local_sems.at[len(local_copies) + 1]
    )
    dense_sends, dense_arrival = wires.take(1, 1)
    back_sends, back_arrival = wires.take(2, 2)
    bias_sends, bias_arrival = wires.take(2, 2)
    out_sends, out_arrival = wires.take(2, 2)
    sums_sends, sums_arrival = wires.take(3, 3)

    def along(send, arrival, source, target):
        for step in range(1, LINE):
            there = (z + step) % LINE
            wires.copy(send, arrival, source(there), target, me.line(there)).start()

    def around(send, arrival, source, target):
        for which in range(3):
            wires.copy(send, arrival, source(peers[which]), target, devices[which]).start()

    def norm_rows(rows):
        values = x_all[rows].astype(F32)
        centred = values - jnp.mean(values, axis=-1, keepdims=True)
        rate = lax.rsqrt(jnp.mean(centred * centred, axis=-1, keepdims=True) + NORM_EPS)
        return centred * rate, rate

    def norm_block(block, carry):
        rows = rows_of(block, 128)
        unit, _ = norm_rows(rows)
        normed_m[rows] = (unit * vec_ref[2:3, :] + vec_ref[3:4, :]).astype(BF16)
        return carry

    def attn_norm(block, carry):
        rows = rows_of(block, 128)
        unit, _ = norm_rows(rows)
        normed_a[rows] = (unit * vec_ref[0:1, :] + vec_ref[1:2, :]).astype(BF16)
        return carry

    def activate(half):
        columns = slice(half * 256, (half + 1) * 256)

        def tile_of(tile, carry):
            rows = rows_of(tile, 256)
            up_bias = jnp.concatenate(
                [small_all[me.q, s, 3:4, :] for s in SEATS[half * 2 : half * 2 + 2]], axis=1
            )
            hidden = nn(normed_m[rows], up_w[:, columns]) + up_bias
            share = (1.0 + lax.erf(hidden * 0.5**0.5)) * 0.5
            bell = jnp.exp(hidden * hidden * -0.5) * (2.0 * np.pi) ** -0.5
            slope_ref[rows, columns] = share + hidden * bell
            active_ref[rows, columns] = (hidden * share).astype(BF16)
            return carry

        return tile_of

    activate_a, activate_b = activate(0), activate(1)

    def down_block(block, carry):
        units = rows_of(seat_of(block), 128)
        grad = tn(active_ref[:, units], g_all[...]).astype(BF16)
        down_held[block] = grad[:64]
        late_held[block] = grad[64:]
        return carry

    def feed_back(tile, carry):
        rows = rows_of(tile, 256)
        grad = (nt(g_all[rows], down_w[...]) * slope_ref[rows]).astype(BF16)
        hidden_grad[rows] = grad
        up_bias_held[0:1, :] += jnp.sum(grad.astype(F32), axis=0, keepdims=True)
        return carry

    def feed_in(tile, carry):
        rows = rows_of(tile, 256)
        part_mlp[rows] = nt(hidden_grad[rows], up_w[...]).astype(BF16)
        return carry

    def up_block(block, carry):
        up_held[block] = tn(normed_m[:, rows_of(block, 256)], hidden_grad[...]).astype(BF16)
        return carry

    scale = HD**-0.5

    def attend(seq, carry):
        rows = rows_of(seq, SEQ)
        cosine, toward, away = turn_ref[0], turn_ref[1], turn_ref[2]
        projected = nn(normed_a[rows], qkv_w[...]) + bias_ref[0:1, :]

        def project(which):
            return projected[:, which * PAIR : (which + 1) * PAIR]

        def turned(field):
            return (
                field * cosine
                + pltpu.roll(field, ROT // 2, 1) * away
                + pltpu.roll(field, PAIR - ROT // 2, 1) * toward
            )

        def turned_back(field):
            return (
                field * cosine
                - pltpu.roll(field, ROT // 2, 1) * away
                - pltpu.roll(field, PAIR - ROT // 2, 1) * toward
            )

        query = turned(project(0)).astype(BF16)
        key = turned(project(1)).astype(BF16)
        value = project(2).astype(BF16)
        context_grad = nt(g_all[rows], dense_w[...]).astype(BF16)

        spans = small_all[seq * 2, z, 1:2, :]
        down_pos = lax.broadcasted_iota(jnp.int32, (SEQ, 1), 0).astype(F32)
        over_pos = lax.broadcasted_iota(jnp.int32, (1, SEQ), 1).astype(F32)

        def labels(place):
            total = jnp.zeros(place.shape, F32)
            for span in range(2):
                begin = spans[:, 64 + span : 65 + span]
                end = begin + spans[:, 66 + span : 67 + span]
                total = total + jnp.where((place >= begin) & (place < end), span + 1.0, 0.0)
            return total

        down_label, over_label = labels(down_pos), labels(over_pos)
        allowed = (over_pos <= down_pos) | ((down_label == over_label) & (down_label > 0.0))

        lane = lax.broadcasted_iota(jnp.int32, (SEQ, PAIR), 1)
        parts = []
        for head in range(2):
            mine = (lane >= HD) if head else (lane < HD)
            zero = jnp.zeros_like(query)
            scores = nt(jnp.where(mine, query, zero), key) * scale
            scores = jnp.where(allowed, scores, NEG_FILL)
            exponent = jnp.exp(scores - jnp.max(scores, axis=-1, keepdims=True))
            probs = exponent * (1.0 / jnp.sum(exponent, axis=-1, keepdims=True))
            low = probs.astype(BF16)
            prob_grad = nt(jnp.where(mine, context_grad, zero), value)
            inner = jnp.sum(prob_grad * probs, axis=-1, keepdims=True)
            score_grad = (probs * (prob_grad - inner)).astype(BF16)
            parts.append(
                (
                    nn(low, value),
                    tn(low, context_grad),
                    nn(score_grad, key) * scale,
                    tn(score_grad, query) * scale,
                )
            )
        context, value_grad, query_grad, key_grad = (
            jnp.where(lane < HD, first, second) for first, second in zip(*parts)
        )
        context_ref[rows] = context.astype(BF16)
        grads = (
            turned_back(query_grad).astype(BF16),
            turned_back(key_grad).astype(BF16),
            value_grad.astype(BF16),
        )
        for which in range(3):
            turned_grad[rows, which * PAIR : (which + 1) * PAIR] = grads[which]
            qkv_bias_held[which : which + 1, :] += jnp.sum(
                grads[which].astype(F32), axis=0, keepdims=True
            )
        return carry

    def attend_in(tile, carry):
        rows = rows_of(tile, 256)
        part_attn[rows] = nt(turned_grad[rows], qkv_w[...]).astype(BF16)
        return carry

    def qkv_block(block, carry):
        qkv_held[block] = tn(normed_a[:, rows_of(block, 256)], turned_grad[...]).astype(BF16)
        return carry

    def mix(tile, carry):
        rows = rows_of(tile, 256)
        mixed = nn(context_ref[rows], dense_w[...]) + nn(active_ref[rows], down_w[...])
        part_out[rows] = mixed.astype(BF16)
        return carry

    def locals_done():
        for copy in local_copies[1:]:
            copy.wait()

    def small_line_done():
        three(small_arrival, small_line.at[pl.ds(0, 3)])
        own_small.start()
        for which in range(3):
            gather_small.start(which)

    def upa_start():
        three(up_arrival, up_w.at[pl.ds(0, 96)])
        line_upa.outer()
        line_upa.start(0)
        line_upa.start(1)

    def upb_start():
        three(up_arrival + 1, up_w.at[pl.ds(0, 96)])
        line_upb.outer()
        line_upb.start(0)
        line_upb.start(1)

    def down_outer():
        line_down.outer()

    def qkv_send():
        for which in range(3):
            for part in range(3):
                wires.copy(
                    qkv_sends,
                    qkv_arrival,
                    qkv_hbm.at[part, :, rows_of(peers[which], PAIR)],
                    qkv_w.at[seat, pl.ds(part * PAIR, PAIR)],
                    devices[which],
                ).start()

    def qkv_outer():
        three(qkv_arrival, qkv_w.at[pl.ds(0, 192)])
        line_qkv.outer()

    def qkv_start():
        line_qkv.start(0)
        line_qkv.start(1)

    def down_start():
        line_down.start(0)
        line_down.start(1)

    def dense_send():
        around(
            dense_sends, dense_arrival, lambda to: dense_line.at[to], dense_w.at[rows_of(k, 32)]
        )
        own_dense.start()

    def dense_done():
        three(dense_arrival, dense_w.at[pl.ds(0, 96)])
        own_dense.wait()

    def spread_table(kind, width):
        table = small_all[...].reshape(256, 128).astype(BF16)
        line_id = lax.broadcasted_iota(jnp.int32, (256, width), 0)
        column = lax.broadcasted_iota(jnp.int32, (256, width), 1)
        from_z, from_q = (line_id >> 3) & 3, line_id >> 5
        if width == WIDTH:
            chosen = from_z * 8 + from_q == column >> 5
        else:
            chosen = (from_z == k) & (from_q == (column >> 5) * 2 + t)
        chosen = chosen & ((line_id & 7) == kind)
        spread = tn(table, jnp.where(chosen, 1.0, 0.0).astype(BF16))
        lane_row = lax.broadcasted_iota(jnp.int32, (128, width), 0)
        lane_col = lax.broadcasted_iota(jnp.int32, (128, width), 1) & 31

        def vector(which):
            picked = jnp.where(lane_row == lane_col + which * 32, spread, 0.0)
            return jnp.sum(picked, axis=0, keepdims=True)

        return vector

    def vectors():
        own_small.wait()
        vector = spread_table(0, WIDTH)
        for which in range(4):
            vec_ref[which : which + 1, :] = vector(which)

    def more_vectors():
        vector = spread_table(1, WIDTH)
        for which in range(2):
            vec_ref[4 + which : 5 + which, :] = vector(which)
        vector = spread_table(2, PAIR)
        for which in range(3):
            bias_ref[0:1, which * PAIR : (which + 1) * PAIR] = vector(which)

    def up_bias_send():
        along(
            bias_sends,
            bias_arrival,
            lambda there: up_bias_held.at[:, rows_of(seat_of(there), 128)],
            up_bias_final.at[z],
        )
        up_bias_final[z] = up_bias_held[:, rows_of(seat_of(z), 128)]

    def dense_part():
        dense_held[...] = tn(context_ref[...], g_all[...]).astype(BF16)
        around(
            back_sends, back_arrival, lambda to: dense_held.at[rows_of(to, 32)], dense_mine.at[k]
        )
        around(back_sends + 1, back_arrival + 1, lambda to: qkv_bias_held, qkv_bias_line.at[k])
        dense_mine[k] = dense_held[rows_of(k, 32)]
        qkv_bias_line[k] = qkv_bias_held[...]

    def dense_back():
        three(back_arrival, dense_mine.at[pl.ds(0, 3)])
        three(back_arrival + 1, qkv_bias_line.at[pl.ds(0, 3)])
        along(
            bias_sends + 1,
            bias_arrival + 1,
            lambda there: qkv_bias_line.at[there],
            qkv_bias_final.at[z],
        )
        qkv_bias_final[z] = qkv_bias_line[z]

    def up_out():
        around(
            out_sends, out_arrival, lambda to: up_held.at[z, rows_of(to, 64)], up_final.at[k]
        )
        up_final[k] = up_held[z, rows_of(k, 64)]

    def qkv_out():
        around(
            out_sends + 1,
            out_arrival + 1,
            lambda to: qkv_held.at[z, rows_of(to, 64)],
            qkv_final.at[k],
        )
        qkv_final[k] = qkv_held[z, rows_of(k, 64)]

    def down_out():
        down_grad_ref[0:64, :] = down_held[z]
        down_grad_ref[64:128, :] = late_held[z]

    def dense_out():
        dense_grad_ref[...] = dense_mine[z]

    def up_result():
        three(out_arrival, up_final.at[pl.ds(0, 3)])
        up_grad_ref[...] = up_final[...]

    def qkv_result():
        three(out_arrival + 1, qkv_final.at[pl.ds(0, 3)])
        qkv_grad_ref[...] = qkv_final[...]

    own = rows_of(me.q, 128)
    def layer_out():
        mixed = reduce_out.finish()
        layer_out_ref[...] = (
            x_all[own].astype(F32) + mixed + vec_ref[4:5, :] + vec_ref[5:6, :]
        ).astype(BF16)

    def norm_grads():
        from_attn = reduce_attn.finish()
        from_mlp = reduce_mlp.finish()
        cotangent = g_all[own].astype(F32)
        unit, rate = norm_rows(own)
        sums_held[...] = jnp.zeros_like(sums_held)
        for which, field in enumerate(
            (from_attn * unit, from_attn, from_mlp * unit, from_mlp, cotangent)
        ):
            sums_held[which : which + 1, :] = jnp.sum(field, axis=0, keepdims=True)
        wires.copy(sums_sends, sums_arrival, sums_held, sums_core, me.core).start()
        pulled = from_attn * vec_ref[0:1, :] + from_mlp * vec_ref[2:3, :]
        pulled = (
            pulled
            - jnp.mean(pulled, axis=-1, keepdims=True)
            - unit * jnp.mean(pulled * unit, axis=-1, keepdims=True)
        )
        input_grad_ref[...] = (cotangent + rate * pulled).astype(BF16)

    def sums_plane():
        three(sums_arrival, sums_core)
        sums_chip[...] = sums_held[...] + sums_core[...]
        for which in range(3):
            wires.copy(
                sums_sends + 1,
                sums_arrival + 1,
                sums_chip,
                sums_cross.at[which],
                me.cross[which],
            ).start()

    def sums_send():
        three(sums_arrival + 1, sums_cross)
        sums_total[...] = sums_chip[...] + sums_cross[0] + sums_cross[1] + sums_cross[2]
        along(
            sums_sends + 2,
            sums_arrival + 2,
            lambda there: sums_total.at[:, rows_of(there, 256)],
            sums_line.at[z],
        )
        sums_line[z] = sums_total[:, rows_of(z, 256)]

    def small_result():
        three(sums_arrival + 2, sums_line.at[pl.ds(0, 3)])
        three(bias_arrival, up_bias_final.at[pl.ds(0, 3)])
        three(bias_arrival + 1, qkv_bias_final.at[pl.ds(0, 3)])
        sums = sums_line[0] + sums_line[1] + sums_line[2] + sums_line[3]
        sums = jnp.where(k >= 2, sums[:, 128:], sums[:, :128])
        small_out_ref[0:8, :] = pltpu.roll(sums, (128 - (me.q % 4) * 32) % 128, 1)
        bias_sum = qkv_bias_final[0] + qkv_bias_final[1] + qkv_bias_final[2] + qkv_bias_final[3]
        small_out_ref[8:16, :] = pltpu.roll(bias_sum, (128 - k * 32) % 128, 1)
        small_out_ref[16:24, :] = (
            up_bias_final[0] + up_bias_final[1] + up_bias_final[2] + up_bias_final[3]
        )

    def ends_of(body):
        def outer(index, carry):
            return body(index * (LINE - 1), carry)

        return outer

    locals_done()
    upa_start()
    line_dense.relay(1, 1)
    upb_start()
    small_line_done()
    gather_g.start(0)
    line_dense.relay(0, 1)
    line_dense.relay(1, 2)
    line_upa.relay(0, 1)
    gather_small.forward(0)
    qkv_send()
    line_upa.relay(1, 1)
    gather_x.forward(0)
    line_upb.relay(0, 1)
    gather_x.forward(1)
    gather_small.forward(1)
    qkv_outer()
    down_outer()
    line_upb.relay(1, 1)
    line_dense.finish(1)
    line_dense.relay(0, 2)
    gather_g.start(1)
    line_upa.relay(0, 2)
    qkv_start()
    gather_small.corner()
    gather_x.corner()
    gather_x.finish()
    gather_small.finish()
    vectors()
    line_upb.relay(0, 2)
    gather_g.forward(0)
    line_upb.relay(1, 2)
    line_dense.finish(0)
    line_upa.finish(0)
    line_upa.relay(1, 2)
    lax.fori_loop(4, 8, attn_norm, 0)
    gather_g.start(2)
    lax.fori_loop(0, 4, attn_norm, 0)
    line_qkv.relay(1, 1)
    lax.fori_loop(4, 8, norm_block, 0)
    gather_g.forward(1)
    line_qkv.relay(0, 1)
    dense_send()
    line_upb.finish(0)
    lax.fori_loop(0, 4, norm_block, 0)
    line_upa.finish(1)
    line_upb.finish(1)
    lax.fori_loop(0, 4, activate_b, 0)
    gather_g.corner()
    lax.fori_loop(0, 4, activate_a, 0)
    line_qkv.relay(1, 2)
    line_qkv.relay(0, 2)
    gather_g.finish()
    lax.fori_loop(0, 2, ends_of(down_block), 0)
    dense_done()
    lax.fori_loop(1, 3, down_block, 0)
    reduce_down.slot(0, 0)
    reduce_late.slot(0, 0)
    reduce_down.slot(1, 0)
    down_start()
    more_vectors()
    reduce_late.slot(1, 0)
    line_qkv.finish(0)
    line_qkv.finish(1)
    lax.fori_loop(3, 4, attend, 0)
    lax.fori_loop(0, 1, attend, 0)
    lax.fori_loop(2, 3, attend, 0)
    line_down.relay(0, 1)
    reduce_down.slot(1, 1)
    line_down.relay(1, 1)
    reduce_down.slot(0, 1)
    lax.fori_loop(1, 2, attend, 0)
    lax.fori_loop(0, 2, ends_of(qkv_block), 0)
    reduce_qkv.slot(0, 0)
    reduce_qkv.slot(1, 0)
    reduce_late.slot(1, 1)
    lax.fori_loop(0, 2, attend_in, 0)
    dense_part()
    reduce_attn.pair(0).start()
    reduce_late.slot(0, 1)
    line_down.relay(1, 2)
    line_down.relay(0, 2)
    lax.fori_loop(2, 4, attend_in, 0)
    lax.fori_loop(1, 3, qkv_block, 0)
    reduce_down.slot(0, 2)
    reduce_attn.pair(1).start()
    line_down.finish(0)
    reduce_qkv.slot(0, 1)
    dense_back()
    reduce_qkv.slot(1, 1)
    line_down.finish(1)
    lax.fori_loop(0, 2, feed_back, 0)
    lax.fori_loop(2, 4, feed_back, 0)
    reduce_dense.slot(1, 0)
    lax.fori_loop(0, 2, ends_of(up_block), 0)
    reduce_up.slot(1, 0)
    reduce_up.slot(0, 0)
    reduce_attn.middle()
    lax.fori_loop(0, 2, feed_in, 0)
    lax.fori_loop(2, 4, feed_in, 0)
    reduce_dense.slot(0, 0)
    reduce_mlp.pair(1).start()
    reduce_mlp.pair(0).start()
    reduce_mlp.middle()
    reduce_qkv.slot(1, 2)
    reduce_qkv.slot(0, 2)
    lax.fori_loop(1, 3, up_block, 0)
    lax.fori_loop(2, 4, mix, 0)
    lax.fori_loop(0, 2, mix, 0)
    reduce_down.finish(0)
    reduce_out.pair(1).start()
    reduce_up.slot(1, 1)
    reduce_dense.slot(1, 1)
    reduce_mlp.turn(1)
    reduce_attn.turn(0)
    reduce_down.slot(1, 2)
    reduce_mlp.turn(0)
    reduce_out.pair(0).start()
    reduce_attn.turn(1)
    reduce_up.slot(0, 1)
    reduce_out.middle()
    reduce_qkv.finish(0)
    reduce_up.slot(1, 2)
    reduce_late.slot(1, 2)
    reduce_dense.slot(0, 1)
    norm_grads()
    reduce_up.slot(0, 2)
    reduce_dense.slot(1, 2)
    reduce_late.slot(0, 2)
    sums_plane()
    reduce_qkv.finish(1)
    qkv_out()
    reduce_dense.slot(0, 2)
    up_bias_send()
    reduce_out.turn(1)
    reduce_out.turn(0)
    reduce_down.finish(1)
    sums_send()
    reduce_up.finish(1)
    reduce_up.finish(0)
    up_out()
    layer_out()
    reduce_late.finish(1)
    reduce_late.finish(0)
    qkv_result()
    down_out()
    reduce_dense.finish(1)
    reduce_dense.finish(0)
    dense_out()
    up_result()
    small_result()

    for send, view in (
        (up_send, up_w.at[pl.ds(0, 192)]),
        (qkv_sends, qkv_w.at[pl.ds(0, 192)]),
        (small_send, small_line.at[pl.ds(0, 3)]),
        (dense_sends, dense_w.at[pl.ds(0, 96)]),
        (back_sends, dense_mine.at[pl.ds(0, 3)]),
        (back_sends + 1, qkv_bias_line.at[pl.ds(0, 3)]),
        (bias_sends, up_bias_final.at[pl.ds(0, 3)]),
        (bias_sends + 1, qkv_bias_final.at[pl.ds(0, 3)]),
        (out_sends, up_final.at[pl.ds(0, 3)]),
        (out_sends + 1, qkv_final.at[pl.ds(0, 3)]),
        (sums_sends, sums_core),
        (sums_sends + 1, sums_cross),
        (sums_sends + 2, sums_line.at[pl.ds(0, 3)]),
    ):
        wires.all_sent(send, view, me.core)
    for item in (
        gather_x,
        gather_g,
        gather_small,
        line_dense,
        line_qkv,
        line_upa,
        line_upb,
        line_down,
        reduce_attn,
        reduce_out,
        reduce_mlp,
        reduce_qkv,
        reduce_dense,
        reduce_down,
        reduce_late,
        reduce_up,
    ):
        item.drain()


def final_kernel(
    layer_out_ref,
    input_grad_ref,
    qkv_ref,
    dense_ref,
    up_ref,
    down_ref,
    small_ref,
    layer_out,
    input_grad,
    attn_gain_grad,
    attn_shift_grad,
    mlp_gain_grad,
    mlp_shift_grad,
    qkv_grad,
    qkv_bias_grad,
    dense_grad,
    dense_bias_grad,
    up_grad,
    up_bias_grad,
    down_grad,
    down_bias_grad,
):
    layer_out[...] = layer_out_ref[...]
    input_grad[...] = input_grad_ref[...]
    for row, out in enumerate((attn_gain_grad, attn_shift_grad, mlp_gain_grad, mlp_shift_grad)):
        out[...] = small_ref[row, :32]
    dense_bias_grad[...] = small_ref[4, :32]
    down_bias_grad[...] = small_ref[4, :32]
    qkv_bias_grad[...] = small_ref[8:11, :32]
    up_bias_grad[...] = small_ref[16, :]
    for origin in range(4):
        for which in range(3):
            qkv_grad[which, :, origin * PAIR : (origin + 1) * PAIR] = qkv_ref[
                origin, :, which * PAIR : (which + 1) * PAIR
            ].astype(F32)
        for place, other in enumerate(SEATS):
            first = (other * 4 + origin) * 128
            up_grad[:, first : first + 128] = up_ref[
                origin, :, place * 128 : (place + 1) * 128
            ].astype(F32)
    dense_grad[...] = dense_ref[...].astype(F32)
    down_grad[...] = down_ref[...].astype(F32)


def plane_layer(
    hidden_in,
    out_grad,
    span_start,
    span_length,
    attn_gain,
    attn_shift,
    mlp_gain,
    mlp_shift,
    qkv_weight,
    qkv_bias,
    dense_weight,
    dense_bias,
    up_weight,
    up_bias,
    down_weight,
    down_bias,
):
    vmem = pl.BlockSpec(memory_space=pltpu.VMEM)
    anywhere = pl.BlockSpec(memory_space=pl.ANY)
    tokens = 4 * SEQ
    outs = pl.pallas_call(
        layer_kernel,
        out_shape=(
            jax.ShapeDtypeStruct((128, WIDTH), BF16),
            jax.ShapeDtypeStruct((128, WIDTH), BF16),
            jax.ShapeDtypeStruct((4, 64, 3 * PAIR), BF16),
            jax.ShapeDtypeStruct((32, WIDTH), BF16),
            jax.ShapeDtypeStruct((4, 64, HID), BF16),
            jax.ShapeDtypeStruct((128, WIDTH), BF16),
            jax.ShapeDtypeStruct((24, 128), F32),
        ),
        in_specs=[anywhere] * 7 + [vmem] * 10,
        out_specs=(vmem,) * 7,
        scratch_shapes=[
            pltpu.VMEM((3, SEQ, PAIR), F32),
            pltpu.VMEM((tokens, WIDTH), BF16),
            pltpu.VMEM((tokens, WIDTH), BF16),
            pltpu.VMEM((LINE, 8, 128), F32),
            pltpu.VMEM((8, LINE, 8, 128), F32),
            pltpu.VMEM((WIDTH, 3 * PAIR), BF16),
            pltpu.VMEM((PAIR, WIDTH), BF16),
            pltpu.VMEM((WIDTH, HID), BF16),
            pltpu.VMEM((HID, WIDTH), BF16),
            pltpu.VMEM((8, WIDTH), F32),
            pltpu.VMEM((8, 3 * PAIR), F32),
            pltpu.VMEM((tokens, WIDTH), BF16),
            pltpu.VMEM((tokens, WIDTH), BF16),
            pltpu.VMEM((tokens, PAIR), BF16),
            pltpu.VMEM((tokens, 3 * PAIR), BF16),
            pltpu.VMEM((tokens, HID), BF16),
            pltpu.VMEM((tokens, HID), BF16),
            pltpu.VMEM((tokens, HID), F32),
            pltpu.VMEM((tokens, WIDTH), BF16),
            pltpu.VMEM((tokens, WIDTH), BF16),
            pltpu.VMEM((tokens, WIDTH), BF16),
            pltpu.VMEM((3, 2, SEQ, WIDTH), BF16),
            pltpu.VMEM((3, 3, 128, WIDTH), BF16),
            pltpu.VMEM((LINE, 256, HID), BF16),
            pltpu.VMEM((2, LINE, 256, HID), BF16),
            pltpu.VMEM((LINE, 64, WIDTH), BF16),
            pltpu.VMEM((2, LINE, 64, WIDTH), BF16),
            pltpu.VMEM((LINE, 64, WIDTH), BF16),
            pltpu.VMEM((2, LINE, 64, WIDTH), BF16),
            pltpu.VMEM((LINE, 256, 3 * PAIR), BF16),
            pltpu.VMEM((2, LINE, 256, 3 * PAIR), BF16),
            pltpu.VMEM((4, 64, HID), BF16),
            pltpu.VMEM((4, 64, 3 * PAIR), BF16),
            pltpu.VMEM((LINE, 32, WIDTH), BF16),
            pltpu.VMEM((PAIR, WIDTH), BF16),
            pltpu.VMEM((LINE, 32, WIDTH), BF16),
            pltpu.VMEM((2, LINE, 32, WIDTH), BF16),
            pltpu.VMEM((8, PAIR), F32),
            pltpu.VMEM((4, 8, PAIR), F32),
            pltpu.VMEM((LINE, 8, PAIR), F32),
            pltpu.VMEM((8, HID), F32),
            pltpu.VMEM((LINE, 8, 128), F32),
            pltpu.VMEM((8, WIDTH), F32),
            pltpu.VMEM((8, WIDTH), F32),
            pltpu.VMEM((8, WIDTH), F32),
            pltpu.VMEM((8, WIDTH), F32),
            pltpu.VMEM((3, 8, WIDTH), F32),
            pltpu.VMEM((LINE, 8, 256), F32),
            pltpu.SemaphoreType.DMA((39,)),
            pltpu.SemaphoreType.DMA((98,)),
            pltpu.SemaphoreType.DMA((14,)),
        ],
        compiler_params=pltpu.CompilerParams(
            collective_id=0, has_side_effects=True, vmem_limit_bytes=60 * 2**20
        ),
    )(
        hidden_in,
        out_grad,
        jnp.transpose(qkv_weight, (1, 0, 2)),
        dense_weight,
        up_weight,
        down_weight,
        jnp.asarray(turn_tables()),
        attn_gain,
        attn_shift,
        mlp_gain,
        mlp_shift,
        dense_bias,
        down_bias,
        span_start,
        span_length,
        qkv_bias,
        up_bias,
    )
    wide = jax.ShapeDtypeStruct((32,), F32)
    finals = pl.pallas_call(
        final_kernel,
        out_shape=(
            jax.ShapeDtypeStruct((128, WIDTH), BF16),
            jax.ShapeDtypeStruct((128, WIDTH), BF16),
            wide,
            wide,
            wide,
            wide,
            jax.ShapeDtypeStruct((3, 64, 512), F32),
            jax.ShapeDtypeStruct((3, 32), F32),
            jax.ShapeDtypeStruct((32, WIDTH), F32),
            wide,
            jax.ShapeDtypeStruct((64, 2048), F32),
            jax.ShapeDtypeStruct((128,), F32),
            jax.ShapeDtypeStruct((128, WIDTH), F32),
            wide,
        ),
        in_specs=[vmem] * 7,
        out_specs=(vmem,) * 14,
    )(*outs)
    return (*finals[:6], jnp.transpose(finals[6], (1, 0, 2)), *finals[7:])


def solution(mesh):
    in_specs = (
        P(("dp", "tensor"), None),
        P(("dp", "tensor"), None),
        P("dp", None),
        P("dp", None),
        P(("dp", "tensor")),
        P(("dp", "tensor")),
        P(("dp", "tensor")),
        P(("dp", "tensor")),
        P("dp", None, "tensor"),
        P(None, ("tensor", "dp")),
        P(("tensor", "dp"), None),
        P(("dp", "tensor")),
        P("dp", "tensor"),
        P(("tensor", "dp")),
        P(("tensor", "dp"), None),
        P(("dp", "tensor")),
    )
    out_specs = (
        P(("dp", "tensor"), None),
        P(("dp", "tensor"), None),
        P(("dp", "tensor")),
        P(("dp", "tensor")),
        P(("dp", "tensor")),
        P(("dp", "tensor")),
        P("dp", None, "tensor"),
        P(None, ("tensor", "dp")),
        P(("tensor", "dp"), None),
        P(("dp", "tensor")),
        P("dp", "tensor"),
        P(("tensor", "dp")),
        P(("tensor", "dp"), None),
        P(("dp", "tensor")),
    )
    fast = mesh.shape["dp"] == 16 and mesh.shape["tensor"] == 2
    return jax.shard_map(plane_layer if fast else shards, mesh=mesh, in_specs=in_specs, out_specs=out_specs, check_vma=False)
```

```python
import jax
import jax.numpy as jnp
import numpy as np
from jax import lax
from jax.experimental import pallas as pl
from jax.experimental.pallas import tpu as pltpu
from jax.sharding import PartitionSpec as P

HD = 64
ROT = 16


NORM_EPS = 1e-05
NEG_FILL = -1000000000.0


def layer_norm(rows_in, gain_vec, shift_vec):
    mean_row = jnp.mean(rows_in, axis=-1, keepdims=True)
    centred = rows_in - mean_row
    spread = jnp.mean(centred * centred, axis=-1, keepdims=True)
    return centred * lax.rsqrt(spread + NORM_EPS) * gain_vec + shift_vec


def rotary_tables(length):
    position = jnp.arange(length, dtype=jnp.float32)
    rates = 10000.0 ** (-jnp.arange(ROT // 2, dtype=jnp.float32) * (2.0 / ROT))
    angles = position[:, None] * rates[None, :]
    angles = jnp.concatenate([angles, angles], axis=-1)[:, None, :]
    return (jnp.cos(angles), jnp.sin(angles))


def rotate(field_in, cosine, sines):
    turned = field_in[..., :ROT]
    first_half = turned[..., : ROT // 2]
    second_half = turned[..., ROT // 2 :]
    swapped = jnp.concatenate([-second_half, first_half], axis=-1)
    return jnp.concatenate([turned * cosine + swapped * sines, field_in[..., ROT:]], axis=-1)


def gelu_exact(values_in):
    return jax.nn.gelu(values_in, approximate=False)


def shards(
    hidden_in,
    out_grad,
    span_start,
    span_length,
    attn_gain,
    attn_shift,
    mlp_gain,
    mlp_shift,
    qkv_weight,
    qkv_bias,
    dense_weight,
    dense_bias,
    up_weight,
    up_bias,
    down_weight,
    down_bias,
):
    local_rows = hidden_in.shape[0]
    length = local_rows * lax.axis_size("tensor")
    block_rows = min(512, length)
    block_count = length // block_rows
    score_scale = HD ** (-0.5)
    small_full = (
        lax.all_gather(attn_gain, ("dp", "tensor"), axis=0, tiled=True),
        lax.all_gather(attn_shift, ("dp", "tensor"), axis=0, tiled=True),
        lax.all_gather(mlp_gain, ("dp", "tensor"), axis=0, tiled=True),
        lax.all_gather(mlp_shift, ("dp", "tensor"), axis=0, tiled=True),
        lax.all_gather(dense_bias, ("dp", "tensor"), axis=0, tiled=True),
        lax.all_gather(down_bias, ("dp", "tensor"), axis=0, tiled=True),
    )
    small_vecs = [item.astype(jnp.float32) for item in small_full]
    own_rows = hidden_in.astype(jnp.float32)
    normed_attn = layer_norm(own_rows, small_vecs[0], small_vecs[1]).astype(jnp.bfloat16)
    normed_mlp = layer_norm(own_rows, small_vecs[2], small_vecs[3]).astype(jnp.bfloat16)
    attn_full, mlp_full = (
        lax.all_gather(normed_attn, "tensor", axis=0, tiled=True),
        lax.all_gather(normed_mlp, "tensor", axis=0, tiled=True),
    )
    full_qkv, full_qkv_bias, full_dense, full_up, full_up_bias, full_down = (
        lax.all_gather(qkv_weight, "dp", axis=0, tiled=True),
        lax.all_gather(qkv_bias, "dp", axis=1, tiled=True),
        lax.all_gather(dense_weight, "dp", axis=0, tiled=True),
        lax.all_gather(up_weight, "dp", axis=0, tiled=True),
        lax.all_gather(up_bias, "dp", axis=0, tiled=True),
        lax.all_gather(down_weight, "dp", axis=0, tiled=True),
    )
    model_width = full_qkv.shape[0]
    head_cols = full_qkv.shape[2]
    local_heads = head_cols // HD
    projected = jnp.dot(
        attn_full, full_qkv.reshape(model_width, 3 * head_cols), preferred_element_type=jnp.float32
    )
    projected = projected + full_qkv_bias.reshape(3 * head_cols).astype(jnp.float32)
    projected = projected.reshape(length, 3, local_heads, HD)
    cosine, sines = rotary_tables(length)
    query_rows = rotate(projected[:, 0], cosine, sines).astype(jnp.bfloat16)
    key_rows = rotate(projected[:, 1], cosine, sines).astype(jnp.bfloat16)
    value_rows = projected[:, 2].astype(jnp.bfloat16)
    position = jnp.arange(length, dtype=jnp.int32)
    starts_here = span_start[0]
    lengths_here = span_length[0]
    inside = (position[None, :] >= starts_here[:, None]) & (
        position[None, :] < (starts_here + lengths_here)[:, None]
    )
    marks = (jnp.arange(starts_here.shape[0], dtype=jnp.int32) + 1)[:, None]
    labels = jnp.sum(jnp.where(inside, marks, 0), axis=0)

    def block_scores(first_row, query_block):
        raw_scores = (
            jnp.einsum("qhe,khe->hqk", query_block, key_rows, preferred_element_type=jnp.float32)
            * score_scale
        )
        row_pos = first_row + jnp.arange(block_rows, dtype=jnp.int32)
        allowed = (position[None, :] <= row_pos[:, None]) | (labels[:, None] == labels[None, :]) & (
            labels[:, None] > 0
        )
        return jnp.where(allowed[None], raw_scores, NEG_FILL)

    def attend(first_row):
        scores = block_scores(first_row, query_rows)
        row_top = jnp.max(scores, axis=-1, keepdims=True)
        exponent = jnp.exp(scores - row_top)
        summed = jnp.sum(exponent, axis=-1, keepdims=True)
        prob_low = (exponent / summed).astype(jnp.bfloat16)
        context_block = jnp.einsum(
            "hqk,khe->qhe", prob_low, value_rows, preferred_element_type=jnp.float32
        )
        return (context_block.astype(jnp.bfloat16), (row_top + jnp.log(summed))[..., 0])

    block_starts = jnp.arange(block_count, dtype=jnp.int32) * block_rows
    context_blocks, lse_blocks = lax.map(attend, block_starts)
    context = context_blocks.reshape(length, head_cols)
    attn_part = jnp.dot(context, full_dense, preferred_element_type=jnp.float32)
    attn_mixed = lax.psum_scatter(
        attn_part.astype(jnp.bfloat16), "tensor", scatter_dimension=0, tiled=True
    ).astype(jnp.float32)
    hidden = jnp.dot(mlp_full, full_up, preferred_element_type=jnp.float32) + full_up_bias.astype(
        jnp.float32
    )
    active = gelu_exact(hidden).astype(jnp.bfloat16)
    mlp_part = jnp.dot(active, full_down, preferred_element_type=jnp.float32)
    mixed_rows = attn_mixed + lax.psum_scatter(
        mlp_part.astype(jnp.bfloat16), "tensor", scatter_dimension=0, tiled=True
    ).astype(jnp.float32)
    layer_out = (own_rows + mixed_rows + small_vecs[4] + small_vecs[5]).astype(jnp.bfloat16)
    cot_full = lax.all_gather(out_grad, "tensor", axis=0, tiled=True)
    full_qkv, full_dense, full_up, full_down = (
        lax.all_gather(qkv_weight, "dp", axis=0, tiled=True),
        lax.all_gather(dense_weight, "dp", axis=0, tiled=True),
        lax.all_gather(up_weight, "dp", axis=0, tiled=True),
        lax.all_gather(down_weight, "dp", axis=0, tiled=True),
    )
    down_grad = jnp.einsum("lf,ld->fd", active, cot_full, preferred_element_type=jnp.float32)
    dense_grad = jnp.einsum("le,ld->ed", context, cot_full, preferred_element_type=jnp.float32)
    active_grad = jnp.einsum("ld,fd->lf", cot_full, full_down, preferred_element_type=jnp.float32)
    hidden_grad = jax.vjp(gelu_exact, hidden)[1](active_grad)[0].astype(jnp.bfloat16)
    up_grad = jnp.einsum("ld,lf->df", mlp_full, hidden_grad, preferred_element_type=jnp.float32)
    up_bias_grad = jnp.sum(hidden_grad, axis=0, dtype=jnp.float32)
    mlp_in_grad = jnp.einsum("lf,df->ld", hidden_grad, full_up, preferred_element_type=jnp.float32)
    context_grad = jnp.einsum("ld,ed->le", cot_full, full_dense, preferred_element_type=jnp.float32)
    context_grad = context_grad.astype(jnp.bfloat16).reshape(length, local_heads, HD)

    def attend_back(carried, inputs):
        key_acc, value_acc = carried
        first_row, lse_block = inputs
        scores = block_scores(first_row, query_rows)
        prob_rows = jnp.exp(scores - lse_block[..., None])
        prob_low = prob_rows.astype(jnp.bfloat16)
        value_acc = value_acc + jnp.einsum(
            "hqk,qhe->khe", prob_low, context_grad, preferred_element_type=jnp.float32
        )
        prob_grad = jnp.einsum(
            "qhe,khe->hqk", context_grad, value_rows, preferred_element_type=jnp.float32
        )
        score_grad = prob_rows * (
            prob_grad - jnp.sum(prob_grad * prob_rows, axis=-1, keepdims=True)
        )
        score_grad = score_grad.astype(jnp.bfloat16)
        query_grad = (
            jnp.einsum("hqk,khe->qhe", score_grad, key_rows, preferred_element_type=jnp.float32)
            * score_scale
        )
        key_acc = (
            key_acc
            + jnp.einsum("hqk,qhe->khe", score_grad, query_rows, preferred_element_type=jnp.float32)
            * score_scale
        )
        return ((key_acc, value_acc), query_grad)

    zero_rows = jnp.zeros((length, local_heads, HD), jnp.float32)
    (key_grad, value_grad), query_blocks = lax.scan(
        attend_back, (zero_rows, zero_rows), (block_starts, lse_blocks)
    )
    query_grad = query_blocks.reshape(length, local_heads, HD)

    def turn(field_in):
        return rotate(field_in, cosine, sines)

    turn_back = jax.vjp(turn, zero_rows)[1]
    projected_grad = jnp.stack(
        [turn_back(query_grad)[0], turn_back(key_grad)[0], value_grad], axis=1
    )
    projected_grad = projected_grad.astype(jnp.bfloat16).reshape(length, 3 * head_cols)
    qkv_weight_grad = jnp.einsum(
        "ld,lc->dc", attn_full, projected_grad, preferred_element_type=jnp.float32
    )
    qkv_weight_grad = qkv_weight_grad.reshape(model_width, 3, head_cols)
    qkv_bias_grad = jnp.sum(projected_grad, axis=0, dtype=jnp.float32).reshape(3, head_cols)
    attn_in_grad = jnp.einsum(
        "lc,dc->ld",
        projected_grad,
        full_qkv.reshape(model_width, 3 * head_cols),
        preferred_element_type=jnp.float32,
    )
    reduced = (
        lax.psum_scatter(qkv_weight_grad, "dp", scatter_dimension=0, tiled=True),
        lax.psum_scatter(qkv_bias_grad, "dp", scatter_dimension=1, tiled=True),
        lax.psum_scatter(dense_grad, "dp", scatter_dimension=0, tiled=True),
        lax.psum_scatter(up_grad, "dp", scatter_dimension=0, tiled=True),
        lax.psum_scatter(up_bias_grad, "dp", scatter_dimension=0, tiled=True),
        lax.psum_scatter(down_grad, "dp", scatter_dimension=0, tiled=True),
    )
    attn_local, mlp_local = (
        lax.psum_scatter(
            attn_in_grad.astype(jnp.bfloat16), "tensor", scatter_dimension=0, tiled=True
        ).astype(jnp.float32),
        lax.psum_scatter(
            mlp_in_grad.astype(jnp.bfloat16), "tensor", scatter_dimension=0, tiled=True
        ).astype(jnp.float32),
    )
    pull_attn = jax.vjp(layer_norm, own_rows, small_vecs[0], small_vecs[1])[1]
    pull_mlp = jax.vjp(layer_norm, own_rows, small_vecs[2], small_vecs[3])[1]
    rows_grad_attn, gain_grad_attn, shift_grad_attn = pull_attn(attn_local)
    rows_grad_mlp, gain_grad_mlp, shift_grad_mlp = pull_mlp(mlp_local)
    cot_rows = out_grad.astype(jnp.float32)
    input_grad = (cot_rows + rows_grad_attn + rows_grad_mlp).astype(jnp.bfloat16)
    bias_total = jnp.sum(cot_rows, axis=0)
    small_sums = (
        lax.psum_scatter(gain_grad_attn, ("dp", "tensor"), scatter_dimension=0, tiled=True),
        lax.psum_scatter(shift_grad_attn, ("dp", "tensor"), scatter_dimension=0, tiled=True),
        lax.psum_scatter(gain_grad_mlp, ("dp", "tensor"), scatter_dimension=0, tiled=True),
        lax.psum_scatter(shift_grad_mlp, ("dp", "tensor"), scatter_dimension=0, tiled=True),
        lax.psum_scatter(bias_total, ("dp", "tensor"), scatter_dimension=0, tiled=True),
    )
    return (
        layer_out,
        input_grad,
        small_sums[0],
        small_sums[1],
        small_sums[2],
        small_sums[3],
        reduced[0],
        reduced[1],
        reduced[2],
        small_sums[4],
        reduced[3],
        reduced[4],
        reduced[5],
        small_sums[4],
    )


F32 = jnp.float32
BF16 = jnp.bfloat16
MESH_ID = pl.DeviceIdType.MESH
LINE = 4
SEQ = 256
WIDTH = 1024
HID = 512
PAIR = 128


def nn(a, b):
    return jnp.dot(a, b, preferred_element_type=F32)


def nt(a, b):
    return lax.dot_general(a, b, (((1,), (1,)), ((), ())), preferred_element_type=F32)


def tn(a, b):
    return lax.dot_general(a, b, (((0,), (0,)), ((), ())), preferred_element_type=F32)


def turn_tables():
    position = np.arange(SEQ, dtype=np.float64)[:, None]
    lane = np.arange(PAIR) % HD
    rates = 10000.0 ** (-(lane % (ROT // 2)) * (2.0 / ROT))
    angles = position * rates[None, :]
    cosine = np.where(lane < ROT, np.cos(angles), 1.0)
    toward = np.where(lane < ROT // 2, -np.sin(angles), 0.0)
    away = np.where((lane >= ROT // 2) & (lane < ROT), np.sin(angles), 0.0)
    return np.stack([cosine, toward, away]).astype(np.float32)


SEATS = (0, 3, 1, 2)


def seat_of(z):
    return (2 * z - z // 2) % LINE


def rows_of(index, count):
    return pl.ds(pl.multiple_of(index * count, count), count)


class Place:
    def __init__(self):
        index = lax.axis_index("dp")
        self.t = lax.axis_index("tensor")
        self.z = index // 4
        self.k = index % 4
        self.y = self.k // 2
        self.c = self.k % 2
        self.kc = self.y * 2 + 1 - self.c
        self.ky = (1 - self.y) * 2 + self.c
        self.kyc = (1 - self.y) * 2 + 1 - self.c
        self.q = self.k * 2 + self.t
        self.core = self.at(self.z, self.kc, self.t)
        self.cross = (
            self.at(self.z, self.k, 1 - self.t),
            self.at(self.z, self.ky, self.t),
            self.at(self.z, self.ky, 1 - self.t),
        )

    def at(self, z, k, t):
        return (z * 4 + k, t)

    def line(self, z):
        return self.at(z, self.k, self.t)


class Wires:
    def __init__(self, sends, arrivals):
        self.sends, self.arrivals = sends, arrivals
        self.sent, self.landed = 0, 0

    def take(self, sends, arrivals):
        first = (self.sent, self.landed)
        self.sent += sends
        self.landed += arrivals
        return first

    def copy(self, send, arrival, src, dst, device):
        return pltpu.make_async_remote_copy(
            src_ref=src,
            dst_ref=dst,
            send_sem=self.sends.at[send],
            recv_sem=self.arrivals.at[arrival],
            device_id=device,
            device_id_type=MESH_ID,
        )

    def all_sent(self, send, view, device):
        self.copy(send, 0, view, view, device).wait_send()

    def all_landed(self, arrival, view, device):
        self.copy(0, arrival, view, view, device).wait_recv()


class PlaneGather:
    def __init__(self, me, wires, src, slot, split, blocks):
        self.me, self.wires, self.src, self.slot = me, wires, src, slot
        self.blocks = blocks
        self.pieces = (pl.ds(0, split), pl.ds(split, src.shape[0] - split))
        self.send, self.arrivals = wires.take(1, 4)
        self.near_blocks = (
            me.k * 2 + 1 - me.t,
            me.ky * 2 + me.t,
            me.ky * 2 + 1 - me.t,
        )

    def start(self, which):
        device = (self.me.cross[0], self.me.cross[1], self.me.core)[which]
        arrival = self.arrivals + (0, 1, 3)[which]
        self.wires.copy(self.send, arrival, self.src, self.slot(self.me.q), device).start()

    def pass_on(self, which):
        part = self.slot(self.near_blocks[which])
        self.wires.copy(self.send, self.arrivals + 3, part, part, self.me.core).start()

    def forward(self, which):
        block = self.slot(self.near_blocks[which])
        self.wires.all_landed(self.arrivals + which, block, self.me.core)
        part = block.at[self.pieces[which]]
        device = self.me.cross[1 - which]
        self.wires.copy(self.send, self.arrivals + 2, part, part, device).start()
        self.pass_on(which)

    def corner(self):
        block = self.slot(self.near_blocks[2])
        self.wires.all_landed(self.arrivals + 2, block, self.me.core)
        self.pass_on(2)

    def finish(self):
        self.wires.all_landed(self.arrivals + 3, self.blocks(4), self.me.core)

    def drain(self):
        self.wires.all_sent(self.send, self.blocks(7), self.me.core)


class LineGather:
    def __init__(self, me, wires, view):
        self.me, self.wires, self.view = me, wires, view
        self.sends, self.arrivals = wires.take(2, 6)

    def copy(self, way, hop, block):
        z = self.me.z
        view = self.view(block, 1)
        device = self.me.line(z + 1 if way == 0 else z - 1)
        return self.wires.copy(self.sends + way, self.arrivals + way * 3 + hop, view, view, device)

    def send(self, way, hop):
        z = self.me.z
        has = (z >= hop) & (z < LINE - 1) if way == 0 else (z + hop < LINE) & (z > 0)

        @pl.when(has)
        def _():
            self.copy(way, hop, z - hop if way == 0 else z + hop).start()

    def arrive(self, way, hop):
        z = self.me.z

        @pl.when(z > hop if way == 0 else z + 1 + hop < LINE)
        def _():
            self.copy(way, hop, z - 1 - hop if way == 0 else z + 1 + hop).wait_recv()

    def start(self, way):
        @pl.when(self.me.z != (0 if way == 0 else LINE - 1))
        def _():
            self.send(way, 0)

    def outer(self):
        for way in range(2):

            @pl.when(self.me.z == (0 if way == 0 else LINE - 1))
            def _(way=way):
                self.send(way, 0)

    def relay(self, way, hop):
        self.arrive(way, hop - 1)
        self.send(way, hop)

    def finish(self, way):
        self.arrive(way, LINE - 2)

    def drain(self):
        z = self.me.z
        for way in range(2):
            for count in range(1, LINE):

                @pl.when(z == (count - 1 if way == 0 else LINE - count))
                def _():
                    self.wires.all_sent(self.sends + way, self.view(0, count), self.me.core)


class LineReduce:
    def __init__(self, me, wires, held, landed):
        self.me, self.wires, self.held, self.landed = me, wires, held, landed
        self.sends, self.arrivals = wires.take(2, 6)

    def copy(self, way, block):
        z = self.me.z
        device = self.me.line(z - 1 if way == 0 else z + 1)
        return self.wires.copy(
            self.sends + way,
            self.arrivals + way * (LINE - 2) + block,
            self.held.at[block],
            self.landed.at[way, block],
            device,
        )

    def join(self, way, block):
        self.copy(way, block).wait_recv()
        total = self.held[block].astype(F32) + self.landed[way, block].astype(F32)
        self.held[block] = total.astype(BF16)

    def each(self, way, slot, act):
        z = self.me.z
        steps = slot - (LINE - 1 - z if way == 0 else z)
        left = z if way == 0 else LINE - 1 - z
        block = steps if way == 0 else LINE - 1 - steps

        @pl.when((steps >= 0) & (steps < left))
        def _():
            act(block)

    def slot(self, way, slot):
        def act(block):
            if slot > 0:
                started = self.me.z < LINE - 1 if way == 0 else self.me.z > 0

                @pl.when(started)
                def _():
                    self.join(way, block)

            self.copy(way, block).start()

        self.each(way, slot, act)

    def finish(self, way):
        z = self.me.z

        @pl.when(z < LINE - 1 if way == 0 else z > 0)
        def _():
            self.join(way, z)

    def drain(self):
        z = self.me.z
        for way in range(2):
            for count in range(1, LINE):

                @pl.when(z == (count if way == 0 else LINE - 1 - count))
                def _():
                    view = self.held.at[pl.ds(0, count)]
                    self.wires.all_sent(self.sends + way, view, self.me.core)


class PlaneReduce:
    def __init__(self, me, wires, part, paired, crossed):
        self.me, self.wires = me, wires
        self.part, self.paired, self.crossed = part, paired, crossed
        self.send, self.arrivals = wires.take(1, 4)
        self.blocks = (me.ky * 2 + 1 - me.t, me.k * 2 + 1 - me.t, me.ky * 2 + me.t)

    def pair(self, y):
        rows = rows_of(y * 2 + 1 - self.me.c, SEQ)
        return self.wires.copy(
            self.send, self.arrivals, self.part.at[rows], self.paired.at[y], self.me.core
        )

    def rows(self, which, half):
        first = pl.multiple_of(self.blocks[which] * 128 + half * 64, 64)
        return pl.ds(first, 64)

    def cross(self, which, half):
        way = (half, 0, 1)[which]
        return self.wires.copy(
            self.send,
            self.arrivals + (1 + half if which == 0 else 3),
            self.part.at[self.rows(which, half)],
            self.crossed.at[which, pl.ds(half * 64, 64)],
            self.me.cross[way],
        )

    def middle(self):
        self.wires.all_landed(self.arrivals, self.part.at[pl.ds(0, 2 * SEQ)], self.me.core)
        for y in range(2):
            rows = rows_of(y * 2 + self.me.c, SEQ)
            total = self.part[rows].astype(F32) + self.paired[y].astype(F32)
            self.part[rows] = total.astype(BF16)
        for which, half in ((0, 0), (0, 1), (1, 0), (2, 1)):
            self.cross(which, half).start()

    def turn(self, half):
        self.cross(0, half).wait_recv()
        rows = self.rows(2 - half, half)
        total = self.part[rows].astype(F32) + self.crossed[0, pl.ds(half * 64, 64)].astype(F32)
        self.part[rows] = total.astype(BF16)
        self.cross(2 - half, half).start()

    def finish(self):
        self.wires.all_landed(self.arrivals + 3, self.part.at[pl.ds(0, SEQ)], self.me.core)
        total = self.part[rows_of(self.me.q, 128)].astype(F32)
        return total + self.crossed[1].astype(F32) + self.crossed[2].astype(F32)

    def drain(self):
        self.wires.all_sent(self.send, self.part.at[pl.ds(0, 896)], self.me.core)


def layer_kernel(
    x_hbm,
    g_hbm,
    qkv_hbm,
    dense_hbm,
    up_hbm,
    down_hbm,
    turn_hbm,
    attn_gain_ref,
    attn_shift_ref,
    mlp_gain_ref,
    mlp_shift_ref,
    dense_bias_ref,
    down_bias_ref,
    starts_ref,
    lengths_ref,
    qkv_bias_ref,
    up_bias_ref,
    layer_out_ref,
    input_grad_ref,
    qkv_grad_ref,
    dense_grad_ref,
    up_grad_ref,
    down_grad_ref,
    small_out_ref,
    turn_ref,
    x_all,
    g_all,
    small_line,
    small_all,
    qkv_w,
    dense_w,
    up_w,
    down_w,
    vec_ref,
    bias_ref,
    normed_a,
    normed_m,
    context_ref,
    turned_grad,
    active_ref,
    hidden_grad,
    slope_ref,
    part_out,
    part_attn,
    part_mlp,
    paired_ref,
    crossed_ref,
    up_held,
    up_landed,
    down_held,
    down_landed,
    late_held,
    late_landed,
    qkv_held,
    qkv_landed,
    up_final,
    qkv_final,
    dense_line,
    dense_held,
    dense_mine,
    dense_landed,
    qkv_bias_held,
    qkv_bias_line,
    qkv_bias_final,
    up_bias_held,
    up_bias_final,
    sums_held,
    sums_chip,
    sums_total,
    sums_core,
    sums_cross,
    sums_line,
    sends,
    arrivals,
    local_sems,
):
    me = Place()
    wires = Wires(sends, arrivals)
    z, k, t = me.z, me.k, me.t

    barrier = pltpu.get_barrier_semaphore()

    def greet(device):
        pl.semaphore_signal(barrier, inc=1, device_id=device, device_id_type=MESH_ID)

    greet(me.core)
    greet(me.at(z, me.kyc, t))
    for device in me.cross:
        greet(device)
    for step in range(1, LINE):
        greet(me.line((z + step) % LINE))
    local_copies = []

    def local(src, dst):
        copy = pltpu.make_async_copy(src, dst, local_sems.at[len(local_copies)])
        local_copies.append(copy)
        copy.start()

    seat = pl.ds(pl.multiple_of(z * 256 + k * 64, 64), 64)
    peers = (me.kc, me.ky, me.kyc)
    devices = tuple(me.at(z, peer, t) for peer in peers)

    def three(arrival, view):
        wires.all_landed(arrival, view, me.core)

    local(dense_hbm, dense_line.at[z])
    for place, other in enumerate(SEATS):
        local(
            up_hbm.at[:, rows_of(other * 4 + k, 128)],
            up_w.at[seat, pl.ds(place * 128, 128)],
        )
    local(down_hbm, down_w.at[rows_of(seat_of(z), 128)])
    for which in range(3):
        local(
            qkv_hbm.at[which, :, rows_of(k, PAIR)],
            qkv_w.at[seat, pl.ds(which * PAIR, PAIR)],
        )
    local(x_hbm, x_all.at[rows_of(me.q, 128)])
    local(g_hbm, g_all.at[rows_of(me.q, 128)])
    local(turn_hbm, turn_ref)
    qkv_bias_held[...] = jnp.zeros_like(qkv_bias_held)
    up_bias_held[...] = jnp.zeros_like(up_bias_held)

    def side_by_side(*fields):
        return jnp.concatenate(
            [field.astype(F32).reshape(1, field.shape[-1]) for field in fields], axis=1
        )

    triple = qkv_bias_ref[...]
    blank = jnp.zeros((1, 60), F32)
    small_line[z] = jnp.concatenate(
        [
            side_by_side(
                attn_gain_ref[...], attn_shift_ref[...], mlp_gain_ref[...], mlp_shift_ref[...]
            ),
            side_by_side(
                dense_bias_ref[...], down_bias_ref[...], starts_ref[...], lengths_ref[...], blank
            ),
            side_by_side(triple[0:1], triple[1:2], triple[2:3], blank[:, :32]),
            side_by_side(up_bias_ref[...]),
            jnp.zeros((4, 128), F32),
        ],
        axis=0,
    )
    pl.semaphore_wait(barrier, 8)

    up_send, up_arrival = wires.take(1, 2)
    for place, other in enumerate(SEATS):
        for which in range(3):
            wires.copy(
                up_send,
                up_arrival + place // 2,
                up_hbm.at[:, rows_of(other * 4 + peers[which], 128)],
                up_w.at[seat, pl.ds(place * 128, 128)],
                devices[which],
            ).start()

    qkv_sends, qkv_arrival = wires.take(1, 1)

    def rows_slot(ref):
        return (lambda block: ref.at[rows_of(block, 128)]), (
            lambda count: ref.at[pl.ds(0, count * 128)]
        )

    slot, blocks = rows_slot(x_all)
    gather_x = PlaneGather(me, wires, x_hbm, slot, 48, blocks)
    for which in range(3):
        gather_x.start(which)
    slot, blocks = rows_slot(g_all)
    gather_g = PlaneGather(me, wires, g_hbm, slot, 48, blocks)
    gather_small = PlaneGather(
        me,
        wires,
        small_line,
        lambda block: small_all.at[block],
        2,
        lambda count: small_all.at[pl.ds(0, count)],
    )
    small_send, small_arrival = wires.take(1, 1)
    for step in range(1, LINE):
        wires.copy(
            small_send,
            small_arrival,
            small_line.at[z],
            small_line.at[z],
            me.line((z + step) % LINE),
        ).start()

    def line_gather(ref, count):
        return LineGather(
            me, wires, lambda s, n: ref.at[pl.ds(pl.multiple_of(s * count, count), n * count)]
        )

    line_dense = LineGather(me, wires, lambda s, n: dense_line.at[pl.ds(s, n)])
    line_qkv = line_gather(qkv_w, 256)
    line_upa, line_upb = (
        LineGather(
            me,
            wires,
            lambda s, n, first=first: up_w.at[
                pl.ds(pl.multiple_of(s * 256, 256), n * 256), pl.ds(first, 256)
            ],
        )
        for first in (0, 256)
    )
    line_down = LineGather(
        me,
        wires,
        lambda s, n: down_w.at[pl.ds(pl.multiple_of(seat_of(s) * 128, 128), n * 128)],
    )
    reduce_down = LineReduce(
        me, wires, down_held, down_landed
    )
    reduce_late = LineReduce(
        me, wires, late_held, late_landed
    )
    reduce_up = LineReduce(
        me, wires, up_held, up_landed
    )
    reduce_qkv = LineReduce(
        me, wires, qkv_held, qkv_landed
    )
    reduce_dense = LineReduce(
        me, wires, dense_mine, dense_landed
    )
    reduce_attn = PlaneReduce(me, wires, part_attn, paired_ref.at[0], crossed_ref.at[0])
    reduce_out = PlaneReduce(me, wires, part_out, paired_ref.at[1], crossed_ref.at[1])
    reduce_mlp = PlaneReduce(me, wires, part_mlp, paired_ref.at[2], crossed_ref.at[2])

    local_copies[0].wait()
    line_dense.outer()
    line_dense.start(0)
    line_dense.start(1)

    own_small = pltpu.make_async_copy(
        small_line, small_all.at[me.q], local_sems.at[len(local_copies)]
    )
    own_dense = pltpu.make_async_copy(
        dense_line.at[k], dense_w.at[rows_of(k, 32)], local_sems.at[len(local_copies) + 1]
    )
    dense_sends, dense_arrival = wires.take(1, 1)
    back_sends, back_arrival = wires.take(2, 2)
    bias_sends, bias_arrival = wires.take(2, 2)
    out_sends, out_arrival = wires.take(2, 2)
    sums_sends, sums_arrival = wires.take(3, 3)

    def along(send, arrival, source, target):
        for step in range(1, LINE):
            there = (z + step) % LINE
            wires.copy(send, arrival, source(there), target, me.line(there)).start()

    def around(send, arrival, source, target):
        for which in range(3):
            wires.copy(send, arrival, source(peers[which]), target, devices[which]).start()

    def norm_rows(rows):
        values = x_all[rows].astype(F32)
        centred = values - jnp.mean(values, axis=-1, keepdims=True)
        rate = lax.rsqrt(jnp.mean(centred * centred, axis=-1, keepdims=True) + NORM_EPS)
        return centred * rate, rate

    def norm_block(block, carry):
        rows = rows_of(block, 128)
        unit, _ = norm_rows(rows)
        normed_m[rows] = (unit * vec_ref[2:3, :] + vec_ref[3:4, :]).astype(BF16)
        return carry

    def attn_norm(block, carry):
        rows = rows_of(block, 128)
        unit, _ = norm_rows(rows)
        normed_a[rows] = (unit * vec_ref[0:1, :] + vec_ref[1:2, :]).astype(BF16)
        return carry

    def activate(half):
        columns = slice(half * 256, (half + 1) * 256)

        def tile_of(tile, carry):
            rows = rows_of(tile, 256)
            up_bias = jnp.concatenate(
                [small_all[me.q, s, 3:4, :] for s in SEATS[half * 2 : half * 2 + 2]], axis=1
            )
            hidden = nn(normed_m[rows], up_w[:, columns]) + up_bias
            share = (1.0 + lax.erf(hidden * 0.5**0.5)) * 0.5
            bell = jnp.exp(hidden * hidden * -0.5) * (2.0 * np.pi) ** -0.5
            slope_ref[rows, columns] = share + hidden * bell
            active_ref[rows, columns] = (hidden * share).astype(BF16)
            return carry

        return tile_of

    activate_a, activate_b = activate(0), activate(1)

    def down_block(block, carry):
        units = rows_of(seat_of(block), 128)
        grad = tn(active_ref[:, units], g_all[...]).astype(BF16)
        down_held[block] = grad[:64]
        late_held[block] = grad[64:]
        return carry

    def feed_back(tile, carry):
        rows = rows_of(tile, 256)
        grad = (nt(g_all[rows], down_w[...]) * slope_ref[rows]).astype(BF16)
        hidden_grad[rows] = grad
        up_bias_held[0:1, :] += jnp.sum(grad.astype(F32), axis=0, keepdims=True)
        return carry

    def feed_in(tile, carry):
        rows = rows_of(tile, 256)
        part_mlp[rows] = nt(hidden_grad[rows], up_w[...]).astype(BF16)
        return carry

    def up_block(block, carry):
        up_held[block] = tn(normed_m[:, rows_of(block, 256)], hidden_grad[...]).astype(BF16)
        return carry

    scale = HD**-0.5

    def attend(seq, carry):
        rows = rows_of(seq, SEQ)
        cosine, toward, away = turn_ref[0], turn_ref[1], turn_ref[2]
        projected = nn(normed_a[rows], qkv_w[...]) + bias_ref[0:1, :]

        def project(which):
            return projected[:, which * PAIR : (which + 1) * PAIR]

        def turned(field):
            return (
                field * cosine
                + pltpu.roll(field, ROT // 2, 1) * away
                + pltpu.roll(field, PAIR - ROT // 2, 1) * toward
            )

        def turned_back(field):
            return (
                field * cosine
                - pltpu.roll(field, ROT // 2, 1) * away
                - pltpu.roll(field, PAIR - ROT // 2, 1) * toward
            )

        query = turned(project(0)).astype(BF16)
        key = turned(project(1)).astype(BF16)
        value = project(2).astype(BF16)
        context_grad = nt(g_all[rows], dense_w[...]).astype(BF16)

        spans = small_all[seq * 2, z, 1:2, :]
        down_pos = lax.broadcasted_iota(jnp.int32, (SEQ, 1), 0).astype(F32)
        over_pos = lax.broadcasted_iota(jnp.int32, (1, SEQ), 1).astype(F32)

        def labels(place):
            total = jnp.zeros(place.shape, F32)
            for span in range(2):
                begin = spans[:, 64 + span : 65 + span]
                end = begin + spans[:, 66 + span : 67 + span]
                total = total + jnp.where((place >= begin) & (place < end), span + 1.0, 0.0)
            return total

        down_label, over_label = labels(down_pos), labels(over_pos)
        allowed = (over_pos <= down_pos) | ((down_label == over_label) & (down_label > 0.0))

        lane = lax.broadcasted_iota(jnp.int32, (SEQ, PAIR), 1)
        parts = []
        for head in range(2):
            mine = (lane >= HD) if head else (lane < HD)
            zero = jnp.zeros_like(query)
            scores = nt(jnp.where(mine, query, zero), key) * scale
            scores = jnp.where(allowed, scores, NEG_FILL)
            exponent = jnp.exp(scores - jnp.max(scores, axis=-1, keepdims=True))
            probs = exponent * (1.0 / jnp.sum(exponent, axis=-1, keepdims=True))
            low = probs.astype(BF16)
            prob_grad = nt(jnp.where(mine, context_grad, zero), value)
            inner = jnp.sum(prob_grad * probs, axis=-1, keepdims=True)
            score_grad = (probs * (prob_grad - inner)).astype(BF16)
            parts.append(
                (
                    nn(low, value),
                    tn(low, context_grad),
                    nn(score_grad, key) * scale,
                    tn(score_grad, query) * scale,
                )
            )
        context, value_grad, query_grad, key_grad = (
            jnp.where(lane < HD, first, second) for first, second in zip(*parts)
        )
        context_ref[rows] = context.astype(BF16)
        grads = (
            turned_back(query_grad).astype(BF16),
            turned_back(key_grad).astype(BF16),
            value_grad.astype(BF16),
        )
        for which in range(3):
            turned_grad[rows, which * PAIR : (which + 1) * PAIR] = grads[which]
            qkv_bias_held[which : which + 1, :] += jnp.sum(
                grads[which].astype(F32), axis=0, keepdims=True
            )
        return carry

    def attend_in(tile, carry):
        rows = rows_of(tile, 256)
        part_attn[rows] = nt(turned_grad[rows], qkv_w[...]).astype(BF16)
        return carry

    def qkv_block(block, carry):
        qkv_held[block] = tn(normed_a[:, rows_of(block, 256)], turned_grad[...]).astype(BF16)
        return carry

    def mix(tile, carry):
        rows = rows_of(tile, 256)
        mixed = nn(context_ref[rows], dense_w[...]) + nn(active_ref[rows], down_w[...])
        part_out[rows] = mixed.astype(BF16)
        return carry

    def locals_done():
        for copy in local_copies[1:]:
            copy.wait()

    def small_line_done():
        three(small_arrival, small_line.at[pl.ds(0, 3)])
        own_small.start()
        for which in range(3):
            gather_small.start(which)

    def upa_start():
        three(up_arrival, up_w.at[pl.ds(0, 96)])
        line_upa.outer()
        line_upa.start(0)
        line_upa.start(1)

    def upb_start():
        three(up_arrival + 1, up_w.at[pl.ds(0, 96)])
        line_upb.outer()
        line_upb.start(0)
        line_upb.start(1)

    def down_outer():
        line_down.outer()

    def qkv_send():
        for which in range(3):
            for part in range(3):
                wires.copy(
                    qkv_sends,
                    qkv_arrival,
                    qkv_hbm.at[part, :, rows_of(peers[which], PAIR)],
                    qkv_w.at[seat, pl.ds(part * PAIR, PAIR)],
                    devices[which],
                ).start()

    def qkv_outer():
        three(qkv_arrival, qkv_w.at[pl.ds(0, 192)])
        line_qkv.outer()

    def qkv_start():
        line_qkv.start(0)
        line_qkv.start(1)

    def down_start():
        line_down.start(0)
        line_down.start(1)

    def dense_send():
        around(
            dense_sends, dense_arrival, lambda to: dense_line.at[to], dense_w.at[rows_of(k, 32)]
        )
        own_dense.start()

    def dense_done():
        three(dense_arrival, dense_w.at[pl.ds(0, 96)])
        own_dense.wait()

    def spread_table(kind, width):
        table = small_all[...].reshape(256, 128).astype(BF16)
        line_id = lax.broadcasted_iota(jnp.int32, (256, width), 0)
        column = lax.broadcasted_iota(jnp.int32, (256, width), 1)
        from_z, from_q = (line_id >> 3) & 3, line_id >> 5
        if width == WIDTH:
            chosen = from_z * 8 + from_q == column >> 5
        else:
            chosen = (from_z == k) & (from_q == (column >> 5) * 2 + t)
        chosen = chosen & ((line_id & 7) == kind)
        spread = tn(table, jnp.where(chosen, 1.0, 0.0).astype(BF16))
        lane_row = lax.broadcasted_iota(jnp.int32, (128, width), 0)
        lane_col = lax.broadcasted_iota(jnp.int32, (128, width), 1) & 31

        def vector(which):
            picked = jnp.where(lane_row == lane_col + which * 32, spread, 0.0)
            return jnp.sum(picked, axis=0, keepdims=True)

        return vector

    def vectors():
        own_small.wait()
        vector = spread_table(0, WIDTH)
        for which in range(4):
            vec_ref[which : which + 1, :] = vector(which)

    def more_vectors():
        vector = spread_table(1, WIDTH)
        for which in range(2):
            vec_ref[4 + which : 5 + which, :] = vector(which)
        vector = spread_table(2, PAIR)
        for which in range(3):
            bias_ref[0:1, which * PAIR : (which + 1) * PAIR] = vector(which)

    def up_bias_send():
        along(
            bias_sends,
            bias_arrival,
            lambda there: up_bias_held.at[:, rows_of(seat_of(there), 128)],
            up_bias_final.at[z],
        )
        up_bias_final[z] = up_bias_held[:, rows_of(seat_of(z), 128)]

    def dense_part():
        dense_held[...] = tn(context_ref[...], g_all[...]).astype(BF16)
        around(
            back_sends, back_arrival, lambda to: dense_held.at[rows_of(to, 32)], dense_mine.at[k]
        )
        around(back_sends + 1, back_arrival + 1, lambda to: qkv_bias_held, qkv_bias_line.at[k])
        dense_mine[k] = dense_held[rows_of(k, 32)]
        qkv_bias_line[k] = qkv_bias_held[...]

    def dense_back():
        three(back_arrival, dense_mine.at[pl.ds(0, 3)])
        three(back_arrival + 1, qkv_bias_line.at[pl.ds(0, 3)])
        along(
            bias_sends + 1,
            bias_arrival + 1,
            lambda there: qkv_bias_line.at[there],
            qkv_bias_final.at[z],
        )
        qkv_bias_final[z] = qkv_bias_line[z]

    def up_out():
        around(
            out_sends, out_arrival, lambda to: up_held.at[z, rows_of(to, 64)], up_final.at[k]
        )
        up_final[k] = up_held[z, rows_of(k, 64)]

    def qkv_out():
        around(
            out_sends + 1,
            out_arrival + 1,
            lambda to: qkv_held.at[z, rows_of(to, 64)],
            qkv_final.at[k],
        )
        qkv_final[k] = qkv_held[z, rows_of(k, 64)]

    def down_out():
        down_grad_ref[0:64, :] = down_held[z]
        down_grad_ref[64:128, :] = late_held[z]

    def dense_out():
        dense_grad_ref[...] = dense_mine[z]

    def up_result():
        three(out_arrival, up_final.at[pl.ds(0, 3)])
        up_grad_ref[...] = up_final[...]

    def qkv_result():
        three(out_arrival + 1, qkv_final.at[pl.ds(0, 3)])
        qkv_grad_ref[...] = qkv_final[...]

    own = rows_of(me.q, 128)
    def layer_out():
        mixed = reduce_out.finish()
        layer_out_ref[...] = (
            x_all[own].astype(F32) + mixed + vec_ref[4:5, :] + vec_ref[5:6, :]
        ).astype(BF16)

    def norm_grads():
        from_attn = reduce_attn.finish()
        from_mlp = reduce_mlp.finish()
        cotangent = g_all[own].astype(F32)
        unit, rate = norm_rows(own)
        sums_held[...] = jnp.zeros_like(sums_held)
        for which, field in enumerate(
            (from_attn * unit, from_attn, from_mlp * unit, from_mlp, cotangent)
        ):
            sums_held[which : which + 1, :] = jnp.sum(field, axis=0, keepdims=True)
        wires.copy(sums_sends, sums_arrival, sums_held, sums_core, me.core).start()
        pulled = from_attn * vec_ref[0:1, :] + from_mlp * vec_ref[2:3, :]
        pulled = (
            pulled
            - jnp.mean(pulled, axis=-1, keepdims=True)
            - unit * jnp.mean(pulled * unit, axis=-1, keepdims=True)
        )
        input_grad_ref[...] = (cotangent + rate * pulled).astype(BF16)

    def sums_plane():
        three(sums_arrival, sums_core)
        sums_chip[...] = sums_held[...] + sums_core[...]
        for which in range(3):
            wires.copy(
                sums_sends + 1,
                sums_arrival + 1,
                sums_chip,
                sums_cross.at[which],
                me.cross[which],
            ).start()

    def sums_send():
        three(sums_arrival + 1, sums_cross)
        sums_total[...] = sums_chip[...] + sums_cross[0] + sums_cross[1] + sums_cross[2]
        along(
            sums_sends + 2,
            sums_arrival + 2,
            lambda there: sums_total.at[:, rows_of(there, 256)],
            sums_line.at[z],
        )
        sums_line[z] = sums_total[:, rows_of(z, 256)]

    def small_result():
        three(sums_arrival + 2, sums_line.at[pl.ds(0, 3)])
        three(bias_arrival, up_bias_final.at[pl.ds(0, 3)])
        three(bias_arrival + 1, qkv_bias_final.at[pl.ds(0, 3)])
        sums = sums_line[0] + sums_line[1] + sums_line[2] + sums_line[3]
        sums = jnp.where(k >= 2, sums[:, 128:], sums[:, :128])
        small_out_ref[0:8, :] = pltpu.roll(sums, (128 - (me.q % 4) * 32) % 128, 1)
        bias_sum = qkv_bias_final[0] + qkv_bias_final[1] + qkv_bias_final[2] + qkv_bias_final[3]
        small_out_ref[8:16, :] = pltpu.roll(bias_sum, (128 - k * 32) % 128, 1)
        small_out_ref[16:24, :] = (
            up_bias_final[0] + up_bias_final[1] + up_bias_final[2] + up_bias_final[3]
        )

    def ends_of(body):
        def outer(index, carry):
            return body(index * (LINE - 1), carry)

        return outer

    locals_done()
    upa_start()
    line_dense.relay(1, 1)
    upb_start()
    small_line_done()
    gather_g.start(0)
    line_dense.relay(0, 1)
    line_dense.relay(1, 2)
    line_upa.relay(0, 1)
    gather_small.forward(0)
    qkv_send()
    line_upa.relay(1, 1)
    gather_x.forward(0)
    line_upb.relay(0, 1)
    gather_x.forward(1)
    gather_small.forward(1)
    qkv_outer()
    down_outer()
    line_upb.relay(1, 1)
    line_dense.finish(1)
    line_dense.relay(0, 2)
    gather_g.start(1)
    line_upa.relay(0, 2)
    qkv_start()
    gather_small.corner()
    gather_x.corner()
    gather_x.finish()
    gather_small.finish()
    vectors()
    line_upb.relay(0, 2)
    gather_g.forward(0)
    line_dense.finish(0)
    line_upa.finish(0)
    line_upb.relay(1, 2)
    line_upa.relay(1, 2)
    lax.fori_loop(4, 8, attn_norm, 0)
    gather_g.start(2)
    lax.fori_loop(0, 4, attn_norm, 0)
    line_qkv.relay(1, 1)
    lax.fori_loop(4, 8, norm_block, 0)
    gather_g.forward(1)
    line_qkv.relay(0, 1)
    dense_send()
    line_upb.finish(0)
    lax.fori_loop(0, 4, norm_block, 0)
    line_upa.finish(1)
    line_upb.finish(1)
    lax.fori_loop(0, 4, activate_b, 0)
    gather_g.corner()
    lax.fori_loop(0, 4, activate_a, 0)
    line_qkv.relay(0, 2)
    line_qkv.relay(1, 2)
    gather_g.finish()
    lax.fori_loop(0, 2, ends_of(down_block), 0)
    dense_done()
    lax.fori_loop(1, 3, down_block, 0)
    reduce_down.slot(0, 0)
    reduce_late.slot(0, 0)
    reduce_down.slot(1, 0)
    down_start()
    more_vectors()
    line_qkv.finish(0)
    reduce_late.slot(1, 0)
    line_qkv.finish(1)
    lax.fori_loop(3, 4, attend, 0)
    lax.fori_loop(0, 1, attend, 0)
    lax.fori_loop(2, 3, attend, 0)
    line_down.relay(0, 1)
    reduce_down.slot(1, 1)
    line_down.relay(1, 1)
    reduce_down.slot(0, 1)
    lax.fori_loop(1, 2, attend, 0)
    lax.fori_loop(0, 2, ends_of(qkv_block), 0)
    reduce_qkv.slot(0, 0)
    reduce_qkv.slot(1, 0)
    reduce_late.slot(1, 1)
    lax.fori_loop(0, 2, attend_in, 0)
    dense_part()
    reduce_attn.pair(0).start()
    line_down.relay(1, 2)
    reduce_late.slot(0, 1)
    line_down.relay(0, 2)
    lax.fori_loop(2, 4, attend_in, 0)
    lax.fori_loop(1, 3, qkv_block, 0)
    reduce_down.slot(0, 2)
    reduce_attn.pair(1).start()
    line_down.finish(0)
    reduce_qkv.slot(0, 1)
    dense_back()
    reduce_qkv.slot(1, 1)
    line_down.finish(1)
    lax.fori_loop(0, 2, feed_back, 0)
    lax.fori_loop(2, 4, feed_back, 0)
    reduce_dense.slot(1, 0)
    lax.fori_loop(0, 2, ends_of(up_block), 0)
    reduce_up.slot(0, 0)
    reduce_up.slot(1, 0)
    reduce_attn.middle()
    lax.fori_loop(2, 4, feed_in, 0)
    lax.fori_loop(0, 2, feed_in, 0)
    reduce_dense.slot(0, 0)
    reduce_mlp.pair(0).start()
    reduce_mlp.pair(1).start()
    reduce_mlp.middle()
    reduce_qkv.slot(0, 2)
    reduce_qkv.slot(1, 2)
    lax.fori_loop(1, 3, up_block, 0)
    lax.fori_loop(0, 2, mix, 0)
    lax.fori_loop(2, 4, mix, 0)
    reduce_down.finish(0)
    reduce_out.pair(1).start()
    reduce_up.slot(1, 1)
    reduce_dense.slot(1, 1)
    reduce_mlp.turn(1)
    reduce_out.pair(0).start()
    reduce_attn.turn(0)
    reduce_down.slot(1, 2)
    reduce_mlp.turn(0)
    reduce_attn.turn(1)
    reduce_up.slot(0, 1)
    reduce_out.middle()
    reduce_qkv.finish(0)
    reduce_up.slot(1, 2)
    reduce_late.slot(1, 2)
    reduce_dense.slot(0, 1)
    norm_grads()
    reduce_up.slot(0, 2)
    reduce_dense.slot(1, 2)
    sums_plane()
    reduce_late.slot(0, 2)
    reduce_qkv.finish(1)
    reduce_out.turn(0)
    qkv_out()
    reduce_dense.slot(0, 2)
    up_bias_send()
    reduce_out.turn(1)
    reduce_up.finish(1)
    reduce_up.finish(0)
    reduce_down.finish(1)
    sums_send()
    up_out()
    layer_out()
    reduce_late.finish(1)
    reduce_late.finish(0)
    down_out()
    reduce_dense.finish(1)
    reduce_dense.finish(0)
    qkv_result()
    small_result()
    up_result()
    dense_out()

    for send, view in (
        (up_send, up_w.at[pl.ds(0, 192)]),
        (qkv_sends, qkv_w.at[pl.ds(0, 192)]),
        (small_send, small_line.at[pl.ds(0, 3)]),
        (dense_sends, dense_w.at[pl.ds(0, 96)]),
        (back_sends, dense_mine.at[pl.ds(0, 3)]),
        (back_sends + 1, qkv_bias_line.at[pl.ds(0, 3)]),
        (bias_sends, up_bias_final.at[pl.ds(0, 3)]),
        (bias_sends + 1, qkv_bias_final.at[pl.ds(0, 3)]),
        (out_sends, up_final.at[pl.ds(0, 3)]),
        (out_sends + 1, qkv_final.at[pl.ds(0, 3)]),
        (sums_sends, sums_core),
        (sums_sends + 1, sums_cross),
        (sums_sends + 2, sums_line.at[pl.ds(0, 3)]),
    ):
        wires.all_sent(send, view, me.core)
    for item in (
        gather_x,
        gather_g,
        gather_small,
        line_dense,
        line_qkv,
        line_upa,
        line_upb,
        line_down,
        reduce_attn,
        reduce_out,
        reduce_mlp,
        reduce_qkv,
        reduce_dense,
        reduce_down,
        reduce_late,
        reduce_up,
    ):
        item.drain()


def final_kernel(
    layer_out_ref,
    input_grad_ref,
    qkv_ref,
    dense_ref,
    up_ref,
    down_ref,
    small_ref,
    layer_out,
    input_grad,
    attn_gain_grad,
    attn_shift_grad,
    mlp_gain_grad,
    mlp_shift_grad,
    qkv_grad,
    qkv_bias_grad,
    dense_grad,
    dense_bias_grad,
    up_grad,
    up_bias_grad,
    down_grad,
    down_bias_grad,
):
    layer_out[...] = layer_out_ref[...]
    input_grad[...] = input_grad_ref[...]
    for row, out in enumerate((attn_gain_grad, attn_shift_grad, mlp_gain_grad, mlp_shift_grad)):
        out[...] = small_ref[row, :32]
    dense_bias_grad[...] = small_ref[4, :32]
    down_bias_grad[...] = small_ref[4, :32]
    qkv_bias_grad[...] = small_ref[8:11, :32]
    up_bias_grad[...] = small_ref[16, :]
    for origin in range(4):
        for which in range(3):
            qkv_grad[which, :, origin * PAIR : (origin + 1) * PAIR] = qkv_ref[
                origin, :, which * PAIR : (which + 1) * PAIR
            ].astype(F32)
        for place, other in enumerate(SEATS):
            first = (other * 4 + origin) * 128
            up_grad[:, first : first + 128] = up_ref[
                origin, :, place * 128 : (place + 1) * 128
            ].astype(F32)
    dense_grad[...] = dense_ref[...].astype(F32)
    down_grad[...] = down_ref[...].astype(F32)


def plane_layer(
    hidden_in,
    out_grad,
    span_start,
    span_length,
    attn_gain,
    attn_shift,
    mlp_gain,
    mlp_shift,
    qkv_weight,
    qkv_bias,
    dense_weight,
    dense_bias,
    up_weight,
    up_bias,
    down_weight,
    down_bias,
):
    vmem = pl.BlockSpec(memory_space=pltpu.VMEM)
    anywhere = pl.BlockSpec(memory_space=pl.ANY)
    tokens = 4 * SEQ
    outs = pl.pallas_call(
        layer_kernel,
        out_shape=(
            jax.ShapeDtypeStruct((128, WIDTH), BF16),
            jax.ShapeDtypeStruct((128, WIDTH), BF16),
            jax.ShapeDtypeStruct((4, 64, 3 * PAIR), BF16),
            jax.ShapeDtypeStruct((32, WIDTH), BF16),
            jax.ShapeDtypeStruct((4, 64, HID), BF16),
            jax.ShapeDtypeStruct((128, WIDTH), BF16),
            jax.ShapeDtypeStruct((24, 128), F32),
        ),
        in_specs=[anywhere] * 7 + [vmem] * 10,
        out_specs=(vmem,) * 7,
        scratch_shapes=[
            pltpu.VMEM((3, SEQ, PAIR), F32),
            pltpu.VMEM((tokens, WIDTH), BF16),
            pltpu.VMEM((tokens, WIDTH), BF16),
            pltpu.VMEM((LINE, 8, 128), F32),
            pltpu.VMEM((8, LINE, 8, 128), F32),
            pltpu.VMEM((WIDTH, 3 * PAIR), BF16),
            pltpu.VMEM((PAIR, WIDTH), BF16),
            pltpu.VMEM((WIDTH, HID), BF16),
            pltpu.VMEM((HID, WIDTH), BF16),
            pltpu.VMEM((8, WIDTH), F32),
            pltpu.VMEM((8, 3 * PAIR), F32),
            pltpu.VMEM((tokens, WIDTH), BF16),
            pltpu.VMEM((tokens, WIDTH), BF16),
            pltpu.VMEM((tokens, PAIR), BF16),
            pltpu.VMEM((tokens, 3 * PAIR), BF16),
            pltpu.VMEM((tokens, HID), BF16),
            pltpu.VMEM((tokens, HID), BF16),
            pltpu.VMEM((tokens, HID), F32),
            pltpu.VMEM((tokens, WIDTH), BF16),
            pltpu.VMEM((tokens, WIDTH), BF16),
            pltpu.VMEM((tokens, WIDTH), BF16),
            pltpu.VMEM((3, 2, SEQ, WIDTH), BF16),
            pltpu.VMEM((3, 3, 128, WIDTH), BF16),
            pltpu.VMEM((LINE, 256, HID), BF16),
            pltpu.VMEM((2, LINE, 256, HID), BF16),
            pltpu.VMEM((LINE, 64, WIDTH), BF16),
            pltpu.VMEM((2, LINE, 64, WIDTH), BF16),
            pltpu.VMEM((LINE, 64, WIDTH), BF16),
            pltpu.VMEM((2, LINE, 64, WIDTH), BF16),
            pltpu.VMEM((LINE, 256, 3 * PAIR), BF16),
            pltpu.VMEM((2, LINE, 256, 3 * PAIR), BF16),
            pltpu.VMEM((4, 64, HID), BF16),
            pltpu.VMEM((4, 64, 3 * PAIR), BF16),
            pltpu.VMEM((LINE, 32, WIDTH), BF16),
            pltpu.VMEM((PAIR, WIDTH), BF16),
            pltpu.VMEM((LINE, 32, WIDTH), BF16),
            pltpu.VMEM((2, LINE, 32, WIDTH), BF16),
            pltpu.VMEM((8, PAIR), F32),
            pltpu.VMEM((4, 8, PAIR), F32),
            pltpu.VMEM((LINE, 8, PAIR), F32),
            pltpu.VMEM((8, HID), F32),
            pltpu.VMEM((LINE, 8, 128), F32),
            pltpu.VMEM((8, WIDTH), F32),
            pltpu.VMEM((8, WIDTH), F32),
            pltpu.VMEM((8, WIDTH), F32),
            pltpu.VMEM((8, WIDTH), F32),
            pltpu.VMEM((3, 8, WIDTH), F32),
            pltpu.VMEM((LINE, 8, 256), F32),
            pltpu.SemaphoreType.DMA((39,)),
            pltpu.SemaphoreType.DMA((98,)),
            pltpu.SemaphoreType.DMA((14,)),
        ],
        compiler_params=pltpu.CompilerParams(
            collective_id=0, has_side_effects=True, vmem_limit_bytes=60 * 2**20
        ),
    )(
        hidden_in,
        out_grad,
        jnp.transpose(qkv_weight, (1, 0, 2)),
        dense_weight,
        up_weight,
        down_weight,
        jnp.asarray(turn_tables()),
        attn_gain,
        attn_shift,
        mlp_gain,
        mlp_shift,
        dense_bias,
        down_bias,
        span_start,
        span_length,
        qkv_bias,
        up_bias,
    )
    wide = jax.ShapeDtypeStruct((32,), F32)
    finals = pl.pallas_call(
        final_kernel,
        out_shape=(
            jax.ShapeDtypeStruct((128, WIDTH), BF16),
            jax.ShapeDtypeStruct((128, WIDTH), BF16),
            wide,
            wide,
            wide,
            wide,
            jax.ShapeDtypeStruct((3, 64, 512), F32),
            jax.ShapeDtypeStruct((3, 32), F32),
            jax.ShapeDtypeStruct((32, WIDTH), F32),
            wide,
            jax.ShapeDtypeStruct((64, 2048), F32),
            jax.ShapeDtypeStruct((128,), F32),
            jax.ShapeDtypeStruct((128, WIDTH), F32),
            wide,
        ),
        in_specs=[vmem] * 7,
        out_specs=(vmem,) * 14,
    )(*outs)
    return (*finals[:6], jnp.transpose(finals[6], (1, 0, 2)), *finals[7:])


def solution(mesh):
    in_specs = (
        P(("dp", "tensor"), None),
        P(("dp", "tensor"), None),
        P("dp", None),
        P("dp", None),
        P(("dp", "tensor")),
        P(("dp", "tensor")),
        P(("dp", "tensor")),
        P(("dp", "tensor")),
        P("dp", None, "tensor"),
        P(None, ("tensor", "dp")),
        P(("tensor", "dp"), None),
        P(("dp", "tensor")),
        P("dp", "tensor"),
        P(("tensor", "dp")),
        P(("tensor", "dp"), None),
        P(("dp", "tensor")),
    )
    out_specs = (
        P(("dp", "tensor"), None),
        P(("dp", "tensor"), None),
        P(("dp", "tensor")),
        P(("dp", "tensor")),
        P(("dp", "tensor")),
        P(("dp", "tensor")),
        P("dp", None, "tensor"),
        P(None, ("tensor", "dp")),
        P(("tensor", "dp"), None),
        P(("dp", "tensor")),
        P("dp", "tensor"),
        P(("tensor", "dp")),
        P(("tensor", "dp"), None),
        P(("dp", "tensor")),
    )
    fast = mesh.shape["dp"] == 16 and mesh.shape["tensor"] == 2
    return jax.shard_map(plane_layer if fast else shards, mesh=mesh, in_specs=in_specs, out_specs=out_specs, check_vma=False)
```
